256 devices in a mesh: seq: 64 (over z, x_lo, y), ch: 4 (over x_hi, core).
Axes of the slice: x: 4 (x_hi: 2, x_lo: 2; x = x_hi * 2 + x_lo), y: 4, z: 8, core: 2. Of those that a mesh axis runs over, the one named last changes fastest.
Arguments:
- hidden_in: bfloat16 [32768, 1024], P('seq'), may hold values from -6 to 6
- proj_zx: bfloat16 [512, 2, 1024], P(None, None, 'ch'), may hold values from -0.25 to 0.25
- proj_bc: bfloat16 [512, 128], replicated, may hold values from -0.0625 to 0.0625
- proj_dt: bfloat16 [512, 16], P(None, 'ch'), may hold values from -0.25 to 0.25
- conv_x: bfloat16 [4, 1024], P(None, 'ch'), may hold values from -3 to 3
- conv_bc: bfloat16 [4, 128], replicated, may hold values from -3 to 3
- dt_bias: float32 [16], P('ch'), may hold values from -7 to 1, as said below
- decay_exp: int32 [16], P('ch'), may hold values from 2 to 25
- skip_gain: float32 [16], P('ch'), may hold values from 0.5 to 1.5
- norm_gain: float32 [1024], P('ch'), may hold values from 0.5 to 2
- out_proj: bfloat16 [1024, 512], P('ch'), may hold values from -0.1875 to 0.1875
Outputs:
- hidden_out: bfloat16 [32768, 1024], P('seq', 'ch')
The draws below stay inside these ranges and needn't reach their ends.
Inputs may be any that keep to these rules, and one draw needn't show every extreme that they name: `dt_bias`: added to each head's step size logits before the softplus.
All inputs are finite; a program needn't handle non-finite values.
Results may differ from the reference program's by a relative error of at most 0.013.
Values may be sent and summed in bfloat16 or wider, within the bound.
No kernel may reach another device: no remote copies, remote signals or barrier semaphores. Data moves between devices by JAX's collectives and lax.ppermute only.
A program may use at most 128 MiB of HBM per device.

```python
import jax
import jax.numpy as jnp
from jax import lax

D = 512
INNER = 1024
HEADS = 16
STATE = 64
KERNEL = 4
BLOCK = 256
HEADP = 64
TOKENS = 32768


def draw_dt_bias(key, part):
    return jax.random.uniform(key, (HEADS,), jnp.float32, -2.0, 1.0)


def plant(values, rng, smallest, largest):
    shape = values.shape
    index_at = [jax.random.randint(jax.random.fold_in(rng, axis), (), 0, shape[axis]) for axis in range(len(shape))]
    values = values.at[tuple(index_at)].set(smallest)
    longest = shape.index(max(shape))
    index_at[longest] = (index_at[longest] + 1) % shape[longest]
    return values.at[tuple(index_at)].set(largest)


def steps_of(rng, extent, shards, smallest, high):
    factor_of, own = 1.0, jax.random.fold_in(rng, 6)
    for dim, parts in shards:
        steps = jnp.exp(jax.random.uniform(jax.random.fold_in(own, dim), (parts,), jnp.float32, smallest / len(shards), high / len(shards)))
        factor_of = factor_of * jnp.repeat(steps, extent[dim] // parts).reshape([-1 if axis == dim else 1 for axis in range(len(extent))])
    return factor_of


def centred(stream_key, shape, spread, bound, cuts=(), held_as=jnp.bfloat16):
    values = jax.random.normal(stream_key, shape, jnp.float32) * spread
    if len(cuts) > 0:
        values = steps_of(stream_key, shape, cuts, -0.22, 0.18) * values
    return jnp.clip(values, min=-bound, max=bound).astype(held_as)


def setup_inputs(seed: int = 0) -> dict:
    key_list = jax.random.split(jax.random.key(seed), 12)
    hidden_in = centred(key_list[0], (TOKENS, 2 * D), 1.0, 6.0, ((0, 64),))
    proj_zx = centred(key_list[1], (D, 2, INNER), D ** -0.5, 0.25, ((2, 4),))
    proj_bc = centred(key_list[2], (D, 2 * STATE), (16 * D) ** -0.5, 0.0625)
    proj_dt = centred(key_list[3], (D, HEADS), D ** -0.5, 0.25, ((1, 4),))
    conv_x = centred(key_list[4], (KERNEL, INNER), KERNEL ** -0.5, 3.0, ((1, 4),))
    conv_bc = centred(key_list[5], (KERNEL, 2 * STATE), KERNEL ** -0.5, 3.0)
    dt_bias = draw_dt_bias(jax.random.fold_in(key_list[11], 71), 0)
    decay_exp = plant(jax.random.randint(key_list[7], (HEADS,), 2, 26), jax.random.fold_in(key_list[7], 1), 2, 25).astype(jnp.int32)
    skip_gain = jnp.clip(0.5 + 1.0 * jax.random.uniform(key_list[8], (HEADS,), jnp.float32) ** steps_of(key_list[8], (HEADS,), ((0, 4),), -0.2, 0.2), 0.5, 1.5)
    norm_gain = jnp.clip(0.5 + 1.5 * jax.random.uniform(key_list[9], (INNER,), jnp.float32) ** steps_of(key_list[9], (INNER,), ((0, 4),), -0.2, 0.2), 0.5, 2.0)
    out_proj = centred(key_list[10], (INNER, D), INNER ** -0.5, 0.1875, ((0, 4),))
    return dict(hidden_in=hidden_in, proj_zx=proj_zx, proj_bc=proj_bc, proj_dt=proj_dt, conv_x=conv_x, conv_bc=conv_bc, dt_bias=dt_bias, decay_exp=decay_exp, skip_gain=skip_gain, norm_gain=norm_gain, out_proj=out_proj)


EPS = 1e-05

def causal_conv(padded, kernel_taps, row_count):
    accumulated = jnp.zeros((row_count, padded.shape[1]), jnp.float32)
    for offset in range(kernel_taps.shape[0]):
        accumulated = accumulated + kernel_taps[offset].astype(jnp.float32) * padded[offset:offset + row_count].astype(jnp.float32)
    return jax.nn.silu(accumulated).astype(jnp.bfloat16)

def block_step(carry_state, values, b_rows, c_rows, dt_block, ld_block, skip_gain):
    block_rows = values.shape[0]
    cumulative = jnp.cumsum(ld_block, axis=0)
    scores = jnp.dot(c_rows, b_rows.T, preferred_element_type=jnp.float32)
    differences = cumulative.T[:, :, None] - cumulative.T[:, None, :]
    positions = jnp.arange(block_rows, dtype=jnp.int32)
    causal_mask = positions[:, None] >= positions[None, :]
    decays = jnp.exp(jnp.where(causal_mask[None], differences, -jnp.inf))
    weights = (scores[None] * decays * dt_block.T[:, None, :]).astype(jnp.bfloat16)
    within = jnp.einsum('hts,shp->thp', weights.astype(jnp.float32), values.astype(jnp.float32))
    carried = jnp.exp(cumulative)[:, :, None] * jnp.einsum('tn,hpn->thp', c_rows.astype(jnp.float32), carry_state, precision=lax.Precision.HIGHEST)
    to_end = jnp.exp(cumulative[-1:] - cumulative) * dt_block
    loaded = (values.astype(jnp.float32) * to_end[:, :, None]).astype(jnp.bfloat16)
    added_state = jnp.einsum('thp,tn->hpn', loaded.astype(jnp.float32), b_rows.astype(jnp.float32))
    next_state = jnp.exp(cumulative[-1])[:, None, None] * carry_state + added_state
    result = within + carried + skip_gain[None, :, None] * values.astype(jnp.float32)
    return (next_state, result)

def local_pass(conv_out, step_size, log_decay, skip_gain, head_count, head_size, state_size):
    row_count = conv_out.shape[0]
    inner_width = head_count * head_size
    blocks = row_count // BLOCK
    values = conv_out[:, :inner_width].reshape(blocks, BLOCK, head_count, head_size)
    b_rows = conv_out[:, inner_width:inner_width + state_size].reshape(blocks, BLOCK, state_size)
    c_rows = conv_out[:, inner_width + state_size:].reshape(blocks, BLOCK, state_size)
    dt_blocks = step_size.reshape(blocks, BLOCK, head_count)
    ld_blocks = log_decay.reshape(blocks, BLOCK, head_count)

    def advance(carry_state, inputs):
        return block_step(carry_state, inputs[0], inputs[1], inputs[2], inputs[3], inputs[4], skip_gain)
    start_state = jnp.zeros((head_count, head_size, state_size), jnp.float32)
    final_state, outputs = lax.scan(advance, start_state, (values, b_rows, c_rows, dt_blocks, ld_blocks))
    return (outputs.reshape(row_count, head_count, head_size), final_state)

def gate_norm(mixer_out, gate_z, norm_gain):
    row_count, head_count, head_size = mixer_out.shape
    gated_out = mixer_out * jax.nn.silu(gate_z.astype(jnp.float32)).reshape(row_count, head_count, head_size)
    mean_square = lax.optimization_barrier(jnp.mean(gated_out * gated_out, axis=2, keepdims=True))
    return (gated_out * lax.rsqrt(mean_square + EPS)).reshape(row_count, head_count * head_size) * norm_gain

def strand_mix(inputs, all_weights, kernel_taps, dt_bias, decay_rate, skip_gain, norm_gain):
    projected = jnp.dot(inputs, all_weights, preferred_element_type=jnp.float32)
    gate_z = projected[:, :INNER].astype(jnp.bfloat16)
    conv_input = projected[:, INNER:2 * INNER + 2 * STATE].astype(jnp.bfloat16)
    step_size = jax.nn.softplus(projected[:, 2 * INNER + 2 * STATE:] + dt_bias)
    log_decay = -step_size * decay_rate
    padded = jnp.pad(conv_input, ((KERNEL - 1, KERNEL - 1), (0, 0)))
    ahead_conv = causal_conv(padded, kernel_taps, TOKENS)
    behind_conv = causal_conv(padded[::-1], kernel_taps, TOKENS)
    ahead_out, _ = local_pass(ahead_conv, step_size, log_decay, skip_gain, HEADS, HEADP, STATE)
    behind_out, _ = local_pass(behind_conv, step_size[::-1], log_decay[::-1], skip_gain, HEADS, HEADP, STATE)
    behind_out = behind_out[::-1]
    combined = gate_norm(ahead_out, gate_z, norm_gain) + gate_norm(behind_out, gate_z, norm_gain)
    return combined.astype(jnp.bfloat16)

def reference(hidden_in, proj_zx, proj_bc, proj_dt, conv_x, conv_bc, dt_bias, decay_exp, skip_gain, norm_gain, out_proj):
    forward_in = hidden_in[:, :D]
    reverse_in = hidden_in[:, D:][::-1, ::-1]
    all_weights = jnp.concatenate([proj_zx[:, 0, :], proj_zx[:, 1, :], proj_bc, proj_dt], axis=1)
    kernel_taps = jnp.concatenate([conv_x, conv_bc], axis=1)
    decay_rate = jnp.exp2(-decay_exp.astype(jnp.float32))
    mixed_forward = strand_mix(forward_in, all_weights, kernel_taps, dt_bias, decay_rate, skip_gain, norm_gain)
    mixed_reverse = strand_mix(reverse_in, all_weights, kernel_taps, dt_bias, decay_rate, skip_gain, norm_gain)[::-1]
    branch_forward = jnp.dot(mixed_forward, out_proj, preferred_element_type=jnp.float32)
    branch_reverse = jnp.dot(mixed_reverse, out_proj, preferred_element_type=jnp.float32)[:, ::-1]
    branch = jnp.concatenate([branch_forward, branch_reverse], axis=1)
    return (hidden_in.astype(jnp.float32) + branch).astype(jnp.bfloat16)
```

```python
import functools
import math

import jax
import jax.numpy as jnp
from jax import lax
from jax.experimental import pallas as pl
from jax.experimental.pallas import tpu as pltpu
from jax.sharding import Mesh
from jax.sharding import PartitionSpec as P

BLOCK = 256
STATE = 64
HEADP = 64
REACH = 3
HALO = 8
LANES = 128
SEQ = ("seq_0", "seq_1", "seq_2")
CH = ("x_hi", "core")
EPS = 1e-05
LOG2E = math.log2(math.e)
F32 = jnp.float32
BF16 = jnp.bfloat16

VMEM = pl.BlockSpec(memory_space=pltpu.VMEM)
SMEM = pl.BlockSpec(memory_space=pltpu.SMEM)


def params():
    return pltpu.CompilerParams(vmem_limit_bytes=40 * 1024 * 1024)


def cost(flops, transcendentals, bytes_accessed):
    return pl.CostEstimate(
        flops=flops, transcendentals=transcendentals, bytes_accessed=bytes_accessed
    )


def iota(shape, dim):
    return lax.broadcasted_iota(jnp.int32, shape, dim)


def dot(a, b):
    return jnp.dot(a, b, preferred_element_type=F32)


def dot_nt(a, b):
    return lax.dot_general(a, b, (((1,), (1,)), ((), ())), preferred_element_type=F32)


def sigmoid(v):
    return 0.5 * jnp.tanh(0.5 * v) + 0.5


def flipper(n):
    return (iota((n, n), 0) + iota((n, n), 1) == n - 1).astype(BF16)


def head_row(ref, lanes):
    heads = ref.shape[0]
    lane = iota((1, lanes), 1) % heads
    row = jnp.full((1, lanes), ref[0], ref.dtype)
    for h in range(1, heads):
        row = jnp.where(lane == h, ref[h], row)
    return row


def channel_row(ref):
    heads = ref.shape[0]
    lane = iota((1, heads * HEADP), 1) // HEADP
    row = jnp.full((1, heads * HEADP), ref[0], ref.dtype)
    for h in range(1, heads):
        row = jnp.where(lane == h, ref[h], row)
    return row


def three_parts(value):
    hi = value.astype(BF16).astype(F32)
    rest = value - hi
    mid = rest.astype(BF16).astype(F32)
    low = rest - mid
    lane = iota(value.shape, 1)
    packed = jnp.where(
        lane < 16,
        hi,
        jnp.where(lane < 32, pltpu.roll(mid, 16, 1), pltpu.roll(low, 32, 1)),
    )
    return jnp.where(lane < 48, packed, 0.0).astype(BF16)


def add_parts(value):
    return value + pltpu.roll(value, LANES - 16, 1) + pltpu.roll(value, LANES - 32, 1)


def project_kernel(
    hidden_ref, zx_ref, bc_ref, dtw_ref, bias_ref, exp_ref, z_ref, xbc_ref, cols_ref, rows_ref
):
    row_count, width = hidden_ref.shape[0], hidden_ref.shape[1] // 2
    inner = zx_ref.shape[1] // 2
    forward = hidden_ref[:, :width]
    reverse = dot(hidden_ref[:, width:], flipper(width)).astype(BF16)
    raw = []
    for strand, u in enumerate((forward, reverse)):
        z_ref[strand] = dot(u, zx_ref[:, :inner]).astype(BF16)
        xbc_ref[strand, :, :inner] = dot(u, zx_ref[:, inner:]).astype(BF16)
        xbc_ref[strand, :, inner:] = dot(u, bc_ref[...]).astype(BF16)
        raw.append(dot(u, dtw_ref[...]))
    lane = iota((row_count, LANES), 1)
    bias = head_row(bias_ref, LANES)
    rate = jnp.exp2(-head_row(exp_ref, LANES).astype(F32)) * LOG2E
    v = jnp.where(lane % 8 < 4, raw[0], raw[1]) + bias
    step = jnp.maximum(v, 0.0) + jnp.log1p(jnp.exp(-jnp.abs(v)))
    parts = three_parts(-step * rate)
    down = (iota((BLOCK, BLOCK), 0) >= iota((BLOCK, BLOCK), 1)).astype(BF16)
    up = (iota((BLOCK, BLOCK), 0) <= iota((BLOCK, BLOCK), 1)).astype(BF16)
    ahead_lane = iota((BLOCK, LANES), 1) % 16 < 8
    cums, totals = [], []
    for b in range(row_count // BLOCK):
        piece = parts[b * BLOCK : (b + 1) * BLOCK]
        cum = jnp.where(ahead_lane, add_parts(dot(down, piece)), add_parts(dot(up, piece)))
        cums.append(cum)
        last = jnp.where(iota((1, LANES), 1) % 16 < 8, cum[BLOCK - 1 :], cum[:1])
        totals.append(jnp.broadcast_to(last, (BLOCK, LANES)))
    cum = jnp.concatenate(cums, axis=0)
    total = jnp.concatenate(totals, axis=0)
    cols_ref[...] = cum
    to_end = jnp.exp2(jnp.minimum(total - cum, 0.0)) * step
    source = cum - jnp.log2(step)
    packed = jnp.where(
        lane < 16,
        cum,
        jnp.where(lane < 32, pltpu.roll(source, 16, 1), pltpu.roll(to_end, 32, 1)),
    )
    rows_ref[...] = packed.T[: rows_ref.shape[0]]


def conv_kernel(
    xbc_ref,
    prev_ref,
    next_ref,
    zx_ref,
    bc_ref,
    tapx_ref,
    tapbc_ref,
    rows_ref,
    cols_ref,
    x_ref,
    b_ref,
    c_ref,
    first_ref,
    send_ref,
    pad_ref,
):
    row_count, width = xbc_ref.shape[1], zx_ref.shape[0]
    inner = zx_ref.shape[1] // 2
    edge = jnp.concatenate([prev_ref[...].astype(F32), next_ref[...].astype(F32)], axis=0)
    edge = edge.astype(BF16)
    edges = (edge[:, :width], dot(edge[:, width:], flipper(width)).astype(BF16))
    taps = jnp.concatenate([tapx_ref[...].astype(F32), tapbc_ref[...].astype(F32)], axis=1)
    groups = taps.shape[1] // LANES
    lane = iota((BLOCK, LANES), 1)
    chunk = 32
    for strand in range(2):
        u = edges[strand]
        outer = jnp.concatenate([dot(u, zx_ref[:, inner:]), dot(u, bc_ref[...])], axis=1)
        outer = outer.astype(BF16).astype(F32)
        pad_ref[strand, :HALO] = outer[:HALO]
        pad_ref[strand, HALO + row_count :] = outer[HALO:]
        pad_ref[strand, HALO : HALO + row_count] = xbc_ref[strand].astype(F32)
        for group in range(groups):
            at = slice(group * LANES, (group + 1) * LANES)
            tap = [taps[j : j + 1, at] for j in range(REACH + 1)]
            for r in range(0, row_count, chunk):
                start = r + HALO - REACH
                window = [
                    pad_ref[strand, start + k : start + k + chunk, at]
                    for k in range(2 * REACH + 1)
                ]
                for way in range(2):
                    pick = (lambda j: j) if way == 0 else (lambda j: 2 * REACH - j)
                    acc = tap[0] * window[pick(0)]
                    for j in range(1, REACH + 1):
                        acc = acc + tap[j] * window[pick(j)]
                    value = (acc * sigmoid(acc)).astype(BF16)
                    if group < groups - 1:
                        x_ref[way, strand, r : r + chunk, at] = value
                    else:
                        b_ref[way, strand, r : r + chunk, :] = value
                        swapped = pltpu.roll(value.astype(F32), LANES - STATE, 1)
                        c_ref[way, strand, r : r + chunk, :] = jnp.where(
                            lane[:chunk] < STATE, swapped, 0.0
                        ).astype(BF16)
    half = iota((STATE, LANES), 1) < HEADP
    row_half = iota((1, LANES), 1) < HEADP
    for way in range(2):
        for strand in range(2):
            sd = way * 2 + strand
            states = []
            for b in range(2):
                block = slice(b * BLOCK, (b + 1) * BLOCK)
                bt = b_ref[way, strand, block, :].astype(F32).T[:STATE]
                scaled = jnp.concatenate(
                    [
                        (bt * rows_ref[32 + sd * 4 + h : 33 + sd * 4 + h, block]).astype(BF16)
                        for h in range(4)
                    ],
                    axis=0,
                )
                full = dot(scaled, x_ref[way, strand, block, :])
                states.append(
                    jnp.concatenate(
                        [
                            jnp.where(half, full[:64, :128], full[64:128, :128]),
                            jnp.where(half, full[128:192, 128:], full[192:, 128:]),
                        ],
                        axis=1,
                    )
                )
            first, last, end = (0, 1, row_count - 1) if way == 0 else (1, 0, 0)
            factor = [
                jnp.exp2(
                    jnp.broadcast_to(rows_ref[sd * 4 + h : sd * 4 + h + 1, end : end + 1], (1, LANES))
                )
                for h in range(4)
            ]
            factor = jnp.concatenate(
                [
                    jnp.where(row_half, factor[0], factor[1]),
                    jnp.where(row_half, factor[2], factor[3]),
                ],
                axis=1,
            )
            first_ref[way, strand] = states[first]
            send_ref[:, sd * 256 : (sd + 1) * 256] = (
                factor * states[first] + states[last]
            ).astype(BF16)
    total = jnp.where(
        iota((8, LANES), 1) % 16 < 8,
        jnp.broadcast_to(cols_ref[BLOCK - 1 : BLOCK] + cols_ref[row_count - 1 :], (8, LANES)),
        jnp.broadcast_to(cols_ref[:1] + cols_ref[BLOCK : BLOCK + 1], (8, LANES)),
    )
    send_ref[:, 1024:] = jnp.broadcast_to(
        three_parts(total).astype(F32)[:1], (STATE, LANES)
    ).astype(BF16)


def scan_kernel(got_ref, out_ref):
    count = got_ref.shape[0]
    parts = got_ref[:, 1024:]
    row, col = iota((count, count), 0), iota((count, count), 1)

    def summed(mask):
        return add_parts(dot(mask.astype(BF16), parts))

    ahead_lane = iota((count, LANES), 1) % 16 < 8
    upto = jnp.where(ahead_lane, summed(row >= col), summed(row <= col))
    before = jnp.where(ahead_lane, summed(row > col), summed(row < col))
    upto_t = upto.T
    half = iota((count, LANES), 1) < HEADP
    for sd in range(4):
        seen = row > col if sd < 2 else row < col
        factors = []
        for h in range(4):
            i = sd * 4 + h
            gap = before[:, i : i + 1] - upto_t[i : i + 1, :]
            factors.append(jnp.exp2(jnp.where(seen, gap, -jnp.inf)).astype(BF16))
        full = dot(jnp.concatenate(factors, axis=0), got_ref[:, sd * 256 : (sd + 1) * 256])
        out_ref[:, sd * 256 : (sd + 1) * 256] = jnp.concatenate(
            [
                jnp.where(half, full[:count, :128], full[count : 2 * count, :128]),
                jnp.where(half, full[2 * count : 3 * count, 128:], full[3 * count :, 128:]),
            ],
            axis=1,
        ).astype(BF16)


def inside_kernel(x_ref, b_ref, c_ref, rows_ref, cols_ref, skip_ref, y_ref):
    skip = channel_row(skip_ref)
    size = 128
    low = iota((size, size), 0) >= iota((size, size), 1)
    high = iota((size, size), 0) <= iota((size, size), 1)
    half = iota((size, LANES), 1) < HEADP
    for way in range(2):
        for strand in range(2):
            sd = way * 2 + strand
            for b in range(x_ref.shape[2] // BLOCK):
                block = slice(b * BLOCK, (b + 1) * BLOCK)
                scores = dot_nt(c_ref[way, strand, block, :], b_ref[way, strand, block, :])
                for pair in range(2):
                    at = slice(pair * LANES, (pair + 1) * LANES)
                    for t in range(2):
                        here = slice(b * BLOCK + t * size, b * BLOCK + (t + 1) * size)
                        seen = [s for s in range(2) if (s <= t if way == 0 else s >= t)]
                        outs = []
                        for h in (2 * pair, 2 * pair + 1):
                            i = sd * 4 + h
                            gone = jnp.broadcast_to(cols_ref[here, i : i + 1], (size, size))
                            tiles = []
                            for s in seen:
                                there = slice(b * BLOCK + s * size, b * BLOCK + (s + 1) * size)
                                gap = gone - rows_ref[16 + i : 17 + i, there]
                                if s == t:
                                    gap = jnp.where(low if way == 0 else high, gap, -jnp.inf)
                                part = scores[t * size : (t + 1) * size, s * size : (s + 1) * size]
                                tiles.append((part * jnp.exp2(gap)).astype(BF16))
                            weights = tiles[0] if len(tiles) == 1 else jnp.concatenate(tiles, axis=1)
                            lo = b * BLOCK + seen[0] * size
                            hi = b * BLOCK + (seen[-1] + 1) * size
                            outs.append(dot(weights, x_ref[way, strand, lo:hi, at]))
                        y_ref[way, strand, here, at] = (
                            jnp.where(half, outs[0], outs[1])
                            + skip[:, at] * x_ref[way, strand, here, at].astype(F32)
                        )


def finish_kernel(
    strand_ref, y_ref, c_ref, ahead_ref, behind_ref, first_ref, cols_ref, z_ref, gain_ref, out_ref
):
    strand = strand_ref[0]
    inner = z_ref.shape[2]
    same = (iota((inner, inner), 0) // HEADP == iota((inner, inner), 1) // HEADP).astype(BF16)
    half = iota((BLOCK, LANES), 1) < HEADP
    row_half = iota((1, LANES), 1) < HEADP
    gain = gain_ref[...]
    lane_of = iota((BLOCK, LANES), 1)
    for b in range(2):
        block = slice(b * BLOCK, (b + 1) * BLOCK)
        z = z_ref[0, block, :].astype(F32)
        gate = z * sigmoid(z)
        normed = []
        for way in range(2):
            came = (ahead_ref if way == 0 else behind_ref)[...].astype(F32)
            cols = jnp.where(
                strand == 0,
                cols_ref[...],
                pltpu.roll(cols_ref[...], LANES - 4, 1),
            ) if False else cols_ref[...]
            decay_all = jnp.exp2(cols[block])
            spread = []
            for h in range(4):
                i = way * 8 + h
                column = jnp.where(
                    strand == 0, decay_all[:, i : i + 1], decay_all[:, i + 4 : i + 5]
                )
                spread.append(jnp.broadcast_to(column, (BLOCK, LANES)))
            decay = jnp.concatenate(
                [jnp.where(half, spread[0], spread[1]), jnp.where(half, spread[2], spread[3])],
                axis=1,
            )
            if b == way:
                state = came
            else:
                edge = slice(BLOCK - 1, BLOCK) if way == 0 else slice(BLOCK, BLOCK + 1)
                total = jnp.exp2(cols[edge])
                picks = []
                for h in range(4):
                    i = way * 8 + h
                    value = jnp.where(strand == 0, total[:, i : i + 1], total[:, i + 4 : i + 5])
                    picks.append(jnp.broadcast_to(value, (1, LANES)))
                factor = jnp.concatenate(
                    [jnp.where(row_half, picks[0], picks[1]), jnp.where(row_half, picks[2], picks[3])],
                    axis=1,
                )
                state = factor * came + first_ref[way, 0]
            state = jnp.concatenate([state, jnp.zeros_like(state)], axis=0).astype(BF16)
            mixer = y_ref[way, 0, block, :] + decay * dot(c_ref[way, 0, block, :], state)
            gated = mixer * gate
            mean = dot((gated * gated).astype(BF16), same) * (1.0 / HEADP)
            normed.append(gated * lax.rsqrt(mean + EPS))
        out_ref[block, :] = ((normed[0] + normed[1]) * gain).astype(BF16)


def weights_kernel(place_ref, own_ref, other_ref, out_ref):
    rows, columns = own_ref.shape
    part = columns // 2
    source, target = iota((columns, columns), 0), iota((columns, columns), 1)
    core = place_ref[1]
    column = jnp.where(target < part, target + core * part, target - core * part)
    wanted = jnp.where(place_ref[0] == 0, column, columns - 1 - column)
    chosen = (source == wanted).astype(BF16)
    out_ref[:rows] = dot(own_ref[...], chosen).astype(BF16)
    out_ref[rows:] = dot(other_ref[...], chosen).astype(BF16)


def output_kernel(place_ref, own_ref, got_ref, w_ref, hidden_ref, keep_ref, send_ref):
    rows = own_ref.shape[1]
    part = w_ref.shape[1] // 2
    send_ref[...] = (
        dot(own_ref[...], w_ref[:rows, part:]) + dot(got_ref[...], w_ref[rows:, part:])
    ).astype(BF16)
    keep_ref[...] = (
        dot(own_ref[...], w_ref[:rows, :part])
        + dot(got_ref[...], w_ref[rows:, :part])
        + hidden_ref[...].astype(F32)
    )


def call(kernel, out_shape, specs, out_specs, estimate, scratch=()):
    return pl.pallas_call(
        kernel,
        out_shape=out_shape,
        in_specs=specs,
        out_specs=out_specs,
        scratch_shapes=scratch,
        compiler_params=params(),
        cost_estimate=estimate,
    )


def struct(shape, dtype):
    return jax.ShapeDtypeStruct(shape, dtype)


def shards(
    hidden_in,
    proj_zx,
    proj_bc,
    proj_dt,
    conv_x,
    conv_bc,
    dt_bias,
    decay_exp,
    skip_gain,
    norm_gain,
    out_proj,
):
    rows = hidden_in.shape[0]
    inner = proj_zx.shape[2]
    count = math.prod(lax.axis_size(axis) for axis in SEQ)
    rise = [(i, i + 1) for i in range(count - 1)]
    fall = [(i + 1, i) for i in range(count - 1)]
    swap = [(0, 1), (1, 0)]
    prev = lax.ppermute(hidden_in[rows - HALO :], SEQ, rise)
    following = lax.ppermute(hidden_in[:HALO], SEQ, fall)
    x_hi, core = lax.axis_index("x_hi"), lax.axis_index("core")
    place = jnp.stack([x_hi, core]).astype(jnp.int32)
    zx = proj_zx.reshape(proj_zx.shape[0], 2 * inner)
    dtw = jnp.tile(proj_dt, (1, LANES // proj_dt.shape[1]))

    z, xbc, cols, turned = call(
        project_kernel,
        (
            struct((2, rows, inner), BF16),
            struct((2, rows, inner + LANES), BF16),
            struct((rows, LANES), F32),
            struct((48, rows), F32),
        ),
        [VMEM] * 4 + [SMEM] * 2,
        (VMEM,) * 4,
        cost(2_000_000_000, 300_000, 4_000_000),
    )(hidden_in, zx, proj_bc, dtw, dt_bias, decay_exp)

    x, b, c, first, send = call(
        conv_kernel,
        (
            struct((2, 2, rows, inner), BF16),
            struct((2, 2, rows, LANES), BF16),
            struct((2, 2, rows, LANES), BF16),
            struct((2, 2, STATE, inner), F32),
            struct((STATE, 4 * inner + LANES), BF16),
        ),
        [VMEM] * 9,
        (VMEM,) * 5,
        cost(2_000_000_000, 800_000, 6_000_000),
        [pltpu.VMEM((2, rows + 2 * HALO, inner + LANES), F32)],
    )(xbc, prev, following, zx, proj_bc, conv_x, conv_bc, turned, cols)

    got = lax.all_to_all(send, SEQ, 0, 0, tiled=True)
    other_proj = lax.ppermute(out_proj, "x_hi", swap)
    y = call(
        inside_kernel,
        struct((2, 2, rows, inner), F32),
        [VMEM] * 5 + [SMEM],
        VMEM,
        cost(4_000_000_000, 2_000_000, 6_000_000),
    )(x, b, c, turned, cols, skip_gain)
    weights = call(
        weights_kernel,
        struct((2 * inner, 2 * inner), BF16),
        [SMEM, VMEM, VMEM],
        VMEM,
        cost(500_000_000, 0, 1_000_000),
    )(place, out_proj, other_proj)

    scanned = call(
        scan_kernel,
        struct((count, 4 * inner), BF16),
        [VMEM],
        VMEM,
        cost(100_000_000, 70_000, 300_000),
    )(got)
    came = lax.all_to_all(scanned, SEQ, 0, 0, tiled=True)

    gain = norm_gain.reshape(1, inner)

    def finish(strand):
        return pl.pallas_call(
            finish_kernel,
            out_shape=struct((rows, inner), BF16),
            grid_spec=pltpu.PrefetchScalarGridSpec(
                num_scalar_prefetch=1,
                grid=(1,),
                in_specs=[
                    pl.BlockSpec((2, 1, rows, inner), lambda i, s: (0, s[0], 0, 0)),
                    pl.BlockSpec((2, 1, rows, LANES), lambda i, s: (0, s[0], 0, 0)),
                    pl.BlockSpec((STATE, inner), lambda i, s: (0, s[0])),
                    pl.BlockSpec((STATE, inner), lambda i, s: (0, 2 + s[0])),
                    pl.BlockSpec((2, 1, STATE, inner), lambda i, s: (0, s[0], 0, 0)),
                    pl.BlockSpec((rows, LANES), lambda i, s: (0, 0)),
                    pl.BlockSpec((1, rows, inner), lambda i, s: (s[0], 0, 0)),
                    pl.BlockSpec((1, inner), lambda i, s: (0, 0)),
                ],
                out_specs=pl.BlockSpec((rows, inner), lambda i, s: (0, 0)),
            ),
            compiler_params=params(),
            cost_estimate=cost(1_000_000_000, 500_000, 3_000_000),
        )(strand.reshape(1).astype(jnp.int32), y, c, came, came, first, cols, z, gain)

    away = finish(1 - x_hi)
    arrived = lax.ppermute(away, "x_hi", swap)
    own = finish(x_hi)

    keep, give = pl.pallas_call(
        output_kernel,
        out_shape=(struct((rows, inner), F32), struct((rows, inner), BF16)),
        grid_spec=pltpu.PrefetchScalarGridSpec(
            num_scalar_prefetch=1,
            grid=(1,),
            in_specs=[
                pl.BlockSpec((rows, inner), lambda i, p: (0, 0)),
                pl.BlockSpec((rows, inner), lambda i, p: (0, 0)),
                pl.BlockSpec((2 * inner, 2 * inner), lambda i, p: (0, 0)),
                pl.BlockSpec((rows, inner), lambda i, p: (0, 2 * p[0] + p[1])),
            ],
            out_specs=(
                pl.BlockSpec((rows, inner), lambda i, p: (0, 0)),
                pl.BlockSpec((rows, inner), lambda i, p: (0, 0)),
            ),
        ),
        compiler_params=params(),
        cost_estimate=cost(600_000_000, 0, 2_000_000),
    )(place, own, arrived, weights, hidden_in)
    taken = lax.ppermute(give, "core", swap)
    return (keep + taken.astype(F32)).astype(BF16)


def solution(mesh):
    torus = Mesh(mesh.devices.reshape(8, 2, 4, 2, 2), SEQ + CH)
    placed = (
        P(SEQ, None),
        P(None, None, CH),
        P(),
        P(None, CH),
        P(None, CH),
        P(),
        P(CH),
        P(CH),
        P(CH),
        P(CH),
        P(CH, None),
    )
    return jax.shard_map(
        shards, mesh=torus, in_specs=placed, out_specs=P(SEQ, CH), check_vma=False
    )
```

```python
import math

import jax
import jax.numpy as jnp
from jax import lax
from jax.experimental import pallas as pl
from jax.experimental.pallas import tpu as pltpu
from jax.sharding import Mesh
from jax.sharding import PartitionSpec as P

BLOCK = 256
STATE = 64
HEADP = 64
REACH = 3
HALO = 8
LANES = 128
SEQ = ("seq_0", "seq_1", "seq_2")
CH = ("x_hi", "core")
EPS = 1e-05
LOG2E = math.log2(math.e)
F32 = jnp.float32
BF16 = jnp.bfloat16

VMEM = pl.BlockSpec(memory_space=pltpu.VMEM)
HBM = pl.BlockSpec(memory_space=pltpu.HBM)
SMEM = pl.BlockSpec(memory_space=pltpu.SMEM)


def cost(flops, transcendentals, bytes_accessed):
    return pl.CostEstimate(
        flops=flops, transcendentals=transcendentals, bytes_accessed=bytes_accessed
    )


def struct(shape, dtype):
    return jax.ShapeDtypeStruct(shape, dtype)


def stored(shape, dtype):
    return pltpu.HBM(shape, dtype)


def lying(*arrays):
    return [pltpu.with_memory_space_constraint(array, pltpu.HBM) for array in arrays]


def start_copies(pairs, sems):
    copies = [
        pltpu.make_async_copy(source, target, sems.at[i]) for i, (source, target) in enumerate(pairs)
    ]
    for copy in copies:
        copy.start()
    return copies


def dma(n):
    return pltpu.SemaphoreType.DMA((n,))


def call(kernel, out_shape, specs, out_specs, estimate, mib=16, scratch=()):
    return pl.pallas_call(
        kernel,
        out_shape=out_shape,
        in_specs=specs,
        out_specs=out_specs,
        scratch_shapes=scratch,
        compiler_params=pltpu.CompilerParams(vmem_limit_bytes=mib * 1024 * 1024),
        cost_estimate=estimate,
    )


def iota(shape, dim):
    return lax.broadcasted_iota(jnp.int32, shape, dim)


def dot(a, b):
    return jnp.dot(a, b, preferred_element_type=F32)


def dot_nt(a, b):
    return lax.dot_general(a, b, (((1,), (1,)), ((), ())), preferred_element_type=F32)


def sigmoid(v):
    return 0.5 * jnp.tanh(0.5 * v) + 0.5


def parts_of(value):
    hi = value.astype(BF16).astype(F32)
    rest = value - hi
    mid = rest.astype(BF16).astype(F32)
    return hi, mid, rest - mid


def orient(n, strand):
    source, target = iota((n, n), 0), iota((n, n), 1)
    return (source == jnp.where(strand == 0, target, n - 1 - target)).astype(BF16)


DT_AT, TAP_AT, SMALL_AT, PACKED = 512, 520, 528, 544


def pack_kernel(
    place_ref, x_ref, dt_hbm, taps_hbm, bias_hbm, exp_hbm, skip_hbm, gain_hbm, hidden_hbm,
    pack_ref, head_ref, tail_ref,
    dt_ref, taps_ref, bias_ref, exp_ref, skip_ref, gain_ref, sems,
):
    inner, heads = x_ref.shape[1], dt_ref.shape[0]
    rows, width = hidden_hbm.shape[0], hidden_hbm.shape[1] // 2
    columns = pl.ds(pl.multiple_of(place_ref[0] * width, width), width)
    copies = start_copies(
        (
            (dt_hbm, dt_ref),
            (taps_hbm, taps_ref),
            (bias_hbm, bias_ref),
            (exp_hbm, exp_ref),
            (skip_hbm, skip_ref),
            (gain_hbm, gain_ref),
            (hidden_hbm.at[pl.ds(0, HALO), columns], head_ref),
            (hidden_hbm.at[pl.ds(rows - HALO, HALO), columns], tail_ref),
        ),
        sems,
    )
    pack_ref[:DT_AT] = x_ref[...]
    for copy in copies:
        copy.wait()
    lane = iota((1, inner), 1)
    small = jnp.zeros((1, inner), F32)
    for h in range(heads):
        for k, ref in enumerate((bias_ref, exp_ref, skip_ref)):
            value = ref[:, h : h + 1].astype(F32)
            small = jnp.where(lane == k * heads + h, jnp.broadcast_to(value, (1, inner)), small)
    packed = [dt_ref[:, :inner].astype(F32), dt_ref[:, inner:].astype(F32), taps_ref[...].astype(F32)]
    packed.append(jnp.zeros((SMALL_AT - TAP_AT - taps_ref.shape[0], inner), F32))
    packed += parts_of(small) + parts_of(gain_ref[...])
    packed.append(jnp.zeros((PACKED - SMALL_AT - 6, inner), F32))
    pack_ref[DT_AT:] = jnp.concatenate(packed, axis=0).astype(BF16)


def unpack(ref):
    tail = ref[SMALL_AT:].astype(F32)
    return tail[0:1] + tail[1:2] + tail[2:3], tail[3:4] + tail[4:5] + tail[5:6]


def column_of(smalls, at):
    row = iota((8, 1), 0)
    out = jnp.zeros((8, 1), F32)
    for g in range(2):
        for h in range(4):
            out = jnp.where(row == g * 4 + h, smalls[g][:, at + h : at + h + 1], out)
    return out


def spread(pieces, rows):
    half = iota((rows, LANES), 1) < HEADP
    wide = [jnp.broadcast_to(piece, (rows, LANES)) for piece in pieces]
    return jnp.concatenate(
        [jnp.where(half, wide[2 * q], wide[2 * q + 1]) for q in range(4)], axis=1
    )


def front_kernel(
    place_ref, hidden_ref, prev_ref, next_ref, own_ref, other_ref, bc_ref, tapbc_ref,
    u_hbm, x_hbm, b_hbm, c_hbm, cols_hbm, rows_hbm, first_hbm, gains_hbm, send_hbm,
    u_ref, x_ref, b_ref, c_ref, cols_ref, rows_ref, first_ref, gains_ref, send_ref, pad_ref, sems,
):
    copies = []

    def keep(source, target):
        copies.append(pltpu.make_async_copy(source, target, sems.at[len(copies)]))
        copies[-1].start()

    row_count, width = hidden_ref.shape[0], hidden_ref.shape[1] // 2
    inner = own_ref.shape[1]
    strand, position, count = place_ref[0], place_ref[2], place_ref[3]
    packs = (own_ref, other_ref)
    turn = orient(width, strand)
    u = dot(hidden_ref[:, pl.ds(pl.multiple_of(strand * width, width), width)], turn).astype(BF16)
    u_ref[...] = u
    keep(u_ref, u_hbm)
    before = jnp.where(position > 0, prev_ref[...].astype(F32), 0.0)
    after = jnp.where(position < count - 1, next_ref[...].astype(F32), 0.0)
    edge = dot(jnp.concatenate([before, after], axis=0).astype(BF16), turn).astype(BF16)

    raw = jnp.concatenate(
        [
            dot_nt(
                jnp.concatenate(
                    [ref[DT_AT : DT_AT + 4].astype(F32), ref[DT_AT + 4 : DT_AT + 8].astype(F32)],
                    axis=1,
                ).astype(BF16),
                u,
            )
            for ref in packs
        ],
        axis=0,
    )
    smalls, gains = zip(*[unpack(ref) for ref in packs])
    gains_ref[...] = jnp.concatenate(
        [
            jnp.concatenate(gains, axis=1),
            spread([smalls[g][:, 8 + h : 9 + h] for g in range(2) for h in range(4)], 1),
            jnp.zeros((6, 2 * inner), F32),
        ],
        axis=0,
    )
    keep(gains_ref, gains_hbm)
    v = raw + column_of(smalls, 0)
    rate = jnp.exp2(-column_of(smalls, 4)) * LOG2E
    step = jnp.maximum(v, 0.0) + jnp.log1p(jnp.exp(-jnp.abs(v)))
    parts = jnp.concatenate(parts_of(-step * rate), axis=0).astype(BF16)
    ahead = (iota((BLOCK, BLOCK), 0) <= iota((BLOCK, BLOCK), 1)).astype(BF16)
    behind = (iota((BLOCK, BLOCK), 0) >= iota((BLOCK, BLOCK), 1)).astype(BF16)
    cums, ends = [], []
    for b in range(2):
        piece = parts[:, b * BLOCK : (b + 1) * BLOCK]
        both = []
        for mask in (ahead, behind):
            full = dot(piece, mask)
            both.append(full[:8] + full[8:16] + full[16:])
        cums.append(jnp.concatenate(both, axis=0))
        last = jnp.concatenate([both[0][:, BLOCK - 1 :], both[1][:, :1]], axis=0)
        ends.append(jnp.broadcast_to(last, (16, BLOCK)))
    cum = jnp.concatenate(cums, axis=1)
    end = jnp.concatenate(ends, axis=1)
    step = jnp.concatenate([step, step], axis=0)
    rows_ref[:16] = cum
    rows_ref[16:32] = cum - jnp.log2(step)
    rows_ref[32:] = jnp.exp2(jnp.minimum(end - cum, 0.0)) * step
    cols_ref[...] = jnp.concatenate([cum, jnp.zeros((LANES - 16, row_count), F32)], axis=0).T
    totals = [ends[b][:, :1] for b in range(2)]
    keep(rows_ref, rows_hbm)
    keep(cols_ref, cols_hbm)

    chunk = 32
    mains = [(u, slice(HALO, HALO + row_count)), (edge, None)]
    for piece, where in mains:
        for g in range(3):
            w = packs[g][:DT_AT] if g < 2 else bc_ref[...]
            full = dot(piece, w).astype(BF16).astype(F32)
            for k in range(w.shape[1] // LANES):
                value, at = full[:, k * LANES : (k + 1) * LANES], g * inner // LANES + k
                if where is not None:
                    pad_ref[at, where] = value
                else:
                    pad_ref[at, :HALO] = value[:HALO]
                    pad_ref[at, HALO + row_count :] = value[HALO:]
    taps = jnp.concatenate(
        [ref[TAP_AT : TAP_AT + REACH + 1].astype(F32) for ref in packs]
        + [tapbc_ref[...].astype(F32)],
        axis=1,
    )
    groups = taps.shape[1] // LANES
    low_lane = iota((chunk, LANES), 1) < STATE
    for group in range(groups):
        at = slice(group * LANES, (group + 1) * LANES)
        tap = [taps[j : j + 1, at] for j in range(REACH + 1)]
        for r in range(0, row_count, chunk):
            start = r + HALO - REACH
            window = [
                pad_ref[group, start + k : start + k + chunk] for k in range(2 * REACH + 1)
            ]
            for way in range(2):
                acc = tap[0] * window[0 if way == 0 else 2 * REACH]
                for j in range(1, REACH + 1):
                    acc = acc + tap[j] * window[j if way == 0 else 2 * REACH - j]
                value = (acc * sigmoid(acc)).astype(BF16)
                if group < groups - 1:
                    x_ref[way, r : r + chunk, at] = value
                else:
                    b_ref[way, r : r + chunk, :] = value
                    swapped = pltpu.roll(value.astype(F32), LANES - STATE, 1)
                    c_ref[way, r : r + chunk, :] = jnp.where(low_lane, swapped, 0.0).astype(BF16)

    keep(x_ref, x_hbm)
    keep(b_ref, b_hbm)
    keep(c_ref, c_hbm)

    half = iota((STATE, LANES), 1) < HEADP
    row8 = iota((8, LANES), 0)
    for way in range(2):
        states = []
        for b in range(2):
            block = slice(b * BLOCK, (b + 1) * BLOCK)
            bt = b_ref[way, block, :].astype(F32).T[:STATE]
            tiles = []
            for g in range(2):
                at = 32 + way * 8 + g * 4
                scaled = jnp.concatenate(
                    [
                        (bt * rows_ref[at + h : at + h + 1, block]).astype(BF16)
                        for h in range(4)
                    ],
                    axis=0,
                )
                full = dot(scaled, x_ref[way, block, g * inner : (g + 1) * inner])
                tiles.append(jnp.where(half, full[:64, :128], full[64:128, :128]))
                tiles.append(jnp.where(half, full[128:192, 128:], full[192:, 128:]))
            states.append(tiles)
        first, last = (0, 1) if way == 0 else (1, 0)
        at = slice(way * 8, way * 8 + 8)
        last_total = jnp.exp2(totals[last][at])
        both_total = jnp.exp2(totals[0][at] + totals[1][at])
        factor = spread([last_total[i : i + 1] for i in range(8)], 1)
        whole = spread([both_total[i : i + 1] for i in range(8)], 8)
        for q in range(4):
            lanes = slice(q * LANES, (q + 1) * LANES)
            state = factor[:, lanes] * states[first][q] + states[last][q]
            first_ref[way, :, lanes] = states[first][q]
            hi, mid, low = parts_of(whole[:, lanes])
            decay = jnp.where(
                row8 == 0, hi, jnp.where(row8 == 1, mid, jnp.where(row8 == 2, low, 0.0))
            )
            for n in range(8):
                send_ref[way * 32 + n * 4 + q] = jnp.concatenate(
                    [state[n * 8 : n * 8 + 8], decay], axis=0
                ).astype(BF16)
        keep(send_ref.at[pl.ds(way * 32, 32)], send_hbm.at[pl.ds(way * 32, 32)])
    keep(first_ref, first_hbm)
    for copy in copies:
        copy.wait()


def scan_kernel(place_ref, got_ref, after_hbm, out_ref):
    count = got_ref.shape[0]
    backward = place_ref[2] >= count // 2
    state = jnp.zeros((8, LANES), F32)
    for i in range(count):
        k = jnp.where(backward, count - 1 - i, i)
        piece = got_ref[k].astype(F32)
        out_ref[k] = state.astype(BF16)
        decay = jnp.sum(piece[8:], axis=0, keepdims=True)
        state = decay * state + piece[:8]


def inside_kernel(
    x_hbm, b_hbm, c_hbm, rows_hbm, cols_hbm, gains_hbm, y_hbm,
    x_ref, b_ref, c_ref, rows_ref, cols_ref, gains_ref, y_ref, sems,
):
    copies = start_copies(
        (
            (b_hbm, b_ref),
            (c_hbm, c_ref),
            (rows_hbm, rows_ref),
            (cols_hbm, cols_ref),
            (gains_hbm, gains_ref),
            (x_hbm.at[0], x_ref.at[0]),
            (x_hbm.at[1], x_ref.at[1]),
        ),
        sems,
    )
    for copy in copies[:-1]:
        copy.wait()
    results = []
    size = 128
    low = iota((size, size), 0) >= iota((size, size), 1)
    high = iota((size, size), 0) <= iota((size, size), 1)
    half = iota((size, LANES), 1) < HEADP
    skip = gains_ref[1:2]
    for way in range(2):
        if way == 1:
            copies[-1].wait()
        for b in range(2):
            block = slice(b * BLOCK, (b + 1) * BLOCK)
            scores = dot_nt(c_ref[way, block, :], b_ref[way, block, :])
            for pair in range(4):
                at = slice(pair * LANES, (pair + 1) * LANES)
                for t in range(2):
                    here = slice(b * BLOCK + t * size, b * BLOCK + (t + 1) * size)
                    seen = [s for s in range(2) if (s <= t if way == 0 else s >= t)]
                    lo = b * BLOCK + seen[0] * size
                    hi = b * BLOCK + (seen[-1] + 1) * size
                    outs = []
                    for h in (2 * pair, 2 * pair + 1):
                        i = way * 8 + h
                        gone = jnp.broadcast_to(cols_ref[here, i : i + 1], (size, size))
                        tiles = []
                        for s in seen:
                            there = slice(b * BLOCK + s * size, b * BLOCK + (s + 1) * size)
                            gap = gone - rows_ref[16 + i : 17 + i, there]
                            if s == t:
                                gap = jnp.where(low if way == 0 else high, gap, -jnp.inf)
                            part = scores[t * size : (t + 1) * size, s * size : (s + 1) * size]
                            tiles.append((part * jnp.exp2(gap)).astype(BF16))
                        weights = tiles[0] if len(tiles) == 1 else jnp.concatenate(tiles, axis=1)
                        outs.append(dot(weights, x_ref[way, lo:hi, at]))
                    y_ref[way, here, at] = (
                        jnp.where(half, outs[0], outs[1])
                        + skip[:, at] * x_ref[way, here, at].astype(F32)
                    ).astype(BF16)
            results.append(
                pltpu.make_async_copy(
                    y_ref.at[way, block, :], y_hbm.at[way, block, :], sems.at[7 + 2 * way + b]
                )
            )
            results[-1].start()
    for copy in results:
        copy.wait()


def ready_kernel(
    place_ref, u_hbm, own_z_ref, other_z_ref, own_out_ref, other_out_ref, after_hbm,
    gate_hbm, w_hbm,
    u_ref, gate_ref, w_ref, sems,
):
    loading = pltpu.make_async_copy(u_hbm, u_ref, sems.at[0])
    loading.start()
    rows, columns = own_out_ref.shape
    part = columns // 2
    source, target = iota((columns, columns), 0), iota((columns, columns), 1)
    core = place_ref[1]
    column = jnp.where(target < part, target + core * part, target - core * part)
    wanted = jnp.where(place_ref[0] == 0, column, columns - 1 - column)
    chosen = (source == wanted).astype(BF16)
    w_ref[:rows] = dot(own_out_ref[...], chosen).astype(BF16)
    w_ref[rows:] = dot(other_out_ref[...], chosen).astype(BF16)
    copies = [pltpu.make_async_copy(w_ref, w_hbm, sems.at[1])]
    copies[0].start()
    loading.wait()
    inner = own_z_ref.shape[1]
    for g, ref in enumerate((own_z_ref, other_z_ref)):
        z = dot(u_ref[...], ref[...]).astype(BF16).astype(F32)
        gate_ref[:, g * inner : (g + 1) * inner] = (z * sigmoid(z)).astype(BF16)
    copies.append(pltpu.make_async_copy(gate_ref, gate_hbm, sems.at[2]))
    copies[1].start()
    for copy in copies:
        copy.wait()


def back_kernel(
    place_ref, y_hbm, c_hbm, came_ref, first_hbm, cols_hbm, gate_hbm, gains_hbm, w_hbm, hidden_hbm,
    keep_ref, give_ref,
    y_ref, c_ref, first_ref, cols_ref, gate_ref, gains_ref, w_ref, hidden_ref, state_ref, sems,
):
    part = w_hbm.shape[1] // 2
    inner = y_hbm.shape[2] // 2
    ours = pl.multiple_of((2 * place_ref[0] + place_ref[1]) * part, part)
    blocks = [slice(b * BLOCK, (b + 1) * BLOCK) for b in range(2)]
    copies = start_copies(
        (
            (cols_hbm, cols_ref),
            (first_hbm, first_ref),
            (c_hbm, c_ref),
            (gains_hbm, gains_ref),
            (gate_hbm.at[blocks[0]], gate_ref.at[blocks[0]]),
            (y_hbm.at[:, blocks[0]], y_ref.at[:, blocks[0]]),
            (w_hbm, w_ref),
            (hidden_hbm.at[:, pl.ds(ours, part)], hidden_ref),
            (gate_hbm.at[blocks[1]], gate_ref.at[blocks[1]]),
            (y_hbm.at[:, blocks[1]], y_ref.at[:, blocks[1]]),
        ),
        sems,
    )
    same = (iota((inner, inner), 0) // HEADP == iota((inner, inner), 1) // HEADP).astype(BF16)
    for way in range(2):
        for n in range(8):
            for q in range(4):
                state_ref[way, n * 8 : n * 8 + 8, q * LANES : (q + 1) * LANES] = came_ref[
                    way * 32 + n * 4 + q
                ].astype(F32)
    for copy in copies[:4]:
        copy.wait()
    for b, block in enumerate(blocks):
        decays = jnp.exp2(cols_ref[block])
        for copy in copies[4:6] if b == 0 else copies[8:]:
            copy.wait()
        gate = gate_ref[block, :].astype(F32)
        total = None
        for way in range(2):
            state = state_ref[way]
            if b != way:
                edge = BLOCK - 1 if way == 0 else BLOCK
                passed = jnp.exp2(cols_ref[edge : edge + 1])
                factor = spread(
                    [passed[:, way * 8 + i : way * 8 + i + 1] for i in range(8)], 1
                )
                state = factor * state + first_ref[way]
            state = jnp.concatenate([state, jnp.zeros_like(state)], axis=0).astype(BF16)
            decay = spread([decays[:, way * 8 + i : way * 8 + i + 1] for i in range(8)], BLOCK)
            mixer = y_ref[way, block, :].astype(F32) + decay * dot(c_ref[way, block, :], state)
            gated = mixer * gate
            square = (gated * gated).astype(BF16)
            mean = jnp.concatenate(
                [dot(square[:, g * inner : (g + 1) * inner], same) for g in range(2)], axis=1
            ) * (1.0 / HEADP)
            normed = gated * lax.rsqrt(mean + EPS)
            total = normed if total is None else total + normed
        mixed = (total * gains_ref[0:1]).astype(BF16)
        for copy in copies[6:8] if b == 0 else ():
            copy.wait()
        give_ref[block, :] = dot(mixed, w_ref[:, part:]).astype(BF16)
        keep_ref[block, :] = dot(mixed, w_ref[:, :part]) + hidden_ref[block, :].astype(F32)


def shards(
    hidden_in,
    proj_zx,
    proj_bc,
    proj_dt,
    conv_x,
    conv_bc,
    dt_bias,
    decay_exp,
    skip_gain,
    norm_gain,
    out_proj,
):
    rows, width = hidden_in.shape[0], hidden_in.shape[1] // 2
    inner = proj_zx.shape[2]
    count = math.prod(lax.axis_size(axis) for axis in SEQ)
    rise = [(i, (i + 1) % count) for i in range(count)]
    fall = [((i + 1) % count, i) for i in range(count)]
    swap = [(0, 1), (1, 0)]
    x_hi, core = lax.axis_index("x_hi"), lax.axis_index("core")
    place = jnp.stack([x_hi, core, lax.axis_index(SEQ), jnp.int32(count)]).astype(jnp.int32)
    zx = proj_zx.reshape(width, 2 * inner)

    pack, head, tail = call(
        pack_kernel,
        (
            struct((PACKED, inner), BF16),
            struct((HALO, width), BF16),
            struct((HALO, width), BF16),
        ),
        [SMEM, VMEM] + [HBM] * 7,
        (VMEM,) * 3,
        cost(1_000_000, 0, 1_000_000),
        scratch=[
            pltpu.VMEM((4, width), BF16),
            pltpu.VMEM((REACH + 1, inner), BF16),
            pltpu.VMEM((1, 4), F32),
            pltpu.VMEM((1, 4), jnp.int32),
            pltpu.VMEM((1, 4), F32),
            pltpu.VMEM((1, inner), F32),
            dma(8),
        ],
    )(
        place,
        zx[:, inner:],
        *lying(
            proj_dt.T,
            conv_x,
            dt_bias.reshape(1, 4),
            decay_exp.reshape(1, 4),
            skip_gain.reshape(1, 4),
            norm_gain.reshape(1, inner),
            hidden_in,
        ),
    )
    beside = (("seq_1", "x_hi"), [(0, 3), (3, 0), (1, 2), (2, 1)])
    other_pack = lax.ppermute(pack, *beside)
    prev = lax.ppermute(tail, SEQ, rise)
    following = lax.ppermute(head, SEQ, fall)

    kept = (
        ((rows, width), BF16),
        ((2, rows, 2 * inner), BF16),
        ((2, rows, LANES), BF16),
        ((2, rows, LANES), BF16),
        ((rows, LANES), F32),
        ((48, rows), F32),
        ((2, STATE, 2 * inner), F32),
        ((8, 2 * inner), F32),
        ((count, 16, LANES), BF16),
    )
    own_z, own_out, prev, following = lax.optimization_barrier(
        (zx[:, :inner], out_proj, prev, following)
    )
    other_z = lax.ppermute(own_z, *beside)
    other_out = lax.ppermute(own_out, *beside)
    u, x, b, c, cols, turned, first, gains, send = call(
        front_kernel,
        tuple(stored(*k) for k in kept),
        [SMEM] + [VMEM] * 7,
        (HBM,) * 9,
        cost(8_000_000_000, 1_000_000, 24_000_000),
        scratch=[pltpu.VMEM(*k) for k in kept]
        + [pltpu.VMEM((2 * inner // LANES + 1, rows + 2 * HALO, LANES), F32), dma(10)],
    )(place, hidden_in, prev, following, pack, other_pack, proj_bc, conv_bc)

    got = lax.all_to_all(send, SEQ, 0, 0, tiled=True)
    y = call(
        inside_kernel,
        stored((2, rows, 2 * inner), BF16),
        [HBM] * 6,
        HBM,
        cost(4_000_000_000, 2_000_000, 6_000_000),
        scratch=[
            pltpu.VMEM((2, rows, 2 * inner), BF16),
            pltpu.VMEM((2, rows, LANES), BF16),
            pltpu.VMEM((2, rows, LANES), BF16),
            pltpu.VMEM((48, rows), F32),
            pltpu.VMEM((rows, LANES), F32),
            pltpu.VMEM((8, 2 * inner), F32),
            pltpu.VMEM((2, rows, 2 * inner), BF16),
            dma(11),
        ],
    )(*lying(x, b, c, turned, cols, gains))
    scanned = call(
        scan_kernel,
        struct((count, 8, LANES), BF16),
        [SMEM, VMEM, HBM],
        VMEM,
        cost(1_000_000, 0, 400_000),
    )(place, got, *lying(y))
    gate, weights = call(
        ready_kernel,
        (stored((rows, 2 * inner), BF16), stored((2 * inner, 2 * inner), BF16)),
        [SMEM, HBM] + [VMEM] * 4 + [HBM],
        (HBM, HBM),
        cost(1_000_000_000, 300_000, 3_000_000),
        scratch=[
            pltpu.VMEM((rows, width), BF16),
            pltpu.VMEM((rows, 2 * inner), BF16),
            pltpu.VMEM((2 * inner, 2 * inner), BF16),
            dma(3),
        ],
    )(place, *lying(u), own_z, other_z, own_out, other_out, *lying(scanned))
    came = lax.all_to_all(scanned, SEQ, 0, 0, tiled=True)

    keep, give = call(
        back_kernel,
        (struct((rows, inner), F32), struct((rows, inner), BF16)),
        [SMEM, HBM, HBM, VMEM] + [HBM] * 6,
        (VMEM, VMEM),
        cost(2_000_000_000, 600_000, 6_000_000),
        scratch=[
            pltpu.VMEM((2, rows, 2 * inner), BF16),
            pltpu.VMEM((2, rows, LANES), BF16),
            pltpu.VMEM((2, STATE, 2 * inner), F32),
            pltpu.VMEM((rows, LANES), F32),
            pltpu.VMEM((rows, 2 * inner), BF16),
            pltpu.VMEM((8, 2 * inner), F32),
            pltpu.VMEM((2 * inner, 2 * inner), BF16),
            pltpu.VMEM((rows, inner), BF16),
            pltpu.VMEM((2, STATE, 2 * inner), F32),
            dma(10),
        ],
    )(
        place,
        *lying(y, c),
        came,
        *lying(first, cols, gate, gains, weights, hidden_in),
    )
    taken = lax.ppermute(give, "core", swap)
    return (keep + taken.astype(F32)).astype(BF16)


def solution(mesh):
    torus = Mesh(mesh.devices.reshape(8, 2, 4, 2, 2), SEQ + CH)
    placed = (
        P(SEQ, None),
        P(None, None, CH),
        P(),
        P(None, CH),
        P(None, CH),
        P(),
        P(CH),
        P(CH),
        P(CH),
        P(CH),
        P(CH, None),
    )
    return jax.shard_map(
        shards, mesh=torus, in_specs=placed, out_specs=P(SEQ, CH), check_vma=False
    )
```

```python
import math

import jax
import jax.numpy as jnp
from jax import lax
from jax.experimental import pallas as pl
from jax.experimental.pallas import tpu as pltpu
from jax.sharding import Mesh
from jax.sharding import PartitionSpec as P

BLOCK = 256
STATE = 64
HEADP = 64
REACH = 3
HALO = 8
LANES = 128
SEQ = ("seq_0", "seq_1", "seq_2")
CH = ("x_hi", "core")
EPS = 1e-05
LOG2E = math.log2(math.e)
F32 = jnp.float32
BF16 = jnp.bfloat16

VMEM = pl.BlockSpec(memory_space=pltpu.VMEM)
HBM = pl.BlockSpec(memory_space=pltpu.HBM)
SMEM = pl.BlockSpec(memory_space=pltpu.SMEM)


def cost(flops, transcendentals, bytes_accessed):
    return pl.CostEstimate(
        flops=flops, transcendentals=transcendentals, bytes_accessed=bytes_accessed
    )


def struct(shape, dtype):
    return jax.ShapeDtypeStruct(shape, dtype)


def lying(*arrays):
    return [pltpu.with_memory_space_constraint(array, pltpu.HBM) for array in arrays]


def start_copies(pairs, sems):
    copies = [
        pltpu.make_async_copy(source, target, sems.at[i]) for i, (source, target) in enumerate(pairs)
    ]
    for copy in copies:
        copy.start()
    return copies


def dma(n):
    return pltpu.SemaphoreType.DMA((n,))


def call(kernel, out_shape, specs, out_specs, estimate, mib=16, scratch=()):
    return pl.pallas_call(
        kernel,
        out_shape=out_shape,
        in_specs=specs,
        out_specs=out_specs,
        scratch_shapes=scratch,
        compiler_params=pltpu.CompilerParams(vmem_limit_bytes=mib * 1024 * 1024),
        cost_estimate=estimate,
    )


def iota(shape, dim):
    return lax.broadcasted_iota(jnp.int32, shape, dim)


def dot(a, b):
    return jnp.dot(a, b, preferred_element_type=F32)


def dot_nt(a, b):
    return lax.dot_general(a, b, (((1,), (1,)), ((), ())), preferred_element_type=F32)


def sigmoid(v):
    return 0.5 * jnp.tanh(0.5 * v) + 0.5


def parts_of(value):
    hi = value.astype(BF16).astype(F32)
    rest = value - hi
    mid = rest.astype(BF16).astype(F32)
    return hi, mid, rest - mid


def orient(n, strand):
    source, target = iota((n, n), 0), iota((n, n), 1)
    return (source == jnp.where(strand == 0, target, n - 1 - target)).astype(BF16)


DT_AT, TAP_AT, SMALL_AT, PACKED = 512, 520, 528, 544


def pack_kernel(
    place_ref, x_ref, dt_hbm, taps_hbm, bias_hbm, exp_hbm, skip_hbm, gain_hbm, hidden_hbm,
    pack_ref, head_ref, tail_ref,
    dt_ref, taps_ref, bias_ref, exp_ref, skip_ref, gain_ref, sems,
):
    inner, heads = x_ref.shape[1], dt_ref.shape[0]
    rows, width = hidden_hbm.shape[0], hidden_hbm.shape[1] // 2
    columns = pl.ds(pl.multiple_of(place_ref[0] * width, width), width)
    copies = start_copies(
        (
            (dt_hbm, dt_ref),
            (taps_hbm, taps_ref),
            (bias_hbm, bias_ref),
            (exp_hbm, exp_ref),
            (skip_hbm, skip_ref),
            (gain_hbm, gain_ref),
            (hidden_hbm.at[pl.ds(0, HALO), columns], head_ref),
            (hidden_hbm.at[pl.ds(rows - HALO, HALO), columns], tail_ref),
        ),
        sems,
    )
    pack_ref[:DT_AT] = x_ref[...]
    for copy in copies:
        copy.wait()
    lane = iota((1, inner), 1)
    small = jnp.zeros((1, inner), F32)
    for h in range(heads):
        for k, ref in enumerate((bias_ref, exp_ref, skip_ref)):
            value = ref[:, h : h + 1].astype(F32)
            small = jnp.where(lane == k * heads + h, jnp.broadcast_to(value, (1, inner)), small)
    packed = [dt_ref[:, :inner].astype(F32), dt_ref[:, inner:].astype(F32), taps_ref[...].astype(F32)]
    packed.append(jnp.zeros((SMALL_AT - TAP_AT - taps_ref.shape[0], inner), F32))
    packed += parts_of(small) + parts_of(gain_ref[...])
    packed.append(jnp.zeros((PACKED - SMALL_AT - 6, inner), F32))
    pack_ref[DT_AT:] = jnp.concatenate(packed, axis=0).astype(BF16)


def unpack(ref):
    tail = ref[SMALL_AT:].astype(F32)
    return tail[0:1] + tail[1:2] + tail[2:3], tail[3:4] + tail[4:5] + tail[5:6]


def column_of(smalls, at):
    row = iota((8, 1), 0)
    out = jnp.zeros((8, 1), F32)
    for g in range(2):
        for h in range(4):
            out = jnp.where(row == g * 4 + h, smalls[g][:, at + h : at + h + 1], out)
    return out


def spread(pieces, rows):
    half = iota((rows, LANES), 1) < HEADP
    wide = [jnp.broadcast_to(piece, (rows, LANES)) for piece in pieces]
    return jnp.concatenate(
        [jnp.where(half, wide[2 * q], wide[2 * q + 1]) for q in range(4)], axis=1
    )


def front_kernel(
    place_ref, hidden_ref, prev_ref, next_ref, own_ref, other_ref, bc_ref, tapbc_ref,
    u_ref, y_ref, c_ref, cols_ref, first_ref, gains_ref, send_ref,
    x_ref, b_ref, rows_ref, pad_ref,
):
    row_count, width = hidden_ref.shape[0], hidden_ref.shape[1] // 2
    inner = own_ref.shape[1]
    strand, position, count = place_ref[0], place_ref[2], place_ref[3]
    packs = (own_ref, other_ref)
    turn = orient(width, strand)
    u = dot(hidden_ref[:, pl.ds(pl.multiple_of(strand * width, width), width)], turn).astype(BF16)
    u_ref[...] = u
    before = jnp.where(position > 0, prev_ref[...].astype(F32), 0.0)
    after = jnp.where(position < count - 1, next_ref[...].astype(F32), 0.0)
    edge = dot(jnp.concatenate([before, after], axis=0).astype(BF16), turn).astype(BF16)

    raw = jnp.concatenate(
        [
            dot_nt(
                jnp.concatenate(
                    [ref[DT_AT : DT_AT + 4].astype(F32), ref[DT_AT + 4 : DT_AT + 8].astype(F32)],
                    axis=1,
                ).astype(BF16),
                u,
            )
            for ref in packs
        ],
        axis=0,
    )
    smalls, gains = zip(*[unpack(ref) for ref in packs])
    gains_ref[...] = jnp.concatenate(
        [
            jnp.concatenate(gains, axis=1),
            spread([smalls[g][:, 8 + h : 9 + h] for g in range(2) for h in range(4)], 1),
            jnp.zeros((6, 2 * inner), F32),
        ],
        axis=0,
    )
    v = raw + column_of(smalls, 0)
    rate = jnp.exp2(-column_of(smalls, 4)) * LOG2E
    step = jnp.maximum(v, 0.0) + jnp.log1p(jnp.exp(-jnp.abs(v)))
    parts = jnp.concatenate(parts_of(-step * rate), axis=0).astype(BF16)
    ahead = (iota((BLOCK, BLOCK), 0) <= iota((BLOCK, BLOCK), 1)).astype(BF16)
    behind = (iota((BLOCK, BLOCK), 0) >= iota((BLOCK, BLOCK), 1)).astype(BF16)
    cums, ends = [], []
    for b in range(2):
        piece = parts[:, b * BLOCK : (b + 1) * BLOCK]
        both = []
        for mask in (ahead, behind):
            full = dot(piece, mask)
            both.append(full[:8] + full[8:16] + full[16:])
        cums.append(jnp.concatenate(both, axis=0))
        last = jnp.concatenate([both[0][:, BLOCK - 1 :], both[1][:, :1]], axis=0)
        ends.append(jnp.broadcast_to(last, (16, BLOCK)))
    cum = jnp.concatenate(cums, axis=1)
    end = jnp.concatenate(ends, axis=1)
    step = jnp.concatenate([step, step], axis=0)
    rows_ref[:16] = cum
    rows_ref[16:32] = cum - jnp.log2(step)
    rows_ref[32:] = jnp.exp2(jnp.minimum(end - cum, 0.0)) * step
    cols_ref[...] = jnp.concatenate([cum, jnp.zeros((LANES - 16, row_count), F32)], axis=0).T
    totals = [ends[b][:, :1] for b in range(2)]

    chunk = 32
    mains = [(u, slice(HALO, HALO + row_count)), (edge, None)]
    for piece, where in mains:
        for g in range(3):
            w = packs[g][:DT_AT] if g < 2 else bc_ref[...]
            full = dot(piece, w).astype(BF16).astype(F32)
            for k in range(w.shape[1] // LANES):
                value, at = full[:, k * LANES : (k + 1) * LANES], g * inner // LANES + k
                if where is not None:
                    pad_ref[at, where] = value
                else:
                    pad_ref[at, :HALO] = value[:HALO]
                    pad_ref[at, HALO + row_count :] = value[HALO:]
    taps = jnp.concatenate(
        [ref[TAP_AT : TAP_AT + REACH + 1].astype(F32) for ref in packs]
        + [tapbc_ref[...].astype(F32)],
        axis=1,
    )
    groups = taps.shape[1] // LANES
    low_lane = iota((chunk, LANES), 1) < STATE
    for group in range(groups):
        at = slice(group * LANES, (group + 1) * LANES)
        tap = [taps[j : j + 1, at] for j in range(REACH + 1)]
        for r in range(0, row_count, chunk):
            start = r + HALO - REACH
            window = [
                pad_ref[group, start + k : start + k + chunk] for k in range(2 * REACH + 1)
            ]
            for way in range(2):
                acc = tap[0] * window[0 if way == 0 else 2 * REACH]
                for j in range(1, REACH + 1):
                    acc = acc + tap[j] * window[j if way == 0 else 2 * REACH - j]
                value = (acc * sigmoid(acc)).astype(BF16)
                if group < groups - 1:
                    x_ref[way, r : r + chunk, at] = value
                else:
                    b_ref[way, r : r + chunk, :] = value
                    swapped = pltpu.roll(value.astype(F32), LANES - STATE, 1)
                    c_ref[way, r : r + chunk, :] = jnp.where(low_lane, swapped, 0.0).astype(BF16)


    half = iota((STATE, LANES), 1) < HEADP
    row8 = iota((8, LANES), 0)
    for way in range(2):
        states = []
        for b in range(2):
            block = slice(b * BLOCK, (b + 1) * BLOCK)
            bt = b_ref[way, block, :].astype(F32).T[:STATE]
            tiles = []
            for g in range(2):
                at = 32 + way * 8 + g * 4
                scaled = jnp.concatenate(
                    [
                        (bt * rows_ref[at + h : at + h + 1, block]).astype(BF16)
                        for h in range(4)
                    ],
                    axis=0,
                )
                full = dot(scaled, x_ref[way, block, g * inner : (g + 1) * inner])
                tiles.append(jnp.where(half, full[:64, :128], full[64:128, :128]))
                tiles.append(jnp.where(half, full[128:192, 128:], full[192:, 128:]))
            states.append(tiles)
        first, last = (0, 1) if way == 0 else (1, 0)
        at = slice(way * 8, way * 8 + 8)
        last_total = jnp.exp2(totals[last][at])
        both_total = jnp.exp2(totals[0][at] + totals[1][at])
        factor = spread([last_total[i : i + 1] for i in range(8)], 1)
        whole = spread([both_total[i : i + 1] for i in range(8)], 8)
        for q in range(4):
            lanes = slice(q * LANES, (q + 1) * LANES)
            state = factor[:, lanes] * states[first][q] + states[last][q]
            first_ref[way, :, lanes] = states[first][q]
            hi, mid, low = parts_of(whole[:, lanes])
            decay = jnp.where(
                row8 == 0, hi, jnp.where(row8 == 1, mid, jnp.where(row8 == 2, low, 0.0))
            )
            for n in range(8):
                send_ref[way * 32 + n * 4 + q] = jnp.concatenate(
                    [state[n * 8 : n * 8 + 8], decay], axis=0
                ).astype(BF16)
    inside(x_ref, b_ref, c_ref, rows_ref, cols_ref, gains_ref, y_ref)


def scan_kernel(place_ref, got_ref, out_ref):
    count = got_ref.shape[0]
    backward = place_ref[2] >= count // 2
    state = jnp.zeros((8, LANES), F32)
    for i in range(count):
        k = jnp.where(backward, count - 1 - i, i)
        piece = got_ref[k].astype(F32)
        out_ref[k] = state.astype(BF16)
        decay = jnp.sum(piece[8:], axis=0, keepdims=True)
        state = decay * state + piece[:8]


def inside(x_ref, b_ref, c_ref, rows_ref, cols_ref, gains_ref, y_ref):
    size = 128
    low = iota((size, size), 0) >= iota((size, size), 1)
    high = iota((size, size), 0) <= iota((size, size), 1)
    half = iota((size, LANES), 1) < HEADP
    skip = gains_ref[1:2]
    for way in range(2):
        for b in range(2):
            block = slice(b * BLOCK, (b + 1) * BLOCK)
            scores = dot_nt(c_ref[way, block, :], b_ref[way, block, :])
            for pair in range(4):
                at = slice(pair * LANES, (pair + 1) * LANES)
                for t in range(2):
                    here = slice(b * BLOCK + t * size, b * BLOCK + (t + 1) * size)
                    seen = [s for s in range(2) if (s <= t if way == 0 else s >= t)]
                    lo = b * BLOCK + seen[0] * size
                    hi = b * BLOCK + (seen[-1] + 1) * size
                    outs = []
                    for h in (2 * pair, 2 * pair + 1):
                        i = way * 8 + h
                        gone = jnp.broadcast_to(cols_ref[here, i : i + 1], (size, size))
                        tiles = []
                        for s in seen:
                            there = slice(b * BLOCK + s * size, b * BLOCK + (s + 1) * size)
                            gap = gone - rows_ref[16 + i : 17 + i, there]
                            if s == t:
                                gap = jnp.where(low if way == 0 else high, gap, -jnp.inf)
                            part = scores[t * size : (t + 1) * size, s * size : (s + 1) * size]
                            tiles.append((part * jnp.exp2(gap)).astype(BF16))
                        weights = tiles[0] if len(tiles) == 1 else jnp.concatenate(tiles, axis=1)
                        outs.append(dot(weights, x_ref[way, lo:hi, at]))
                    y_ref[way, here, at] = (
                        jnp.where(half, outs[0], outs[1])
                        + skip[:, at] * x_ref[way, here, at].astype(F32)
                    )


def ready_kernel(
    place_ref, u_ref, own_z_ref, other_z_ref, own_out_ref, other_out_ref, gate_ref, w_ref
):
    rows, columns = own_out_ref.shape
    part = columns // 2
    source, target = iota((columns, columns), 0), iota((columns, columns), 1)
    core = place_ref[1]
    column = jnp.where(target < part, target + core * part, target - core * part)
    wanted = jnp.where(place_ref[0] == 0, column, columns - 1 - column)
    chosen = (source == wanted).astype(BF16)
    w_ref[:rows] = dot(own_out_ref[...], chosen).astype(BF16)
    w_ref[rows:] = dot(other_out_ref[...], chosen).astype(BF16)
    inner = own_z_ref.shape[1]
    for g, ref in enumerate((own_z_ref, other_z_ref)):
        z = dot(u_ref[...], ref[...]).astype(BF16).astype(F32)
        gate_ref[:, g * inner : (g + 1) * inner] = z * sigmoid(z)


def back_kernel(
    place_ref, y_ref, c_ref, came_ref, first_ref, cols_ref, gate_ref, gains_ref, w_ref, hidden_ref,
    keep_ref, give_ref, state_ref,
):
    part = w_ref.shape[1] // 2
    inner = y_ref.shape[2] // 2
    ours = pl.multiple_of((2 * place_ref[0] + place_ref[1]) * part, part)
    blocks = [slice(b * BLOCK, (b + 1) * BLOCK) for b in range(2)]
    same = (iota((inner, inner), 0) // HEADP == iota((inner, inner), 1) // HEADP).astype(BF16)
    for way in range(2):
        for n in range(8):
            for q in range(4):
                state_ref[way, n * 8 : n * 8 + 8, q * LANES : (q + 1) * LANES] = came_ref[
                    way * 32 + n * 4 + q
                ].astype(F32)
    for b, block in enumerate(blocks):
        decays = jnp.exp2(cols_ref[block])
        gate = gate_ref[block, :]
        total = None
        for way in range(2):
            state = state_ref[way]
            if b != way:
                edge = BLOCK - 1 if way == 0 else BLOCK
                passed = jnp.exp2(cols_ref[edge : edge + 1])
                factor = spread(
                    [passed[:, way * 8 + i : way * 8 + i + 1] for i in range(8)], 1
                )
                state = factor * state + first_ref[way]
            state = jnp.concatenate([state, jnp.zeros_like(state)], axis=0).astype(BF16)
            decay = spread([decays[:, way * 8 + i : way * 8 + i + 1] for i in range(8)], BLOCK)
            mixer = y_ref[way, block, :] + decay * dot(c_ref[way, block, :], state)
            gated = mixer * gate
            square = (gated * gated).astype(BF16)
            mean = jnp.concatenate(
                [dot(square[:, g * inner : (g + 1) * inner], same) for g in range(2)], axis=1
            ) * (1.0 / HEADP)
            normed = gated * lax.rsqrt(mean + EPS)
            total = normed if total is None else total + normed
        mixed = (total * gains_ref[0:1]).astype(BF16)
        give_ref[block, :] = dot(mixed, w_ref[:, part:]).astype(BF16)
        keep_ref[block, :] = dot(mixed, w_ref[:, :part]) + hidden_ref[
            block, pl.ds(ours, part)
        ].astype(F32)


def shards(
    hidden_in,
    proj_zx,
    proj_bc,
    proj_dt,
    conv_x,
    conv_bc,
    dt_bias,
    decay_exp,
    skip_gain,
    norm_gain,
    out_proj,
):
    rows, width = hidden_in.shape[0], hidden_in.shape[1] // 2
    inner = proj_zx.shape[2]
    count = math.prod(lax.axis_size(axis) for axis in SEQ)
    rise = [(i, (i + 1) % count) for i in range(count)]
    fall = [((i + 1) % count, i) for i in range(count)]
    swap = [(0, 1), (1, 0)]
    x_hi, core = lax.axis_index("x_hi"), lax.axis_index("core")
    place = jnp.stack([x_hi, core, lax.axis_index(SEQ), jnp.int32(count)]).astype(jnp.int32)
    zx = proj_zx.reshape(width, 2 * inner)

    pack, head, tail = call(
        pack_kernel,
        (
            struct((PACKED, inner), BF16),
            struct((HALO, width), BF16),
            struct((HALO, width), BF16),
        ),
        [SMEM, VMEM] + [HBM] * 7,
        (VMEM,) * 3,
        cost(1_000_000, 0, 1_000_000),
        scratch=[
            pltpu.VMEM((4, width), BF16),
            pltpu.VMEM((REACH + 1, inner), BF16),
            pltpu.VMEM((1, 4), F32),
            pltpu.VMEM((1, 4), jnp.int32),
            pltpu.VMEM((1, 4), F32),
            pltpu.VMEM((1, inner), F32),
            dma(8),
        ],
    )(
        place,
        zx[:, inner:],
        *lying(
            proj_dt.T,
            conv_x,
            dt_bias.reshape(1, 4),
            decay_exp.reshape(1, 4),
            skip_gain.reshape(1, 4),
            norm_gain.reshape(1, inner),
            hidden_in,
        ),
    )
    beside = (("seq_1", "x_hi"), [(0, 3), (3, 0), (1, 2), (2, 1)])
    other_pack = lax.ppermute(pack, *beside)
    prev = lax.ppermute(tail, SEQ, rise)
    following = lax.ppermute(head, SEQ, fall)

    own_z, own_out, prev, following = lax.optimization_barrier(
        (zx[:, :inner], out_proj, prev, following)
    )
    other_z = lax.ppermute(own_z, *beside)
    other_out = lax.ppermute(own_out, *beside)
    u, y, c, cols, first, gains, send = call(
        front_kernel,
        (
            struct((rows, width), BF16),
            struct((2, rows, 2 * inner), F32),
            struct((2, rows, LANES), BF16),
            struct((rows, LANES), F32),
            struct((2, STATE, 2 * inner), F32),
            struct((8, 2 * inner), F32),
            struct((count, 16, LANES), BF16),
        ),
        [SMEM] + [VMEM] * 7,
        (VMEM,) * 7,
        cost(8_000_000_000, 3_000_000, 24_000_000),
        scratch=[
            pltpu.VMEM((2, rows, 2 * inner), BF16),
            pltpu.VMEM((2, rows, LANES), BF16),
            pltpu.VMEM((48, rows), F32),
            pltpu.VMEM((2 * inner // LANES + 1, rows + 2 * HALO, LANES), F32),
        ],
    )(place, hidden_in, prev, following, pack, other_pack, proj_bc, conv_bc)
    gate, weights = call(
        ready_kernel,
        (struct((rows, 2 * inner), F32), struct((2 * inner, 2 * inner), BF16)),
        [SMEM] + [VMEM] * 5,
        (VMEM, VMEM),
        cost(1_000_000_000, 300_000, 3_000_000),
    )(place, u, own_z, other_z, own_out, other_out)

    send, gate, weights = lax.optimization_barrier((send, gate, weights))
    got = lax.all_to_all(send, SEQ, 0, 0, tiled=True)
    scanned = call(
        scan_kernel,
        struct((count, 8, LANES), BF16),
        [SMEM, VMEM],
        VMEM,
        cost(1_000_000, 0, 400_000),
    )(place, got)
    came = lax.all_to_all(scanned, SEQ, 0, 0, tiled=True)

    keep, give = call(
        back_kernel,
        (struct((rows, inner), F32), struct((rows, inner), BF16)),
        [SMEM] + [VMEM] * 9,
        (VMEM, VMEM),
        cost(2_000_000_000, 600_000, 6_000_000),
        scratch=[pltpu.VMEM((2, STATE, 2 * inner), F32)],
    )(place, y, c, came, first, cols, gate, gains, weights, hidden_in)
    taken = lax.ppermute(give, "core", swap)
    return (keep + taken.astype(F32)).astype(BF16)


def solution(mesh):
    torus = Mesh(mesh.devices.reshape(8, 2, 4, 2, 2), SEQ + CH)
    placed = (
        P(SEQ, None),
        P(None, None, CH),
        P(),
        P(None, CH),
        P(None, CH),
        P(),
        P(CH),
        P(CH),
        P(CH),
        P(CH),
        P(CH, None),
    )
    return jax.shard_map(
        shards, mesh=torus, in_specs=placed, out_specs=P(SEQ, CH), check_vma=False
    )
```

```python
import math

import jax
import jax.numpy as jnp
from jax import lax
from jax.experimental import pallas as pl
from jax.experimental.pallas import tpu as pltpu
from jax.sharding import Mesh
from jax.sharding import PartitionSpec as P

BLOCK = 256
STATE = 64
HEADP = 64
REACH = 3
HALO = 8
LANES = 128
SEQ = ("seq_0", "seq_1", "seq_2")
CH = ("x_hi", "core")
EPS = 1e-05
LOG2E = math.log2(math.e)
F32 = jnp.float32
BF16 = jnp.bfloat16

VMEM = pl.BlockSpec(memory_space=pltpu.VMEM)
HBM = pl.BlockSpec(memory_space=pltpu.HBM)
SMEM = pl.BlockSpec(memory_space=pltpu.SMEM)


def cost(flops, transcendentals, bytes_accessed):
    return pl.CostEstimate(
        flops=flops, transcendentals=transcendentals, bytes_accessed=bytes_accessed
    )


def struct(shape, dtype):
    return jax.ShapeDtypeStruct(shape, dtype)


def lying(*arrays):
    return [pltpu.with_memory_space_constraint(array, pltpu.HBM) for array in arrays]


def start_copies(pairs, sems):
    copies = [
        pltpu.make_async_copy(source, target, sems.at[i]) for i, (source, target) in enumerate(pairs)
    ]
    for copy in copies:
        copy.start()
    return copies


def dma(n):
    return pltpu.SemaphoreType.DMA((n,))


def call(kernel, out_shape, specs, out_specs, estimate, mib=16, scratch=()):
    return pl.pallas_call(
        kernel,
        out_shape=out_shape,
        in_specs=specs,
        out_specs=out_specs,
        scratch_shapes=scratch,
        compiler_params=pltpu.CompilerParams(vmem_limit_bytes=mib * 1024 * 1024),
        cost_estimate=estimate,
    )


def iota(shape, dim):
    return lax.broadcasted_iota(jnp.int32, shape, dim)


def dot(a, b):
    return jnp.dot(a, b, preferred_element_type=F32)


def dot_nt(a, b):
    return lax.dot_general(a, b, (((1,), (1,)), ((), ())), preferred_element_type=F32)


def sigmoid(v):
    return 0.5 * jnp.tanh(0.5 * v) + 0.5


def parts_of(value):
    hi = value.astype(BF16).astype(F32)
    rest = value - hi
    mid = rest.astype(BF16).astype(F32)
    return hi, mid, rest - mid


def orient(n, strand):
    source, target = iota((n, n), 0), iota((n, n), 1)
    return (source == jnp.where(strand == 0, target, n - 1 - target)).astype(BF16)


DT_AT, TAP_AT, SMALL_AT, PACKED = 0, 8, 16, 32


def pack_kernel(
    place_ref, dt_hbm, taps_hbm, bias_hbm, exp_hbm, skip_hbm, gain_hbm, hidden_hbm,
    pack_ref, head_ref, tail_ref,
    dt_ref, taps_ref, bias_ref, exp_ref, skip_ref, gain_ref, sems,
):
    inner, heads = pack_ref.shape[1], dt_ref.shape[0]
    rows, width = hidden_hbm.shape[0], hidden_hbm.shape[1] // 2
    columns = pl.ds(pl.multiple_of(place_ref[0] * width, width), width)
    copies = start_copies(
        (
            (dt_hbm, dt_ref),
            (taps_hbm, taps_ref),
            (bias_hbm, bias_ref),
            (exp_hbm, exp_ref),
            (skip_hbm, skip_ref),
            (gain_hbm, gain_ref),
            (hidden_hbm.at[pl.ds(0, HALO), columns], head_ref),
            (hidden_hbm.at[pl.ds(rows - HALO, HALO), columns], tail_ref),
        ),
        sems,
    )
    for copy in copies:
        copy.wait()
    lane = iota((1, inner), 1)
    small = jnp.zeros((1, inner), F32)
    for h in range(heads):
        for k, ref in enumerate((bias_ref, exp_ref, skip_ref)):
            value = ref[:, h : h + 1].astype(F32)
            small = jnp.where(lane == k * heads + h, jnp.broadcast_to(value, (1, inner)), small)
    packed = [dt_ref[:, :inner].astype(F32), dt_ref[:, inner:].astype(F32), taps_ref[...].astype(F32)]
    packed.append(jnp.zeros((SMALL_AT - TAP_AT - taps_ref.shape[0], inner), F32))
    packed += parts_of(small) + parts_of(gain_ref[...])
    packed.append(jnp.zeros((PACKED - SMALL_AT - 6, inner), F32))
    pack_ref[...] = jnp.concatenate(packed, axis=0).astype(BF16)


def unpack(ref):
    tail = ref[SMALL_AT:].astype(F32)
    return tail[0:1] + tail[1:2] + tail[2:3], tail[3:4] + tail[4:5] + tail[5:6]


def column_of(smalls, at):
    row = iota((8, 1), 0)
    out = jnp.zeros((8, 1), F32)
    for g in range(2):
        for h in range(4):
            out = jnp.where(row == g * 4 + h, smalls[g][:, at + h : at + h + 1], out)
    return out


def spread(pieces, rows):
    half = iota((rows, LANES), 1) < HEADP
    wide = [jnp.broadcast_to(piece, (rows, LANES)) for piece in pieces]
    return jnp.concatenate(
        [jnp.where(half, wide[2 * q], wide[2 * q + 1]) for q in range(4)], axis=1
    )


def front_kernel(
    place_ref, hidden_ref, prev_ref, next_ref, own_zx_ref, other_zx_ref, own_ref, other_ref, bc_ref,
    tapbc_ref, gate_ref, y_ref, c_ref, cols_ref, first_ref, gains_ref, send_ref,
    x_ref, b_ref, rows_ref, pad_ref,
):
    row_count, width = hidden_ref.shape[0], hidden_ref.shape[1] // 2
    inner = own_ref.shape[1]
    strand, position, count = place_ref[0], place_ref[2], place_ref[3]
    packs = (own_ref, other_ref)
    projections = (own_zx_ref, other_zx_ref)
    turn = orient(width, strand)
    u = dot(hidden_ref[:, pl.ds(pl.multiple_of(strand * width, width), width)], turn).astype(BF16)
    before = jnp.where(position > 0, prev_ref[...].astype(F32), 0.0)
    after = jnp.where(position < count - 1, next_ref[...].astype(F32), 0.0)
    edge = dot(jnp.concatenate([before, after], axis=0).astype(BF16), turn).astype(BF16)

    raw = jnp.concatenate(
        [
            dot_nt(
                jnp.concatenate(
                    [ref[DT_AT : DT_AT + 4].astype(F32), ref[DT_AT + 4 : DT_AT + 8].astype(F32)],
                    axis=1,
                ).astype(BF16),
                u,
            )
            for ref in packs
        ],
        axis=0,
    )
    smalls, gains = zip(*[unpack(ref) for ref in packs])
    gains_ref[...] = jnp.concatenate(
        [
            jnp.concatenate(gains, axis=1),
            spread([smalls[g][:, 8 + h : 9 + h] for g in range(2) for h in range(4)], 1),
            jnp.zeros((6, 2 * inner), F32),
        ],
        axis=0,
    )
    v = raw + column_of(smalls, 0)
    rate = jnp.exp2(-column_of(smalls, 4)) * LOG2E
    step = jnp.maximum(v, 0.0) + jnp.log1p(jnp.exp(-jnp.abs(v)))
    parts = jnp.concatenate(parts_of(-step * rate), axis=0).astype(BF16)
    ahead = (iota((BLOCK, BLOCK), 0) <= iota((BLOCK, BLOCK), 1)).astype(BF16)
    behind = (iota((BLOCK, BLOCK), 0) >= iota((BLOCK, BLOCK), 1)).astype(BF16)
    cums, ends = [], []
    for b in range(2):
        piece = parts[:, b * BLOCK : (b + 1) * BLOCK]
        both = []
        for mask in (ahead, behind):
            full = dot(piece, mask)
            both.append(full[:8] + full[8:16] + full[16:])
        cums.append(jnp.concatenate(both, axis=0))
        last = jnp.concatenate([both[0][:, BLOCK - 1 :], both[1][:, :1]], axis=0)
        ends.append(jnp.broadcast_to(last, (16, BLOCK)))
    cum = jnp.concatenate(cums, axis=1)
    end = jnp.concatenate(ends, axis=1)
    step = jnp.concatenate([step, step], axis=0)
    rows_ref[:16] = cum
    rows_ref[16:32] = cum - jnp.log2(step)
    rows_ref[32:] = jnp.exp2(jnp.minimum(end - cum, 0.0)) * step
    cols_ref[...] = jnp.concatenate([cum, jnp.zeros((LANES - 16, row_count), F32)], axis=0).T
    totals = [ends[b][:, :1] for b in range(2)]

    chunk = 32
    mains = [(u, slice(HALO, HALO + row_count)), (edge, None)]
    for piece, where in mains:
        for g in range(3):
            w = projections[g][:, inner:] if g < 2 else bc_ref[...]
            full = dot(piece, w).astype(BF16).astype(F32)
            for k in range(w.shape[1] // LANES):
                value, at = full[:, k * LANES : (k + 1) * LANES], g * inner // LANES + k
                if where is not None:
                    pad_ref[at, where] = value
                else:
                    pad_ref[at, :HALO] = value[:HALO]
                    pad_ref[at, HALO + row_count :] = value[HALO:]
    taps = jnp.concatenate(
        [ref[TAP_AT : TAP_AT + REACH + 1].astype(F32) for ref in packs]
        + [tapbc_ref[...].astype(F32)],
        axis=1,
    )
    groups = taps.shape[1] // LANES
    low_lane = iota((chunk, LANES), 1) < STATE
    for group in range(groups):
        at = slice(group * LANES, (group + 1) * LANES)
        tap = [taps[j : j + 1, at] for j in range(REACH + 1)]
        for r in range(0, row_count, chunk):
            start = r + HALO - REACH
            window = [
                pad_ref[group, start + k : start + k + chunk] for k in range(2 * REACH + 1)
            ]
            for way in range(2):
                acc = tap[0] * window[0 if way == 0 else 2 * REACH]
                for j in range(1, REACH + 1):
                    acc = acc + tap[j] * window[j if way == 0 else 2 * REACH - j]
                value = (acc * sigmoid(acc)).astype(BF16)
                if group < groups - 1:
                    x_ref[way, r : r + chunk, at] = value
                else:
                    b_ref[way, r : r + chunk, :] = value
                    swapped = pltpu.roll(value.astype(F32), LANES - STATE, 1)
                    c_ref[way, r : r + chunk, :] = jnp.where(low_lane, swapped, 0.0).astype(BF16)


    half = iota((STATE, LANES), 1) < HEADP
    row8 = iota((8, LANES), 0)
    for way in range(2):
        states = []
        for b in range(2):
            block = slice(b * BLOCK, (b + 1) * BLOCK)
            bt = b_ref[way, block, :].astype(F32).T[:STATE]
            tiles = []
            for g in range(2):
                at = 32 + way * 8 + g * 4
                scaled = jnp.concatenate(
                    [
                        (bt * rows_ref[at + h : at + h + 1, block]).astype(BF16)
                        for h in range(4)
                    ],
                    axis=0,
                )
                full = dot(scaled, x_ref[way, block, g * inner : (g + 1) * inner])
                tiles.append(jnp.where(half, full[:64, :128], full[64:128, :128]))
                tiles.append(jnp.where(half, full[128:192, 128:], full[192:, 128:]))
            states.append(tiles)
        first, last = (0, 1) if way == 0 else (1, 0)
        at = slice(way * 8, way * 8 + 8)
        last_total = jnp.exp2(totals[last][at])
        both_total = jnp.exp2(totals[0][at] + totals[1][at])
        factor = spread([last_total[i : i + 1] for i in range(8)], 1)
        whole = spread([both_total[i : i + 1] for i in range(8)], 8)
        for q in range(4):
            lanes = slice(q * LANES, (q + 1) * LANES)
            state = factor[:, lanes] * states[first][q] + states[last][q]
            first_ref[way, :, lanes] = states[first][q]
            hi, mid, low = parts_of(whole[:, lanes])
            decay = jnp.where(
                row8 == 0, hi, jnp.where(row8 == 1, mid, jnp.where(row8 == 2, low, 0.0))
            )
            for n in range(8):
                send_ref[way * 32 + n * 4 + q] = jnp.concatenate(
                    [state[n * 8 : n * 8 + 8], decay], axis=0
                ).astype(BF16)
    for g, ref in enumerate(projections):
        z = dot(u, ref[:, :inner]).astype(BF16).astype(F32)
        gate_ref[:, g * inner : (g + 1) * inner] = z * sigmoid(z)
    inside(x_ref, b_ref, c_ref, rows_ref, cols_ref, gains_ref, y_ref)


def scan_kernel(place_ref, got_ref, out_ref):
    count = got_ref.shape[0]
    backward = place_ref[2] >= count // 2
    state = jnp.zeros((8, LANES), F32)
    for i in range(count):
        k = jnp.where(backward, count - 1 - i, i)
        piece = got_ref[k].astype(F32)
        out_ref[k] = state.astype(BF16)
        decay = jnp.sum(piece[8:], axis=0, keepdims=True)
        state = decay * state + piece[:8]


def inside(x_ref, b_ref, c_ref, rows_ref, cols_ref, gains_ref, y_ref):
    size = 128
    low = iota((size, size), 0) >= iota((size, size), 1)
    high = iota((size, size), 0) <= iota((size, size), 1)
    half = iota((size, LANES), 1) < HEADP
    skip = gains_ref[1:2]
    for way in range(2):
        for b in range(2):
            block = slice(b * BLOCK, (b + 1) * BLOCK)
            scores = dot_nt(c_ref[way, block, :], b_ref[way, block, :])
            for pair in range(4):
                at = slice(pair * LANES, (pair + 1) * LANES)
                for t in range(2):
                    here = slice(b * BLOCK + t * size, b * BLOCK + (t + 1) * size)
                    seen = [s for s in range(2) if (s <= t if way == 0 else s >= t)]
                    lo = b * BLOCK + seen[0] * size
                    hi = b * BLOCK + (seen[-1] + 1) * size
                    outs = []
                    for h in (2 * pair, 2 * pair + 1):
                        i = way * 8 + h
                        gone = jnp.broadcast_to(cols_ref[here, i : i + 1], (size, size))
                        tiles = []
                        for s in seen:
                            there = slice(b * BLOCK + s * size, b * BLOCK + (s + 1) * size)
                            gap = gone - rows_ref[16 + i : 17 + i, there]
                            if s == t:
                                gap = jnp.where(low if way == 0 else high, gap, -jnp.inf)
                            part = scores[t * size : (t + 1) * size, s * size : (s + 1) * size]
                            tiles.append((part * jnp.exp2(gap)).astype(BF16))
                        weights = tiles[0] if len(tiles) == 1 else jnp.concatenate(tiles, axis=1)
                        outs.append(dot(weights, x_ref[way, lo:hi, at]))
                    y_ref[way, here, at] = (
                        jnp.where(half, outs[0], outs[1])
                        + skip[:, at] * x_ref[way, here, at].astype(F32)
                    )


def back_kernel(
    place_ref, y_ref, c_ref, came_ref, first_ref, cols_ref, gate_ref, gains_ref, own_out_ref,
    other_out_ref, hidden_ref, keep_ref, give_ref, state_ref, w_ref,
):
    rows, columns = own_out_ref.shape
    part = columns // 2
    source, target = iota((columns, columns), 0), iota((columns, columns), 1)
    column = jnp.where(target < part, target + place_ref[1] * part, target - place_ref[1] * part)
    wanted = jnp.where(place_ref[0] == 0, column, columns - 1 - column)
    chosen = (source == wanted).astype(BF16)
    w_ref[:rows] = dot(own_out_ref[...], chosen).astype(BF16)
    w_ref[rows:] = dot(other_out_ref[...], chosen).astype(BF16)
    inner = y_ref.shape[2] // 2
    ours = pl.multiple_of((2 * place_ref[0] + place_ref[1]) * part, part)
    blocks = [slice(b * BLOCK, (b + 1) * BLOCK) for b in range(2)]
    same = (iota((inner, inner), 0) // HEADP == iota((inner, inner), 1) // HEADP).astype(BF16)
    for way in range(2):
        for n in range(8):
            for q in range(4):
                state_ref[way, n * 8 : n * 8 + 8, q * LANES : (q + 1) * LANES] = came_ref[
                    way * 32 + n * 4 + q
                ].astype(F32)
    for b, block in enumerate(blocks):
        decays = jnp.exp2(cols_ref[block])
        gate = gate_ref[block, :]
        total = None
        for way in range(2):
            state = state_ref[way]
            if b != way:
                edge = BLOCK - 1 if way == 0 else BLOCK
                passed = jnp.exp2(cols_ref[edge : edge + 1])
                factor = spread(
                    [passed[:, way * 8 + i : way * 8 + i + 1] for i in range(8)], 1
                )
                state = factor * state + first_ref[way]
            state = jnp.concatenate([state, jnp.zeros_like(state)], axis=0).astype(BF16)
            decay = spread([decays[:, way * 8 + i : way * 8 + i + 1] for i in range(8)], BLOCK)
            mixer = y_ref[way, block, :] + decay * dot(c_ref[way, block, :], state)
            gated = mixer * gate
            square = (gated * gated).astype(BF16)
            mean = jnp.concatenate(
                [dot(square[:, g * inner : (g + 1) * inner], same) for g in range(2)], axis=1
            ) * (1.0 / HEADP)
            normed = gated * lax.rsqrt(mean + EPS)
            total = normed if total is None else total + normed
        mixed = (total * gains_ref[0:1]).astype(BF16)
        give_ref[block, :] = dot(mixed, w_ref[:, part:]).astype(BF16)
        keep_ref[block, :] = dot(mixed, w_ref[:, :part]) + hidden_ref[
            block, pl.ds(ours, part)
        ].astype(F32)


def shards(
    hidden_in,
    proj_zx,
    proj_bc,
    proj_dt,
    conv_x,
    conv_bc,
    dt_bias,
    decay_exp,
    skip_gain,
    norm_gain,
    out_proj,
):
    rows, width = hidden_in.shape[0], hidden_in.shape[1] // 2
    inner = proj_zx.shape[2]
    count = math.prod(lax.axis_size(axis) for axis in SEQ)
    rise = [(i, (i + 1) % count) for i in range(count)]
    fall = [((i + 1) % count, i) for i in range(count)]
    swap = [(0, 1), (1, 0)]
    x_hi, core = lax.axis_index("x_hi"), lax.axis_index("core")
    place = jnp.stack([x_hi, core, lax.axis_index(SEQ), jnp.int32(count)]).astype(jnp.int32)
    zx = proj_zx.reshape(width, 2 * inner)

    pack, head, tail = call(
        pack_kernel,
        (
            struct((PACKED, inner), BF16),
            struct((HALO, width), BF16),
            struct((HALO, width), BF16),
        ),
        [SMEM] + [HBM] * 7,
        (VMEM,) * 3,
        cost(1_000_000, 0, 1_000_000),
        scratch=[
            pltpu.VMEM((4, width), BF16),
            pltpu.VMEM((REACH + 1, inner), BF16),
            pltpu.VMEM((1, 4), F32),
            pltpu.VMEM((1, 4), jnp.int32),
            pltpu.VMEM((1, 4), F32),
            pltpu.VMEM((1, inner), F32),
            dma(8),
        ],
    )(
        place,
        *lying(
            proj_dt.T,
            conv_x,
            dt_bias.reshape(1, 4),
            decay_exp.reshape(1, 4),
            skip_gain.reshape(1, 4),
            norm_gain.reshape(1, inner),
            hidden_in,
        ),
    )
    beside = (("seq_1", "x_hi"), [(0, 3), (3, 0), (1, 2), (2, 1)])
    other_zx = lax.ppermute(zx, *beside)
    other_pack = lax.ppermute(pack, *beside)
    prev = lax.ppermute(tail, SEQ, rise)
    following = lax.ppermute(head, SEQ, fall)

    own_out, prev, following = lax.optimization_barrier((out_proj, prev, following))
    other_out = lax.ppermute(own_out, *beside)
    gate, y, c, cols, first, gains, send = call(
        front_kernel,
        (
            struct((rows, 2 * inner), F32),
            struct((2, rows, 2 * inner), F32),
            struct((2, rows, LANES), BF16),
            struct((rows, LANES), F32),
            struct((2, STATE, 2 * inner), F32),
            struct((8, 2 * inner), F32),
            struct((count, 16, LANES), BF16),
        ),
        [SMEM] + [VMEM] * 9,
        (VMEM,) * 7,
        cost(8_000_000_000, 3_000_000, 24_000_000),
        scratch=[
            pltpu.VMEM((2, rows, 2 * inner), BF16),
            pltpu.VMEM((2, rows, LANES), BF16),
            pltpu.VMEM((48, rows), F32),
            pltpu.VMEM((2 * inner // LANES + 1, rows + 2 * HALO, LANES), F32),
        ],
    )(place, hidden_in, prev, following, zx, other_zx, pack, other_pack, proj_bc, conv_bc)
    send, other_out = lax.optimization_barrier((send, other_out))
    got = lax.all_to_all(send, SEQ, 0, 0, tiled=True)
    scanned = call(
        scan_kernel,
        struct((count, 8, LANES), BF16),
        [SMEM, VMEM],
        VMEM,
        cost(1_000_000, 0, 400_000),
    )(place, got)
    came = lax.all_to_all(scanned, SEQ, 0, 0, tiled=True)

    keep, give = call(
        back_kernel,
        (struct((rows, inner), F32), struct((rows, inner), BF16)),
        [SMEM] + [VMEM] * 10,
        (VMEM, VMEM),
        cost(2_000_000_000, 600_000, 6_000_000),
        scratch=[
            pltpu.VMEM((2, STATE, 2 * inner), F32),
            pltpu.VMEM((2 * inner, 2 * inner), BF16),
        ],
    )(place, y, c, came, first, cols, gate, gains, out_proj, other_out, hidden_in)
    taken = lax.ppermute(give, "core", swap)
    return (keep + taken.astype(F32)).astype(BF16)


def solution(mesh):
    torus = Mesh(mesh.devices.reshape(8, 2, 4, 2, 2), SEQ + CH)
    placed = (
        P(SEQ, None),
        P(None, None, CH),
        P(),
        P(None, CH),
        P(None, CH),
        P(),
        P(CH),
        P(CH),
        P(CH),
        P(CH),
        P(CH, None),
    )
    return jax.shard_map(
        shards, mesh=torus, in_specs=placed, out_specs=P(SEQ, CH), check_vma=False
    )
```

```python
import math

import jax
import jax.numpy as jnp
from jax import lax
from jax.experimental import pallas as pl
from jax.experimental.pallas import tpu as pltpu
from jax.sharding import Mesh
from jax.sharding import PartitionSpec as P

BLOCK = 256
STATE = 64
HEADP = 64
REACH = 3
HALO = 8
LANES = 128
SEQ = ("seq_0", "seq_1", "seq_2")
CH = ("x_hi", "core")
EPS = 1e-05
LOG2E = math.log2(math.e)
F32 = jnp.float32
BF16 = jnp.bfloat16

VMEM = pl.BlockSpec(memory_space=pltpu.VMEM)
HBM = pl.BlockSpec(memory_space=pltpu.HBM)
SMEM = pl.BlockSpec(memory_space=pltpu.SMEM)


def cost(flops, transcendentals, bytes_accessed):
    return pl.CostEstimate(
        flops=flops, transcendentals=transcendentals, bytes_accessed=bytes_accessed
    )


def struct(shape, dtype):
    return jax.ShapeDtypeStruct(shape, dtype)


def lying(*arrays):
    return [pltpu.with_memory_space_constraint(array, pltpu.HBM) for array in arrays]


def start_copies(pairs, sems):
    copies = [
        pltpu.make_async_copy(source, target, sems.at[i]) for i, (source, target) in enumerate(pairs)
    ]
    for copy in copies:
        copy.start()
    return copies


def dma(n):
    return pltpu.SemaphoreType.DMA((n,))


def call(kernel, out_shape, specs, out_specs, estimate, mib=16, scratch=()):
    return pl.pallas_call(
        kernel,
        out_shape=out_shape,
        in_specs=specs,
        out_specs=out_specs,
        scratch_shapes=scratch,
        compiler_params=pltpu.CompilerParams(vmem_limit_bytes=mib * 1024 * 1024),
        cost_estimate=estimate,
    )


def iota(shape, dim):
    return lax.broadcasted_iota(jnp.int32, shape, dim)


def dot(a, b):
    return jnp.dot(a, b, preferred_element_type=F32)


def dot_nt(a, b):
    return lax.dot_general(a, b, (((1,), (1,)), ((), ())), preferred_element_type=F32)


def sigmoid(v):
    return 0.5 * jnp.tanh(0.5 * v) + 0.5


def parts_of(value):
    hi = value.astype(BF16).astype(F32)
    rest = value - hi
    mid = rest.astype(BF16).astype(F32)
    return hi, mid, rest - mid


def orient(n, strand):
    source, target = iota((n, n), 0), iota((n, n), 1)
    return (source == jnp.where(strand == 0, target, n - 1 - target)).astype(BF16)


DT_AT, TAP_AT, SMALL_AT, PACKED = 512, 520, 528, 544


def pack_kernel(
    place_ref, x_ref, dt_hbm, taps_hbm, bias_hbm, exp_hbm, skip_hbm, gain_hbm, hidden_hbm,
    pack_ref, head_ref, tail_ref,
    dt_ref, taps_ref, bias_ref, exp_ref, skip_ref, gain_ref, sems,
):
    inner, heads = pack_ref.shape[1], dt_ref.shape[0]
    rows, width = hidden_hbm.shape[0], hidden_hbm.shape[1] // 2
    columns = pl.ds(pl.multiple_of(place_ref[0] * width, width), width)
    copies = start_copies(
        (
            (dt_hbm, dt_ref),
            (taps_hbm, taps_ref),
            (bias_hbm, bias_ref),
            (exp_hbm, exp_ref),
            (skip_hbm, skip_ref),
            (gain_hbm, gain_ref),
            (hidden_hbm.at[pl.ds(0, HALO), columns], head_ref),
            (hidden_hbm.at[pl.ds(rows - HALO, HALO), columns], tail_ref),
        ),
        sems,
    )
    pack_ref[:DT_AT] = x_ref[...]
    for copy in copies:
        copy.wait()
    lane = iota((1, inner), 1)
    small = jnp.zeros((1, inner), F32)
    for h in range(heads):
        for k, ref in enumerate((bias_ref, exp_ref, skip_ref)):
            value = ref[:, h : h + 1].astype(F32)
            small = jnp.where(lane == k * heads + h, jnp.broadcast_to(value, (1, inner)), small)
    packed = [dt_ref[:, :inner].astype(F32), dt_ref[:, inner:].astype(F32), taps_ref[...].astype(F32)]
    packed.append(jnp.zeros((SMALL_AT - TAP_AT - taps_ref.shape[0], inner), F32))
    packed += parts_of(small) + parts_of(gain_ref[...])
    packed.append(jnp.zeros((PACKED - SMALL_AT - 6, inner), F32))
    pack_ref[DT_AT:] = jnp.concatenate(packed, axis=0).astype(BF16)


def unpack(ref):
    tail = ref[SMALL_AT:].astype(F32)
    return tail[0:1] + tail[1:2] + tail[2:3], tail[3:4] + tail[4:5] + tail[5:6]


def column_of(smalls, at):
    row = iota((8, 1), 0)
    out = jnp.zeros((8, 1), F32)
    for g in range(2):
        for h in range(4):
            out = jnp.where(row == g * 4 + h, smalls[g][:, at + h : at + h + 1], out)
    return out


def spread(pieces, rows):
    half = iota((rows, LANES), 1) < HEADP
    wide = [jnp.broadcast_to(piece, (rows, LANES)) for piece in pieces]
    return jnp.concatenate(
        [jnp.where(half, wide[2 * q], wide[2 * q + 1]) for q in range(4)], axis=1
    )


def turned_out(place_ref, out_ref):
    columns = out_ref.shape[1]
    part = columns // 2
    source, target = iota((columns, columns), 0), iota((columns, columns), 1)
    column = jnp.where(target < part, target + place_ref[1] * part, target - place_ref[1] * part)
    wanted = jnp.where(place_ref[0] == 0, column, columns - 1 - column)
    return dot(out_ref[...], (source == wanted).astype(BF16)).astype(BF16)


def gated_by(u, w):
    z = dot(u, w).astype(BF16).astype(F32)
    return z * sigmoid(z)


def early_kernel(
    place_ref, hidden_ref, zx_ref, bc_ref, out_ref, u_ref, main_ref, gate_ref, w_ref
):
    width, inner = zx_ref.shape[0], zx_ref.shape[1] // 2
    strand = place_ref[0]
    u = hidden_ref[:, pl.ds(pl.multiple_of(strand * width, width), width)]
    u = dot(u, orient(width, strand)).astype(BF16)
    u_ref[...] = u
    main_ref[:, :inner] = dot(u, zx_ref[:, inner:]).astype(BF16)
    main_ref[:, inner:] = dot(u, bc_ref[...]).astype(BF16)
    gate_ref[...] = gated_by(u, zx_ref[:, :inner])
    w_ref[...] = turned_out(place_ref, out_ref)


def front_kernel(
    place_ref, u_ref, main_ref, prev_ref, next_ref, own_ref, other_ref, bc_ref, tapbc_ref,
    y_ref, c_ref, cols_ref, first_ref, gains_ref, send_ref,
    x_ref, b_ref, rows_ref, pad_ref,
):
    row_count, width = u_ref.shape
    inner = own_ref.shape[1]
    strand, position, count = place_ref[0], place_ref[2], place_ref[3]
    packs = (own_ref, other_ref)
    u = u_ref[...]
    before = jnp.where(position > 0, prev_ref[...].astype(F32), 0.0)
    after = jnp.where(position < count - 1, next_ref[...].astype(F32), 0.0)
    edge = dot(jnp.concatenate([before, after], axis=0).astype(BF16), orient(width, strand))
    edge = edge.astype(BF16)

    raw = jnp.concatenate(
        [
            dot_nt(
                jnp.concatenate(
                    [ref[DT_AT : DT_AT + 4].astype(F32), ref[DT_AT + 4 : DT_AT + 8].astype(F32)],
                    axis=1,
                ).astype(BF16),
                u,
            )
            for ref in packs
        ],
        axis=0,
    )
    smalls, gains = zip(*[unpack(ref) for ref in packs])
    gains_ref[...] = jnp.concatenate(
        [
            jnp.concatenate(gains, axis=1),
            spread([smalls[g][:, 8 + h : 9 + h] for g in range(2) for h in range(4)], 1),
            jnp.zeros((6, 2 * inner), F32),
        ],
        axis=0,
    )
    v = raw + column_of(smalls, 0)
    rate = jnp.exp2(-column_of(smalls, 4)) * LOG2E
    step = jnp.maximum(v, 0.0) + jnp.log1p(jnp.exp(-jnp.abs(v)))
    parts = jnp.concatenate(parts_of(-step * rate), axis=0).astype(BF16)
    ahead = (iota((BLOCK, BLOCK), 0) <= iota((BLOCK, BLOCK), 1)).astype(BF16)
    behind = (iota((BLOCK, BLOCK), 0) >= iota((BLOCK, BLOCK), 1)).astype(BF16)
    cums, ends = [], []
    for b in range(2):
        piece = parts[:, b * BLOCK : (b + 1) * BLOCK]
        both = []
        for mask in (ahead, behind):
            full = dot(piece, mask)
            both.append(full[:8] + full[8:16] + full[16:])
        cums.append(jnp.concatenate(both, axis=0))
        last = jnp.concatenate([both[0][:, BLOCK - 1 :], both[1][:, :1]], axis=0)
        ends.append(jnp.broadcast_to(last, (16, BLOCK)))
    cum = jnp.concatenate(cums, axis=1)
    end = jnp.concatenate(ends, axis=1)
    step = jnp.concatenate([step, step], axis=0)
    rows_ref[:16] = cum
    rows_ref[16:32] = cum - jnp.log2(step)
    rows_ref[32:] = jnp.exp2(jnp.minimum(end - cum, 0.0)) * step
    cols_ref[...] = jnp.concatenate([cum, jnp.zeros((LANES - 16, row_count), F32)], axis=0).T
    totals = [ends[b][:, :1] for b in range(2)]

    chunk = 32
    tiles = inner // LANES
    for g in range(3):
        w = packs[g][:DT_AT] if g < 2 else bc_ref[...]
        if g == 1:
            middle = dot(u, w).astype(BF16)
        else:
            middle = main_ref[:, :inner] if g == 0 else main_ref[:, inner:]
        middle = middle.astype(F32)
        outer = dot(edge, w).astype(BF16).astype(F32)
        for k in range(w.shape[1] // LANES):
            at, lanes = g * tiles + k, slice(k * LANES, (k + 1) * LANES)
            pad_ref[at, :HALO] = outer[:HALO, lanes]
            pad_ref[at, HALO : HALO + row_count] = middle[:, lanes]
            pad_ref[at, HALO + row_count :] = outer[HALO:, lanes]
    taps = jnp.concatenate(
        [ref[TAP_AT : TAP_AT + REACH + 1].astype(F32) for ref in packs]
        + [tapbc_ref[...].astype(F32)],
        axis=1,
    )
    groups = taps.shape[1] // LANES
    low_lane = iota((chunk, LANES), 1) < STATE
    for group in range(groups):
        at = slice(group * LANES, (group + 1) * LANES)
        tap = [taps[j : j + 1, at] for j in range(REACH + 1)]
        for r in range(0, row_count, chunk):
            start = r + HALO - REACH
            window = [
                pad_ref[group, start + k : start + k + chunk] for k in range(2 * REACH + 1)
            ]
            for way in range(2):
                acc = tap[0] * window[0 if way == 0 else 2 * REACH]
                for j in range(1, REACH + 1):
                    acc = acc + tap[j] * window[j if way == 0 else 2 * REACH - j]
                value = (acc * sigmoid(acc)).astype(BF16)
                if group < groups - 1:
                    x_ref[way, r : r + chunk, at] = value
                else:
                    b_ref[way, r : r + chunk, :] = value
                    swapped = pltpu.roll(value.astype(F32), LANES - STATE, 1)
                    c_ref[way, r : r + chunk, :] = jnp.where(low_lane, swapped, 0.0).astype(BF16)


    half = iota((STATE, LANES), 1) < HEADP
    row8 = iota((8, LANES), 0)
    for way in range(2):
        states = []
        for b in range(2):
            block = slice(b * BLOCK, (b + 1) * BLOCK)
            bt = b_ref[way, block, :].astype(F32).T[:STATE]
            tiles = []
            for g in range(2):
                at = 32 + way * 8 + g * 4
                scaled = jnp.concatenate(
                    [
                        (bt * rows_ref[at + h : at + h + 1, block]).astype(BF16)
                        for h in range(4)
                    ],
                    axis=0,
                )
                full = dot(scaled, x_ref[way, block, g * inner : (g + 1) * inner])
                tiles.append(jnp.where(half, full[:64, :128], full[64:128, :128]))
                tiles.append(jnp.where(half, full[128:192, 128:], full[192:, 128:]))
            states.append(tiles)
        first, last = (0, 1) if way == 0 else (1, 0)
        at = slice(way * 8, way * 8 + 8)
        last_total = jnp.exp2(totals[last][at])
        both_total = jnp.exp2(totals[0][at] + totals[1][at])
        factor = spread([last_total[i : i + 1] for i in range(8)], 1)
        whole = spread([both_total[i : i + 1] for i in range(8)], 8)
        for q in range(4):
            lanes = slice(q * LANES, (q + 1) * LANES)
            state = factor[:, lanes] * states[first][q] + states[last][q]
            first_ref[way, :, lanes] = states[first][q]
            hi, mid, low = parts_of(whole[:, lanes])
            decay = jnp.where(
                row8 == 0, hi, jnp.where(row8 == 1, mid, jnp.where(row8 == 2, low, 0.0))
            )
            for n in range(8):
                send_ref[way * 32 + n * 4 + q] = jnp.concatenate(
                    [state[n * 8 : n * 8 + 8], decay], axis=0
                ).astype(BF16)
    inside(x_ref, b_ref, c_ref, rows_ref, cols_ref, gains_ref, y_ref)


def scan_kernel(place_ref, got_ref, out_ref):
    count = got_ref.shape[0]
    backward = place_ref[2] >= count // 2
    state = jnp.zeros((8, LANES), F32)
    for i in range(count):
        k = jnp.where(backward, count - 1 - i, i)
        piece = got_ref[k].astype(F32)
        out_ref[k] = state.astype(BF16)
        decay = jnp.sum(piece[8:], axis=0, keepdims=True)
        state = decay * state + piece[:8]


def inside(x_ref, b_ref, c_ref, rows_ref, cols_ref, gains_ref, y_ref):
    size = 128
    low = iota((size, size), 0) >= iota((size, size), 1)
    high = iota((size, size), 0) <= iota((size, size), 1)
    half = iota((size, LANES), 1) < HEADP
    skip = gains_ref[1:2]
    for way in range(2):
        for b in range(2):
            block = slice(b * BLOCK, (b + 1) * BLOCK)
            scores = dot_nt(c_ref[way, block, :], b_ref[way, block, :])
            for pair in range(4):
                at = slice(pair * LANES, (pair + 1) * LANES)
                for t in range(2):
                    here = slice(b * BLOCK + t * size, b * BLOCK + (t + 1) * size)
                    seen = [s for s in range(2) if (s <= t if way == 0 else s >= t)]
                    lo = b * BLOCK + seen[0] * size
                    hi = b * BLOCK + (seen[-1] + 1) * size
                    outs = []
                    for h in (2 * pair, 2 * pair + 1):
                        i = way * 8 + h
                        gone = jnp.broadcast_to(cols_ref[here, i : i + 1], (size, size))
                        tiles = []
                        for s in seen:
                            there = slice(b * BLOCK + s * size, b * BLOCK + (s + 1) * size)
                            gap = gone - rows_ref[16 + i : 17 + i, there]
                            if s == t:
                                gap = jnp.where(low if way == 0 else high, gap, -jnp.inf)
                            part = scores[t * size : (t + 1) * size, s * size : (s + 1) * size]
                            tiles.append((part * jnp.exp2(gap)).astype(BF16))
                        weights = tiles[0] if len(tiles) == 1 else jnp.concatenate(tiles, axis=1)
                        outs.append(dot(weights, x_ref[way, lo:hi, at]))
                    y_ref[way, here, at] = (
                        jnp.where(half, outs[0], outs[1])
                        + skip[:, at] * x_ref[way, here, at].astype(F32)
                    )


def back_kernel(
    place_ref, y_ref, c_ref, came_ref, first_ref, cols_ref, gains_ref, own_gate_ref, own_w_ref,
    u_ref, other_z_ref, other_out_ref, hidden_ref, keep_ref, give_ref, state_ref, w_ref,
):
    part = own_w_ref.shape[1] // 2
    inner = y_ref.shape[2] // 2
    ours = pl.multiple_of((2 * place_ref[0] + place_ref[1]) * part, part)
    blocks = [slice(b * BLOCK, (b + 1) * BLOCK) for b in range(2)]
    w_ref[:inner] = own_w_ref[...]
    w_ref[inner:] = turned_out(place_ref, other_out_ref)
    same = (iota((inner, inner), 0) // HEADP == iota((inner, inner), 1) // HEADP).astype(BF16)
    for way in range(2):
        for n in range(8):
            for q in range(4):
                state_ref[way, n * 8 : n * 8 + 8, q * LANES : (q + 1) * LANES] = came_ref[
                    way * 32 + n * 4 + q
                ].astype(F32)
    for b, block in enumerate(blocks):
        decays = jnp.exp2(cols_ref[block])
        gate = jnp.concatenate(
            [own_gate_ref[block, :], gated_by(u_ref[block, :], other_z_ref[...])], axis=1
        )
        total = None
        for way in range(2):
            state = state_ref[way]
            if b != way:
                edge = BLOCK - 1 if way == 0 else BLOCK
                passed = jnp.exp2(cols_ref[edge : edge + 1])
                factor = spread(
                    [passed[:, way * 8 + i : way * 8 + i + 1] for i in range(8)], 1
                )
                state = factor * state + first_ref[way]
            state = jnp.concatenate([state, jnp.zeros_like(state)], axis=0).astype(BF16)
            decay = spread([decays[:, way * 8 + i : way * 8 + i + 1] for i in range(8)], BLOCK)
            mixer = y_ref[way, block, :] + decay * dot(c_ref[way, block, :], state)
            gated = mixer * gate
            square = (gated * gated).astype(BF16)
            mean = jnp.concatenate(
                [dot(square[:, g * inner : (g + 1) * inner], same) for g in range(2)], axis=1
            ) * (1.0 / HEADP)
            normed = gated * lax.rsqrt(mean + EPS)
            total = normed if total is None else total + normed
        mixed = (total * gains_ref[0:1]).astype(BF16)
        give_ref[block, :] = dot(mixed, w_ref[:, part:]).astype(BF16)
        keep_ref[block, :] = dot(mixed, w_ref[:, :part]) + hidden_ref[
            block, pl.ds(ours, part)
        ].astype(F32)


def shards(
    hidden_in,
    proj_zx,
    proj_bc,
    proj_dt,
    conv_x,
    conv_bc,
    dt_bias,
    decay_exp,
    skip_gain,
    norm_gain,
    out_proj,
):
    rows, width = hidden_in.shape[0], hidden_in.shape[1] // 2
    inner = proj_zx.shape[2]
    count = math.prod(lax.axis_size(axis) for axis in SEQ)
    rise = [(i, (i + 1) % count) for i in range(count)]
    fall = [((i + 1) % count, i) for i in range(count)]
    swap = [(0, 1), (1, 0)]
    x_hi, core = lax.axis_index("x_hi"), lax.axis_index("core")
    place = jnp.stack([x_hi, core, lax.axis_index(SEQ), jnp.int32(count)]).astype(jnp.int32)
    zx = proj_zx.reshape(width, 2 * inner)

    pack, head, tail = call(
        pack_kernel,
        (
            struct((PACKED, inner), BF16),
            struct((HALO, width), BF16),
            struct((HALO, width), BF16),
        ),
        [SMEM, VMEM] + [HBM] * 7,
        (VMEM,) * 3,
        cost(1_000_000, 0, 1_000_000),
        scratch=[
            pltpu.VMEM((4, width), BF16),
            pltpu.VMEM((REACH + 1, inner), BF16),
            pltpu.VMEM((1, 4), F32),
            pltpu.VMEM((1, 4), jnp.int32),
            pltpu.VMEM((1, 4), F32),
            pltpu.VMEM((1, inner), F32),
            dma(8),
        ],
    )(
        place,
        zx[:, inner:],
        *lying(
            proj_dt.T,
            conv_x,
            dt_bias.reshape(1, 4),
            decay_exp.reshape(1, 4),
            skip_gain.reshape(1, 4),
            norm_gain.reshape(1, inner),
            hidden_in,
        ),
    )
    beside = (("seq_1", "x_hi"), [(0, 3), (3, 0), (1, 2), (2, 1)])
    other_pack = lax.ppermute(pack, *beside)
    prev = lax.ppermute(tail, SEQ, rise)
    following = lax.ppermute(head, SEQ, fall)

    own_z, own_out, pack = lax.optimization_barrier((zx[:, :inner], out_proj, pack))
    other_z = lax.ppermute(own_z, *beside)
    other_out = lax.ppermute(own_out, *beside)
    u, main, own_gate, own_w = call(
        early_kernel,
        (
            struct((rows, width), BF16),
            struct((rows, inner + LANES), BF16),
            struct((rows, inner), F32),
            struct((inner, 2 * inner), BF16),
        ),
        [SMEM] + [VMEM] * 4,
        (VMEM,) * 4,
        cost(2_000_000_000, 130_000, 4_000_000),
    )(place, hidden_in, zx, proj_bc, out_proj)
    y, c, cols, first, gains, send = call(
        front_kernel,
        (
            struct((2, rows, 2 * inner), F32),
            struct((2, rows, LANES), BF16),
            struct((rows, LANES), F32),
            struct((2, STATE, 2 * inner), F32),
            struct((8, 2 * inner), F32),
            struct((count, 16, LANES), BF16),
        ),
        [SMEM] + [VMEM] * 8,
        (VMEM,) * 6,
        cost(8_000_000_000, 3_000_000, 24_000_000),
        scratch=[
            pltpu.VMEM((2, rows, 2 * inner), BF16),
            pltpu.VMEM((2, rows, LANES), BF16),
            pltpu.VMEM((48, rows), F32),
            pltpu.VMEM((2 * inner // LANES + 1, rows + 2 * HALO, LANES), F32),
        ],
    )(place, u, main, prev, following, pack, other_pack, proj_bc, conv_bc)
    send, other_z, other_out = lax.optimization_barrier((send, other_z, other_out))
    got = lax.all_to_all(send, SEQ, 0, 0, tiled=True)
    scanned = call(
        scan_kernel,
        struct((count, 8, LANES), BF16),
        [SMEM, VMEM],
        VMEM,
        cost(1_000_000, 0, 400_000),
    )(place, got)
    came = lax.all_to_all(scanned, SEQ, 0, 0, tiled=True)

    keep, give = call(
        back_kernel,
        (struct((rows, inner), F32), struct((rows, inner), BF16)),
        [SMEM] + [VMEM] * 12,
        (VMEM, VMEM),
        cost(2_000_000_000, 600_000, 6_000_000),
        scratch=[
            pltpu.VMEM((2, STATE, 2 * inner), F32),
            pltpu.VMEM((2 * inner, 2 * inner), BF16),
        ],
    )(
        place, y, c, came, first, cols, gains, own_gate, own_w, u, other_z, other_out, hidden_in
    )
    taken = lax.ppermute(give, "core", swap)
    return (keep + taken.astype(F32)).astype(BF16)


def solution(mesh):
    torus = Mesh(mesh.devices.reshape(8, 2, 4, 2, 2), SEQ + CH)
    placed = (
        P(SEQ, None),
        P(None, None, CH),
        P(),
        P(None, CH),
        P(None, CH),
        P(),
        P(CH),
        P(CH),
        P(CH),
        P(CH),
        P(CH, None),
    )
    return jax.shard_map(
        shards, mesh=torus, in_specs=placed, out_specs=P(SEQ, CH), check_vma=False
    )
```

```python
import math

import jax
import jax.numpy as jnp
from jax import lax
from jax.experimental import pallas as pl
from jax.experimental.pallas import tpu as pltpu
from jax.sharding import Mesh
from jax.sharding import PartitionSpec as P

BLOCK = 256
STATE = 64
HEADP = 64
REACH = 3
HALO = 8
LANES = 128
SEQ = ("seq_0", "seq_1", "seq_2")
CH = ("x_hi", "core")
EPS = 1e-05
LOG2E = math.log2(math.e)
F32 = jnp.float32
BF16 = jnp.bfloat16

VMEM = pl.BlockSpec(memory_space=pltpu.VMEM)
HBM = pl.BlockSpec(memory_space=pltpu.HBM)
SMEM = pl.BlockSpec(memory_space=pltpu.SMEM)


def cost(flops, transcendentals, bytes_accessed):
    return pl.CostEstimate(
        flops=flops, transcendentals=transcendentals, bytes_accessed=bytes_accessed
    )


def struct(shape, dtype):
    return jax.ShapeDtypeStruct(shape, dtype)


def lying(*arrays):
    return [pltpu.with_memory_space_constraint(array, pltpu.HBM) for array in arrays]


def start_copies(pairs, sems):
    copies = [
        pltpu.make_async_copy(source, target, sems.at[i]) for i, (source, target) in enumerate(pairs)
    ]
    for copy in copies:
        copy.start()
    return copies


def dma(n):
    return pltpu.SemaphoreType.DMA((n,))


def call(kernel, out_shape, specs, out_specs, estimate, mib=16, scratch=()):
    return pl.pallas_call(
        kernel,
        out_shape=out_shape,
        in_specs=specs,
        out_specs=out_specs,
        scratch_shapes=scratch,
        compiler_params=pltpu.CompilerParams(vmem_limit_bytes=mib * 1024 * 1024),
        cost_estimate=estimate,
    )


def iota(shape, dim):
    return lax.broadcasted_iota(jnp.int32, shape, dim)


def dot(a, b):
    return jnp.dot(a, b, preferred_element_type=F32)


def dot_nt(a, b):
    return lax.dot_general(a, b, (((1,), (1,)), ((), ())), preferred_element_type=F32)


def sigmoid(v):
    return 0.5 * jnp.tanh(0.5 * v) + 0.5


def parts_of(value):
    hi = value.astype(BF16).astype(F32)
    rest = value - hi
    mid = rest.astype(BF16).astype(F32)
    return hi, mid, rest - mid


def orient(n, strand):
    source, target = iota((n, n), 0), iota((n, n), 1)
    return (source == jnp.where(strand == 0, target, n - 1 - target)).astype(BF16)


DT_AT, TAP_AT, SMALL_AT, PACKED = 512, 520, 528, 544


def pack_kernel(
    place_ref, x_ref, dt_hbm, taps_hbm, bias_hbm, exp_hbm, skip_hbm, gain_hbm, hidden_hbm,
    pack_ref, head_ref, tail_ref,
    dt_ref, taps_ref, bias_ref, exp_ref, skip_ref, gain_ref, sems,
):
    inner, heads = pack_ref.shape[1], dt_ref.shape[0]
    rows, width = hidden_hbm.shape[0], hidden_hbm.shape[1] // 2
    columns = pl.ds(pl.multiple_of(place_ref[0] * width, width), width)
    copies = start_copies(
        (
            (dt_hbm, dt_ref),
            (taps_hbm, taps_ref),
            (bias_hbm, bias_ref),
            (exp_hbm, exp_ref),
            (skip_hbm, skip_ref),
            (gain_hbm, gain_ref),
            (hidden_hbm.at[pl.ds(0, HALO), columns], head_ref),
            (hidden_hbm.at[pl.ds(rows - HALO, HALO), columns], tail_ref),
        ),
        sems,
    )
    pack_ref[:DT_AT] = x_ref[...]
    for copy in copies:
        copy.wait()
    lane = iota((1, inner), 1)
    small = jnp.zeros((1, inner), F32)
    for h in range(heads):
        for k, ref in enumerate((bias_ref, exp_ref, skip_ref)):
            value = ref[:, h : h + 1].astype(F32)
            small = jnp.where(lane == k * heads + h, jnp.broadcast_to(value, (1, inner)), small)
    packed = [dt_ref[:, :inner].astype(F32), dt_ref[:, inner:].astype(F32), taps_ref[...].astype(F32)]
    packed.append(jnp.zeros((SMALL_AT - TAP_AT - taps_ref.shape[0], inner), F32))
    packed += parts_of(small) + parts_of(gain_ref[...])
    packed.append(jnp.zeros((PACKED - SMALL_AT - 6, inner), F32))
    pack_ref[DT_AT:] = jnp.concatenate(packed, axis=0).astype(BF16)


def unpack(ref):
    tail = ref[SMALL_AT:].astype(F32)
    return tail[0:1] + tail[1:2] + tail[2:3], tail[3:4] + tail[4:5] + tail[5:6]


def column_of(smalls, at):
    row = iota((8, 1), 0)
    out = jnp.zeros((8, 1), F32)
    for g in range(2):
        for h in range(4):
            out = jnp.where(row == g * 4 + h, smalls[g][:, at + h : at + h + 1], out)
    return out


def spread(pieces, rows):
    half = iota((rows, LANES), 1) < HEADP
    wide = [jnp.broadcast_to(piece, (rows, LANES)) for piece in pieces]
    return jnp.concatenate(
        [jnp.where(half, wide[2 * q], wide[2 * q + 1]) for q in range(4)], axis=1
    )


def turned_out(place_ref, out_ref):
    columns = out_ref.shape[1]
    part = columns // 2
    source, target = iota((columns, columns), 0), iota((columns, columns), 1)
    column = jnp.where(target < part, target + place_ref[1] * part, target - place_ref[1] * part)
    wanted = jnp.where(place_ref[0] == 0, column, columns - 1 - column)
    return dot(out_ref[...], (source == wanted).astype(BF16)).astype(BF16)


def gated_by(u, w):
    z = dot(u, w).astype(BF16).astype(F32)
    return z * sigmoid(z)


def early_kernel(
    place_ref, hidden_ref, zx_ref, bc_ref, out_ref, u_ref, main_ref, gate_ref, w_ref
):
    width, inner = zx_ref.shape[0], zx_ref.shape[1] // 2
    strand = place_ref[0]
    u = hidden_ref[:, pl.ds(pl.multiple_of(strand * width, width), width)]
    u = dot(u, orient(width, strand)).astype(BF16)
    u_ref[...] = u
    main_ref[:, :inner] = dot(u, zx_ref[:, inner:]).astype(BF16)
    main_ref[:, inner:] = dot(u, bc_ref[...]).astype(BF16)
    gate_ref[...] = gated_by(u, zx_ref[:, :inner])
    w_ref[...] = turned_out(place_ref, out_ref)


def front_kernel(
    place_ref, u_ref, main_ref, prev_ref, next_ref, own_ref, other_ref, bc_ref, tapbc_ref,
    y_ref, c_ref, cols_ref, first_ref, gains_ref, send_ref,
    x_ref, b_ref, rows_ref, pad_ref,
):
    row_count, width = u_ref.shape
    inner = own_ref.shape[1]
    strand, position, count = place_ref[0], place_ref[2], place_ref[3]
    packs = (own_ref, other_ref)
    u = u_ref[...]
    before = jnp.where(position > 0, prev_ref[...].astype(F32), 0.0)
    after = jnp.where(position < count - 1, next_ref[...].astype(F32), 0.0)
    edge = dot(jnp.concatenate([before, after], axis=0).astype(BF16), orient(width, strand))
    edge = edge.astype(BF16)

    raw = jnp.concatenate(
        [
            dot_nt(
                jnp.concatenate(
                    [ref[DT_AT : DT_AT + 4].astype(F32), ref[DT_AT + 4 : DT_AT + 8].astype(F32)],
                    axis=1,
                ).astype(BF16),
                u,
            )
            for ref in packs
        ],
        axis=0,
    )
    smalls, gains = zip(*[unpack(ref) for ref in packs])
    gains_ref[...] = jnp.concatenate(
        [
            jnp.concatenate(gains, axis=1),
            spread([smalls[g][:, 8 + h : 9 + h] for g in range(2) for h in range(4)], 1),
            jnp.zeros((6, 2 * inner), F32),
        ],
        axis=0,
    )
    v = raw + column_of(smalls, 0)
    rate = jnp.exp2(-column_of(smalls, 4)) * LOG2E
    step = jnp.maximum(v, 0.0) + jnp.log1p(jnp.exp(-jnp.abs(v)))
    parts = jnp.concatenate(parts_of(-step * rate), axis=0).astype(BF16)
    ahead = (iota((BLOCK, BLOCK), 0) <= iota((BLOCK, BLOCK), 1)).astype(BF16)
    behind = (iota((BLOCK, BLOCK), 0) >= iota((BLOCK, BLOCK), 1)).astype(BF16)
    cums, ends = [], []
    for b in range(2):
        piece = parts[:, b * BLOCK : (b + 1) * BLOCK]
        both = []
        for mask in (ahead, behind):
            full = dot(piece, mask)
            both.append(full[:8] + full[8:16] + full[16:])
        cums.append(jnp.concatenate(both, axis=0))
        last = jnp.concatenate([both[0][:, BLOCK - 1 :], both[1][:, :1]], axis=0)
        ends.append(jnp.broadcast_to(last, (16, BLOCK)))
    cum = jnp.concatenate(cums, axis=1)
    end = jnp.concatenate(ends, axis=1)
    step = jnp.concatenate([step, step], axis=0)
    rows_ref[:16] = cum
    rows_ref[16:32] = cum - jnp.log2(step)
    rows_ref[32:] = jnp.exp2(jnp.minimum(end - cum, 0.0)) * step
    cols_ref[...] = jnp.concatenate([cum, jnp.zeros((LANES - 16, row_count), F32)], axis=0).T
    totals = [ends[b][:, :1] for b in range(2)]

    chunk = 32
    tiles = inner // LANES
    for g in range(3):
        w = packs[g][:DT_AT] if g < 2 else bc_ref[...]
        if g == 1:
            middle = dot(u, w).astype(BF16)
        else:
            middle = main_ref[:, :inner] if g == 0 else main_ref[:, inner:]
        middle = middle.astype(F32)
        outer = dot(edge, w).astype(BF16).astype(F32)
        for k in range(w.shape[1] // LANES):
            at, lanes = g * tiles + k, slice(k * LANES, (k + 1) * LANES)
            pad_ref[at, :HALO] = outer[:HALO, lanes]
            pad_ref[at, HALO : HALO + row_count] = middle[:, lanes]
            pad_ref[at, HALO + row_count :] = outer[HALO:, lanes]
    taps = jnp.concatenate(
        [ref[TAP_AT : TAP_AT + REACH + 1].astype(F32) for ref in packs]
        + [tapbc_ref[...].astype(F32)],
        axis=1,
    )
    groups = taps.shape[1] // LANES
    low_lane = iota((chunk, LANES), 1) < STATE
    for group in range(groups):
        at = slice(group * LANES, (group + 1) * LANES)
        tap = [taps[j : j + 1, at] for j in range(REACH + 1)]
        for r in range(0, row_count, chunk):
            start = r + HALO - REACH
            window = [
                pad_ref[group, start + k : start + k + chunk] for k in range(2 * REACH + 1)
            ]
            for way in range(2):
                acc = tap[0] * window[0 if way == 0 else 2 * REACH]
                for j in range(1, REACH + 1):
                    acc = acc + tap[j] * window[j if way == 0 else 2 * REACH - j]
                value = (acc * sigmoid(acc)).astype(BF16)
                if group < groups - 1:
                    x_ref[way, r : r + chunk, at] = value
                else:
                    b_ref[way, r : r + chunk, :] = value
                    swapped = pltpu.roll(value.astype(F32), LANES - STATE, 1)
                    c_ref[way, r : r + chunk, :] = jnp.where(low_lane, swapped, 0.0).astype(BF16)


    half = iota((STATE, LANES), 1) < HEADP
    row8 = iota((8, LANES), 0)
    for way in range(2):
        states = []
        for b in range(2):
            block = slice(b * BLOCK, (b + 1) * BLOCK)
            bt = b_ref[way, block, :].astype(F32).T[:STATE]
            tiles = []
            for g in range(2):
                at = 32 + way * 8 + g * 4
                scaled = jnp.concatenate(
                    [
                        (bt * rows_ref[at + h : at + h + 1, block]).astype(BF16)
                        for h in range(4)
                    ],
                    axis=0,
                )
                full = dot(scaled, x_ref[way, block, g * inner : (g + 1) * inner])
                tiles.append(jnp.where(half, full[:64, :128], full[64:128, :128]))
                tiles.append(jnp.where(half, full[128:192, 128:], full[192:, 128:]))
            states.append(tiles)
        first, last = (0, 1) if way == 0 else (1, 0)
        at = slice(way * 8, way * 8 + 8)
        last_total = jnp.exp2(totals[last][at])
        both_total = jnp.exp2(totals[0][at] + totals[1][at])
        factor = spread([last_total[i : i + 1] for i in range(8)], 1)
        whole = spread([both_total[i : i + 1] for i in range(8)], 8)
        for q in range(4):
            lanes = slice(q * LANES, (q + 1) * LANES)
            state = factor[:, lanes] * states[first][q] + states[last][q]
            first_ref[way, :, lanes] = states[first][q]
            hi, mid, low = parts_of(whole[:, lanes])
            decay = jnp.where(
                row8 == 0, hi, jnp.where(row8 == 1, mid, jnp.where(row8 == 2, low, 0.0))
            )
            for n in range(8):
                send_ref[way * 32 + n * 4 + q] = jnp.concatenate(
                    [state[n * 8 : n * 8 + 8], decay], axis=0
                ).astype(BF16)
    inside(x_ref, b_ref, c_ref, rows_ref, cols_ref, gains_ref, y_ref)


def scan_kernel(place_ref, got_ref, out_ref):
    count = got_ref.shape[0]
    backward = place_ref[2] >= count // 2
    state = jnp.zeros((8, LANES), F32)
    for i in range(count):
        k = jnp.where(backward, count - 1 - i, i)
        piece = got_ref[k].astype(F32)
        out_ref[k] = state.astype(BF16)
        decay = jnp.sum(piece[8:], axis=0, keepdims=True)
        state = decay * state + piece[:8]


def inside(x_ref, b_ref, c_ref, rows_ref, cols_ref, gains_ref, y_ref):
    size = 128
    low = iota((size, size), 0) >= iota((size, size), 1)
    high = iota((size, size), 0) <= iota((size, size), 1)
    half = iota((size, LANES), 1) < HEADP
    skip = gains_ref[1:2]
    for way in range(2):
        for b in range(2):
            block = slice(b * BLOCK, (b + 1) * BLOCK)
            scores = dot_nt(c_ref[way, block, :], b_ref[way, block, :])
            for pair in range(4):
                at = slice(pair * LANES, (pair + 1) * LANES)
                for t in range(2):
                    here = slice(b * BLOCK + t * size, b * BLOCK + (t + 1) * size)
                    seen = [s for s in range(2) if (s <= t if way == 0 else s >= t)]
                    lo = b * BLOCK + seen[0] * size
                    hi = b * BLOCK + (seen[-1] + 1) * size
                    outs = []
                    for h in (2 * pair, 2 * pair + 1):
                        i = way * 8 + h
                        gone = jnp.broadcast_to(cols_ref[here, i : i + 1], (size, size))
                        tiles = []
                        for s in seen:
                            there = slice(b * BLOCK + s * size, b * BLOCK + (s + 1) * size)
                            gap = gone - rows_ref[16 + i : 17 + i, there]
                            if s == t:
                                gap = jnp.where(low if way == 0 else high, gap, -jnp.inf)
                            part = scores[t * size : (t + 1) * size, s * size : (s + 1) * size]
                            tiles.append((part * jnp.exp2(gap)).astype(BF16))
                        weights = tiles[0] if len(tiles) == 1 else jnp.concatenate(tiles, axis=1)
                        outs.append(dot(weights, x_ref[way, lo:hi, at]))
                    y_ref[way, here, at] = (
                        jnp.where(half, outs[0], outs[1])
                        + skip[:, at] * x_ref[way, here, at].astype(F32)
                    )


def back_kernel(
    place_ref, y_ref, c_ref, came_ref, first_ref, cols_ref, gains_ref, own_gate_ref, own_w_ref,
    u_ref, other_z_ref, other_out_ref, hidden_ref, keep_ref, give_ref, state_ref, w_ref,
):
    part = own_w_ref.shape[1] // 2
    inner = y_ref.shape[2] // 2
    ours = pl.multiple_of((2 * place_ref[0] + place_ref[1]) * part, part)
    blocks = [slice(b * BLOCK, (b + 1) * BLOCK) for b in range(2)]
    w_ref[:inner] = own_w_ref[...]
    w_ref[inner:] = turned_out(place_ref, other_out_ref)
    same = (iota((inner, inner), 0) // HEADP == iota((inner, inner), 1) // HEADP).astype(BF16)
    for way in range(2):
        for n in range(8):
            for q in range(4):
                state_ref[way, n * 8 : n * 8 + 8, q * LANES : (q + 1) * LANES] = came_ref[
                    way * 32 + n * 4 + q
                ].astype(F32)
    for b, block in enumerate(blocks):
        decays = jnp.exp2(cols_ref[block])
        gate = jnp.concatenate(
            [own_gate_ref[block, :], gated_by(u_ref[block, :], other_z_ref[...])], axis=1
        )
        total = None
        for way in range(2):
            state = state_ref[way]
            if b != way:
                edge = BLOCK - 1 if way == 0 else BLOCK
                passed = jnp.exp2(cols_ref[edge : edge + 1])
                factor = spread(
                    [passed[:, way * 8 + i : way * 8 + i + 1] for i in range(8)], 1
                )
                state = factor * state + first_ref[way]
            state = jnp.concatenate([state, jnp.zeros_like(state)], axis=0).astype(BF16)
            decay = spread([decays[:, way * 8 + i : way * 8 + i + 1] for i in range(8)], BLOCK)
            mixer = y_ref[way, block, :] + decay * dot(c_ref[way, block, :], state)
            gated = mixer * gate
            square = (gated * gated).astype(BF16)
            mean = jnp.concatenate(
                [dot(square[:, g * inner : (g + 1) * inner], same) for g in range(2)], axis=1
            ) * (1.0 / HEADP)
            normed = gated * lax.rsqrt(mean + EPS)
            total = normed if total is None else total + normed
        mixed = (total * gains_ref[0:1]).astype(BF16)
        give_ref[block, :] = dot(mixed, w_ref[:, part:]).astype(BF16)
        keep_ref[block, :] = dot(mixed, w_ref[:, :part]) + hidden_ref[
            block, pl.ds(ours, part)
        ].astype(F32)


def shards(
    hidden_in,
    proj_zx,
    proj_bc,
    proj_dt,
    conv_x,
    conv_bc,
    dt_bias,
    decay_exp,
    skip_gain,
    norm_gain,
    out_proj,
):
    rows, width = hidden_in.shape[0], hidden_in.shape[1] // 2
    inner = proj_zx.shape[2]
    count = math.prod(lax.axis_size(axis) for axis in SEQ)
    rise = [(i, (i + 1) % count) for i in range(count)]
    fall = [((i + 1) % count, i) for i in range(count)]
    swap = [(0, 1), (1, 0)]
    x_hi, core = lax.axis_index("x_hi"), lax.axis_index("core")
    place = jnp.stack([x_hi, core, lax.axis_index(SEQ), jnp.int32(count)]).astype(jnp.int32)
    zx = proj_zx.reshape(width, 2 * inner)

    pack, head, tail = call(
        pack_kernel,
        (
            struct((PACKED, inner), BF16),
            struct((HALO, width), BF16),
            struct((HALO, width), BF16),
        ),
        [SMEM, VMEM] + [HBM] * 7,
        (VMEM,) * 3,
        cost(1_000_000, 0, 1_000_000),
        scratch=[
            pltpu.VMEM((4, width), BF16),
            pltpu.VMEM((REACH + 1, inner), BF16),
            pltpu.VMEM((1, 4), F32),
            pltpu.VMEM((1, 4), jnp.int32),
            pltpu.VMEM((1, 4), F32),
            pltpu.VMEM((1, inner), F32),
            dma(8),
        ],
    )(
        place,
        zx[:, inner:],
        *lying(
            proj_dt.T,
            conv_x,
            dt_bias.reshape(1, 4),
            decay_exp.reshape(1, 4),
            skip_gain.reshape(1, 4),
            norm_gain.reshape(1, inner),
            hidden_in,
        ),
    )
    beside = (("seq_1", "x_hi"), [(0, 3), (3, 0), (1, 2), (2, 1)])
    other_pack = lax.ppermute(pack, *beside)
    prev = lax.ppermute(tail, SEQ, rise)
    following = lax.ppermute(head, SEQ, fall)

    own_z, own_out, pack = lax.optimization_barrier((zx[:, :inner], out_proj, pack))
    other_z = lax.ppermute(own_z, *beside)
    other_out = lax.ppermute(own_out, *beside)
    u, main, own_gate, own_w = call(
        early_kernel,
        (
            struct((rows, width), BF16),
            struct((rows, inner + LANES), BF16),
            struct((rows, inner), F32),
            struct((inner, 2 * inner), BF16),
        ),
        [SMEM] + [VMEM] * 4,
        (VMEM,) * 4,
        cost(2_000_000_000, 130_000, 4_000_000),
    )(place, hidden_in, zx, proj_bc, out_proj)
    y, c, cols, first, gains, send = call(
        front_kernel,
        (
            struct((2, rows, 2 * inner), F32),
            struct((2, rows, LANES), BF16),
            struct((rows, LANES), F32),
            struct((2, STATE, 2 * inner), F32),
            struct((8, 2 * inner), F32),
            struct((count, 16, LANES), BF16),
        ),
        [SMEM] + [VMEM] * 8,
        (VMEM,) * 6,
        cost(8_000_000_000, 3_000_000, 24_000_000),
        scratch=[
            pltpu.VMEM((2, rows, 2 * inner), BF16),
            pltpu.VMEM((2, rows, LANES), BF16),
            pltpu.VMEM((48, rows), F32),
            pltpu.VMEM((2 * inner // LANES + 1, rows + 2 * HALO, LANES), F32),
        ],
    )(place, u, main, prev, following, pack, other_pack, proj_bc, conv_bc)
    def passed_on(place, send, *others):
        got = lax.all_to_all(send, SEQ, 0, 0, tiled=True)
        scanned = call(
            scan_kernel,
            struct((count, 8, LANES), BF16),
            [SMEM, VMEM],
            VMEM,
            cost(1_000_000, 0, 400_000),
        )(place, got)
        return lax.all_to_all(scanned, SEQ, 0, 0, tiled=True), *others

    came, y, c, cols, first, gains, own_gate, own_w, u = lax.cond(
        core < 2,
        passed_on,
        lambda place, send, *others: (send[:, :8], *[-other for other in others]),
        place, send, y, c, cols, first, gains, own_gate, own_w, u,
    )

    keep, give = call(
        back_kernel,
        (struct((rows, inner), F32), struct((rows, inner), BF16)),
        [SMEM] + [VMEM] * 12,
        (VMEM, VMEM),
        cost(2_000_000_000, 600_000, 6_000_000),
        scratch=[
            pltpu.VMEM((2, STATE, 2 * inner), F32),
            pltpu.VMEM((2 * inner, 2 * inner), BF16),
        ],
    )(
        place, y, c, came, first, cols, gains, own_gate, own_w, u, other_z, other_out, hidden_in
    )
    taken = lax.ppermute(give, "core", swap)
    return (keep + taken.astype(F32)).astype(BF16)


def solution(mesh):
    torus = Mesh(mesh.devices.reshape(8, 2, 4, 2, 2), SEQ + CH)
    placed = (
        P(SEQ, None),
        P(None, None, CH),
        P(),
        P(None, CH),
        P(None, CH),
        P(),
        P(CH),
        P(CH),
        P(CH),
        P(CH),
        P(CH, None),
    )
    return jax.shard_map(
        shards, mesh=torus, in_specs=placed, out_specs=P(SEQ, CH), check_vma=False
    )
```

```python
import math

import jax
import jax.numpy as jnp
from jax import lax
from jax.experimental import pallas as pl
from jax.experimental.pallas import tpu as pltpu
from jax.sharding import Mesh
from jax.sharding import PartitionSpec as P

BLOCK = 256
STATE = 64
HEADP = 64
REACH = 3
HALO = 8
LANES = 128
SEQ = ("seq_0", "seq_1", "seq_2")
CH = ("x_hi", "core")
EPS = 1e-05
LOG2E = math.log2(math.e)
F32 = jnp.float32
BF16 = jnp.bfloat16

VMEM = pl.BlockSpec(memory_space=pltpu.VMEM)
HBM = pl.BlockSpec(memory_space=pltpu.HBM)
SMEM = pl.BlockSpec(memory_space=pltpu.SMEM)


def cost(flops, transcendentals, bytes_accessed):
    return pl.CostEstimate(
        flops=flops, transcendentals=transcendentals, bytes_accessed=bytes_accessed
    )


def struct(shape, dtype):
    return jax.ShapeDtypeStruct(shape, dtype)


def lying(*arrays):
    return [pltpu.with_memory_space_constraint(array, pltpu.HBM) for array in arrays]


def start_copies(pairs, sems):
    copies = [
        pltpu.make_async_copy(source, target, sems.at[i]) for i, (source, target) in enumerate(pairs)
    ]
    for copy in copies:
        copy.start()
    return copies


def dma(n):
    return pltpu.SemaphoreType.DMA((n,))


def call(kernel, out_shape, specs, out_specs, estimate, mib=16, scratch=()):
    return pl.pallas_call(
        kernel,
        out_shape=out_shape,
        in_specs=specs,
        out_specs=out_specs,
        scratch_shapes=scratch,
        compiler_params=pltpu.CompilerParams(vmem_limit_bytes=mib * 1024 * 1024),
        cost_estimate=estimate,
    )


def iota(shape, dim):
    return lax.broadcasted_iota(jnp.int32, shape, dim)


def dot(a, b):
    return jnp.dot(a, b, preferred_element_type=F32)


def dot_nt(a, b):
    return lax.dot_general(a, b, (((1,), (1,)), ((), ())), preferred_element_type=F32)


def sigmoid(v):
    return 0.5 * jnp.tanh(0.5 * v) + 0.5


def parts_of(value):
    hi = value.astype(BF16).astype(F32)
    rest = value - hi
    mid = rest.astype(BF16).astype(F32)
    return hi, mid, rest - mid


def orient(n, strand):
    source, target = iota((n, n), 0), iota((n, n), 1)
    return (source == jnp.where(strand == 0, target, n - 1 - target)).astype(BF16)


DT_AT, TAP_AT, SMALL_AT, PACKED = 512, 520, 528, 544


def pack_kernel(
    place_ref, zx_ref, dt_hbm, taps_hbm, bias_hbm, exp_hbm, skip_hbm, gain_hbm, hidden_hbm, out_hbm,
    pack_ref, late_ref, head_ref, tail_ref,
    dt_ref, taps_ref, bias_ref, exp_ref, skip_ref, gain_ref, sems,
):
    inner, heads = pack_ref.shape[1], dt_ref.shape[0]
    rows, width = hidden_hbm.shape[0], hidden_hbm.shape[1] // 2
    columns = pl.ds(pl.multiple_of(place_ref[0] * width, width), width)
    copies = start_copies(
        (
            (dt_hbm, dt_ref),
            (taps_hbm, taps_ref),
            (bias_hbm, bias_ref),
            (exp_hbm, exp_ref),
            (skip_hbm, skip_ref),
            (gain_hbm, gain_ref),
            (hidden_hbm.at[pl.ds(0, HALO), columns], head_ref),
            (hidden_hbm.at[pl.ds(rows - HALO, HALO), columns], tail_ref),
            (out_hbm.at[:, :inner], late_ref.at[:inner, inner:]),
            (out_hbm.at[:, inner:], late_ref.at[inner:, inner:]),
        ),
        sems,
    )
    pack_ref[:DT_AT] = zx_ref[:, inner:]
    late_ref[:, :inner] = zx_ref[:, :inner]
    for copy in copies:
        copy.wait()
    lane = iota((1, inner), 1)
    small = jnp.zeros((1, inner), F32)
    for h in range(heads):
        for k, ref in enumerate((bias_ref, exp_ref, skip_ref)):
            value = ref[:, h : h + 1].astype(F32)
            small = jnp.where(lane == k * heads + h, jnp.broadcast_to(value, (1, inner)), small)
    packed = [dt_ref[:, :inner].astype(F32), dt_ref[:, inner:].astype(F32), taps_ref[...].astype(F32)]
    packed.append(jnp.zeros((SMALL_AT - TAP_AT - taps_ref.shape[0], inner), F32))
    packed += parts_of(small) + parts_of(gain_ref[...])
    packed.append(jnp.zeros((PACKED - SMALL_AT - 6, inner), F32))
    pack_ref[DT_AT:] = jnp.concatenate(packed, axis=0).astype(BF16)


def unpack(ref):
    tail = ref[SMALL_AT:].astype(F32)
    return tail[0:1] + tail[1:2] + tail[2:3], tail[3:4] + tail[4:5] + tail[5:6]


def column_of(smalls, at):
    row = iota((8, 1), 0)
    out = jnp.zeros((8, 1), F32)
    for g in range(2):
        for h in range(4):
            out = jnp.where(row == g * 4 + h, smalls[g][:, at + h : at + h + 1], out)
    return out


def spread(pieces, rows):
    half = iota((rows, LANES), 1) < HEADP
    wide = [jnp.broadcast_to(piece, (rows, LANES)) for piece in pieces]
    return jnp.concatenate(
        [jnp.where(half, wide[2 * q], wide[2 * q + 1]) for q in range(4)], axis=1
    )


def turned_out(place_ref, out):
    columns = out.shape[1]
    part = columns // 2
    source, target = iota((columns, columns), 0), iota((columns, columns), 1)
    column = jnp.where(target < part, target + place_ref[1] * part, target - place_ref[1] * part)
    wanted = jnp.where(place_ref[0] == 0, column, columns - 1 - column)
    return dot(out, (source == wanted).astype(BF16)).astype(BF16)


def gated_by(u, w):
    z = dot(u, w).astype(BF16).astype(F32)
    return z * sigmoid(z)


def front_kernel(
    place_ref, hidden_ref, zx_ref, prev_ref, next_ref, own_ref, other_ref, bc_ref, tapbc_ref,
    u_ref, gate_ref, y_ref, c_ref, cols_ref, first_ref, gains_ref, send_ref,
    x_ref, b_ref, rows_ref, pad_ref,
):
    row_count, width = hidden_ref.shape[0], hidden_ref.shape[1] // 2
    inner = own_ref.shape[1]
    strand, position, count = place_ref[0], place_ref[2], place_ref[3]
    packs = (own_ref, other_ref)
    turn = orient(width, strand)
    u = hidden_ref[:, pl.ds(pl.multiple_of(strand * width, width), width)]
    u = dot(u, turn).astype(BF16)
    u_ref[...] = u
    gate_ref[...] = gated_by(u, zx_ref[:, :inner])
    before = jnp.where(position > 0, prev_ref[...].astype(F32), 0.0)
    after = jnp.where(position < count - 1, next_ref[...].astype(F32), 0.0)
    edge = dot(jnp.concatenate([before, after], axis=0).astype(BF16), turn)
    edge = edge.astype(BF16)

    raw = jnp.concatenate(
        [
            dot_nt(
                jnp.concatenate(
                    [ref[DT_AT : DT_AT + 4].astype(F32), ref[DT_AT + 4 : DT_AT + 8].astype(F32)],
                    axis=1,
                ).astype(BF16),
                u,
            )
            for ref in packs
        ],
        axis=0,
    )
    smalls, gains = zip(*[unpack(ref) for ref in packs])
    gains_ref[...] = jnp.concatenate(
        [
            jnp.concatenate(gains, axis=1),
            spread([smalls[g][:, 8 + h : 9 + h] for g in range(2) for h in range(4)], 1),
            jnp.zeros((6, 2 * inner), F32),
        ],
        axis=0,
    )
    v = raw + column_of(smalls, 0)
    rate = jnp.exp2(-column_of(smalls, 4)) * LOG2E
    step = jnp.maximum(v, 0.0) + jnp.log1p(jnp.exp(-jnp.abs(v)))
    parts = jnp.concatenate(parts_of(-step * rate), axis=0).astype(BF16)
    ahead = (iota((BLOCK, BLOCK), 0) <= iota((BLOCK, BLOCK), 1)).astype(BF16)
    behind = (iota((BLOCK, BLOCK), 0) >= iota((BLOCK, BLOCK), 1)).astype(BF16)
    cums, ends = [], []
    for b in range(2):
        piece = parts[:, b * BLOCK : (b + 1) * BLOCK]
        both = []
        for mask in (ahead, behind):
            full = dot(piece, mask)
            both.append(full[:8] + full[8:16] + full[16:])
        cums.append(jnp.concatenate(both, axis=0))
        last = jnp.concatenate([both[0][:, BLOCK - 1 :], both[1][:, :1]], axis=0)
        ends.append(jnp.broadcast_to(last, (16, BLOCK)))
    cum = jnp.concatenate(cums, axis=1)
    end = jnp.concatenate(ends, axis=1)
    step = jnp.concatenate([step, step], axis=0)
    rows_ref[:16] = cum
    rows_ref[16:32] = cum - jnp.log2(step)
    rows_ref[32:] = jnp.exp2(jnp.minimum(end - cum, 0.0)) * step
    cols_ref[...] = jnp.concatenate([cum, jnp.zeros((LANES - 16, row_count), F32)], axis=0).T
    totals = [ends[b][:, :1] for b in range(2)]

    chunk = 32
    tiles = inner // LANES
    for g in range(3):
        w = packs[g][:DT_AT] if g < 2 else bc_ref[...]
        middle = dot(u, w).astype(BF16).astype(F32)
        outer = dot(edge, w).astype(BF16).astype(F32)
        for k in range(w.shape[1] // LANES):
            at, lanes = g * tiles + k, slice(k * LANES, (k + 1) * LANES)
            pad_ref[at, :HALO] = outer[:HALO, lanes]
            pad_ref[at, HALO : HALO + row_count] = middle[:, lanes]
            pad_ref[at, HALO + row_count :] = outer[HALO:, lanes]
    taps = jnp.concatenate(
        [ref[TAP_AT : TAP_AT + REACH + 1].astype(F32) for ref in packs]
        + [tapbc_ref[...].astype(F32)],
        axis=1,
    )
    groups = taps.shape[1] // LANES
    low_lane = iota((chunk, LANES), 1) < STATE
    for group in range(groups):
        at = slice(group * LANES, (group + 1) * LANES)
        tap = [taps[j : j + 1, at] for j in range(REACH + 1)]
        for r in range(0, row_count, chunk):
            start = r + HALO - REACH
            window = [
                pad_ref[group, start + k : start + k + chunk] for k in range(2 * REACH + 1)
            ]
            for way in range(2):
                acc = tap[0] * window[0 if way == 0 else 2 * REACH]
                for j in range(1, REACH + 1):
                    acc = acc + tap[j] * window[j if way == 0 else 2 * REACH - j]
                value = (acc * sigmoid(acc)).astype(BF16)
                if group < groups - 1:
                    x_ref[way, r : r + chunk, at] = value
                else:
                    b_ref[way, r : r + chunk, :] = value
                    swapped = pltpu.roll(value.astype(F32), LANES - STATE, 1)
                    c_ref[way, r : r + chunk, :] = jnp.where(low_lane, swapped, 0.0).astype(BF16)


    half = iota((STATE, LANES), 1) < HEADP
    row8 = iota((8, LANES), 0)
    for way in range(2):
        states = []
        for b in range(2):
            block = slice(b * BLOCK, (b + 1) * BLOCK)
            bt = b_ref[way, block, :].astype(F32).T[:STATE]
            tiles = []
            for g in range(2):
                at = 32 + way * 8 + g * 4
                scaled = jnp.concatenate(
                    [
                        (bt * rows_ref[at + h : at + h + 1, block]).astype(BF16)
                        for h in range(4)
                    ],
                    axis=0,
                )
                full = dot(scaled, x_ref[way, block, g * inner : (g + 1) * inner])
                tiles.append(jnp.where(half, full[:64, :128], full[64:128, :128]))
                tiles.append(jnp.where(half, full[128:192, 128:], full[192:, 128:]))
            states.append(tiles)
        first, last = (0, 1) if way == 0 else (1, 0)
        at = slice(way * 8, way * 8 + 8)
        last_total = jnp.exp2(totals[last][at])
        both_total = jnp.exp2(totals[0][at] + totals[1][at])
        factor = spread([last_total[i : i + 1] for i in range(8)], 1)
        whole = spread([both_total[i : i + 1] for i in range(8)], 8)
        for q in range(4):
            lanes = slice(q * LANES, (q + 1) * LANES)
            state = factor[:, lanes] * states[first][q] + states[last][q]
            first_ref[way, :, lanes] = states[first][q]
            hi, mid, low = parts_of(whole[:, lanes])
            decay = jnp.where(
                row8 == 0, hi, jnp.where(row8 == 1, mid, jnp.where(row8 == 2, low, 0.0))
            )
            for n in range(8):
                send_ref[way * 32 + n * 4 + q] = jnp.concatenate(
                    [state[n * 8 : n * 8 + 8], decay], axis=0
                ).astype(BF16)
    inside(x_ref, b_ref, c_ref, rows_ref, cols_ref, gains_ref, y_ref)


def scan_kernel(place_ref, got_ref, out_ref):
    count = got_ref.shape[0]
    backward = place_ref[2] >= count // 2
    state = jnp.zeros((8, LANES), F32)
    for i in range(count):
        k = jnp.where(backward, count - 1 - i, i)
        piece = got_ref[k].astype(F32)
        out_ref[k] = state.astype(BF16)
        decay = jnp.sum(piece[8:], axis=0, keepdims=True)
        state = decay * state + piece[:8]


def inside(x_ref, b_ref, c_ref, rows_ref, cols_ref, gains_ref, y_ref):
    size = 128
    low = iota((size, size), 0) >= iota((size, size), 1)
    high = iota((size, size), 0) <= iota((size, size), 1)
    half = iota((size, LANES), 1) < HEADP
    skip = gains_ref[1:2]
    for way in range(2):
        for b in range(2):
            block = slice(b * BLOCK, (b + 1) * BLOCK)
            scores = dot_nt(c_ref[way, block, :], b_ref[way, block, :])
            for pair in range(4):
                at = slice(pair * LANES, (pair + 1) * LANES)
                for t in range(2):
                    here = slice(b * BLOCK + t * size, b * BLOCK + (t + 1) * size)
                    seen = [s for s in range(2) if (s <= t if way == 0 else s >= t)]
                    lo = b * BLOCK + seen[0] * size
                    hi = b * BLOCK + (seen[-1] + 1) * size
                    outs = []
                    for h in (2 * pair, 2 * pair + 1):
                        i = way * 8 + h
                        gone = jnp.broadcast_to(cols_ref[here, i : i + 1], (size, size))
                        tiles = []
                        for s in seen:
                            there = slice(b * BLOCK + s * size, b * BLOCK + (s + 1) * size)
                            gap = gone - rows_ref[16 + i : 17 + i, there]
                            if s == t:
                                gap = jnp.where(low if way == 0 else high, gap, -jnp.inf)
                            part = scores[t * size : (t + 1) * size, s * size : (s + 1) * size]
                            tiles.append((part * jnp.exp2(gap)).astype(BF16))
                        weights = tiles[0] if len(tiles) == 1 else jnp.concatenate(tiles, axis=1)
                        outs.append(dot(weights, x_ref[way, lo:hi, at]))
                    y_ref[way, here, at] = (
                        jnp.where(half, outs[0], outs[1])
                        + skip[:, at] * x_ref[way, here, at].astype(F32)
                    )


def back_kernel(
    place_ref, y_ref, c_ref, came_ref, first_ref, cols_ref, gains_ref, own_gate_ref, u_ref,
    own_out_ref, late_ref, hidden_ref, keep_ref, give_ref, state_ref, w_ref,
):
    part = own_out_ref.shape[1] // 2
    inner = y_ref.shape[2] // 2
    ours = pl.multiple_of((2 * place_ref[0] + place_ref[1]) * part, part)
    blocks = [slice(b * BLOCK, (b + 1) * BLOCK) for b in range(2)]
    w_ref[:inner] = turned_out(place_ref, own_out_ref[...])
    w_ref[inner:] = turned_out(
        place_ref, jnp.concatenate([late_ref[:inner, inner:], late_ref[inner:, inner:]], axis=1)
    )
    same = (iota((inner, inner), 0) // HEADP == iota((inner, inner), 1) // HEADP).astype(BF16)
    for way in range(2):
        for n in range(8):
            for q in range(4):
                state_ref[way, n * 8 : n * 8 + 8, q * LANES : (q + 1) * LANES] = came_ref[
                    way * 32 + n * 4 + q
                ].astype(F32)
    for b, block in enumerate(blocks):
        decays = jnp.exp2(cols_ref[block])
        gate = jnp.concatenate(
            [own_gate_ref[block, :], gated_by(u_ref[block, :], late_ref[:, :inner])], axis=1
        )
        total = None
        for way in range(2):
            state = state_ref[way]
            if b != way:
                edge = BLOCK - 1 if way == 0 else BLOCK
                passed = jnp.exp2(cols_ref[edge : edge + 1])
                factor = spread(
                    [passed[:, way * 8 + i : way * 8 + i + 1] for i in range(8)], 1
                )
                state = factor * state + first_ref[way]
            state = jnp.concatenate([state, jnp.zeros_like(state)], axis=0).astype(BF16)
            decay = spread([decays[:, way * 8 + i : way * 8 + i + 1] for i in range(8)], BLOCK)
            mixer = y_ref[way, block, :] + decay * dot(c_ref[way, block, :], state)
            gated = mixer * gate
            square = (gated * gated).astype(BF16)
            mean = jnp.concatenate(
                [dot(square[:, g * inner : (g + 1) * inner], same) for g in range(2)], axis=1
            ) * (1.0 / HEADP)
            normed = gated * lax.rsqrt(mean + EPS)
            total = normed if total is None else total + normed
        mixed = (total * gains_ref[0:1]).astype(BF16)
        give_ref[block, :] = dot(mixed, w_ref[:, part:]).astype(BF16)
        keep_ref[block, :] = dot(mixed, w_ref[:, :part]) + hidden_ref[
            block, pl.ds(ours, part)
        ].astype(F32)


def shards(
    hidden_in,
    proj_zx,
    proj_bc,
    proj_dt,
    conv_x,
    conv_bc,
    dt_bias,
    decay_exp,
    skip_gain,
    norm_gain,
    out_proj,
):
    rows, width = hidden_in.shape[0], hidden_in.shape[1] // 2
    inner = proj_zx.shape[2]
    count = math.prod(lax.axis_size(axis) for axis in SEQ)
    rise = [(i, (i + 1) % count) for i in range(count)]
    fall = [((i + 1) % count, i) for i in range(count)]
    swap = [(0, 1), (1, 0)]
    x_hi, core = lax.axis_index("x_hi"), lax.axis_index("core")
    place = jnp.stack([x_hi, core, lax.axis_index(SEQ), jnp.int32(count)]).astype(jnp.int32)
    zx = proj_zx.reshape(width, 2 * inner)

    pack, late, head, tail = call(
        pack_kernel,
        (
            struct((PACKED, inner), BF16),
            struct((width, 2 * inner), BF16),
            struct((HALO, width), BF16),
            struct((HALO, width), BF16),
        ),
        [SMEM, VMEM] + [HBM] * 8,
        (VMEM,) * 4,
        cost(1_000_000, 0, 1_000_000),
        scratch=[
            pltpu.VMEM((4, width), BF16),
            pltpu.VMEM((REACH + 1, inner), BF16),
            pltpu.VMEM((1, 4), F32),
            pltpu.VMEM((1, 4), jnp.int32),
            pltpu.VMEM((1, 4), F32),
            pltpu.VMEM((1, inner), F32),
            dma(10),
        ],
    )(
        place,
        zx,
        *lying(
            proj_dt.T,
            conv_x,
            dt_bias.reshape(1, 4),
            decay_exp.reshape(1, 4),
            skip_gain.reshape(1, 4),
            norm_gain.reshape(1, inner),
            hidden_in,
            out_proj,
        ),
    )
    beside = (("seq_1", "x_hi"), [(0, 3), (3, 0), (1, 2), (2, 1)])
    other_pack = lax.ppermute(pack, *beside)
    prev = lax.ppermute(tail, SEQ, rise)
    following = lax.ppermute(head, SEQ, fall)

    other_late = lax.ppermute(late, *beside)
    u, own_gate, y, c, cols, first, gains, send = call(
        front_kernel,
        (
            struct((rows, width), BF16),
            struct((rows, inner), F32),
            struct((2, rows, 2 * inner), F32),
            struct((2, rows, LANES), BF16),
            struct((rows, LANES), F32),
            struct((2, STATE, 2 * inner), F32),
            struct((8, 2 * inner), F32),
            struct((count, 16, LANES), BF16),
        ),
        [SMEM] + [VMEM] * 8,
        (VMEM,) * 8,
        cost(8_000_000_000, 3_000_000, 24_000_000),
        scratch=[
            pltpu.VMEM((2, rows, 2 * inner), BF16),
            pltpu.VMEM((2, rows, LANES), BF16),
            pltpu.VMEM((48, rows), F32),
            pltpu.VMEM((2 * inner // LANES + 1, rows + 2 * HALO, LANES), F32),
        ],
    )(place, hidden_in, zx, prev, following, pack, other_pack, proj_bc, conv_bc)
    def passed_on(place, send, *others):
        got = lax.all_to_all(send, SEQ, 0, 0, tiled=True)
        scanned = call(
            scan_kernel,
            struct((count, 8, LANES), BF16),
            [SMEM, VMEM],
            VMEM,
            cost(1_000_000, 0, 400_000),
        )(place, got)
        return lax.all_to_all(scanned, SEQ, 0, 0, tiled=True), *others

    came, y, c, cols, first, gains, own_gate, u = lax.cond(
        core < 2,
        passed_on,
        lambda place, send, *others: (send[:, :8], *[-other for other in others]),
        place, send, y, c, cols, first, gains, own_gate, u,
    )

    keep, give = call(
        back_kernel,
        (struct((rows, inner), F32), struct((rows, inner), BF16)),
        [SMEM] + [VMEM] * 11,
        (VMEM, VMEM),
        cost(2_000_000_000, 600_000, 6_000_000),
        scratch=[
            pltpu.VMEM((2, STATE, 2 * inner), F32),
            pltpu.VMEM((2 * inner, 2 * inner), BF16),
        ],
    )(
        place, y, c, came, first, cols, gains, own_gate, u, out_proj, other_late, hidden_in
    )
    taken = lax.ppermute(give, "core", swap)
    return (keep + taken.astype(F32)).astype(BF16)


def solution(mesh):
    torus = Mesh(mesh.devices.reshape(8, 2, 4, 2, 2), SEQ + CH)
    placed = (
        P(SEQ, None),
        P(None, None, CH),
        P(),
        P(None, CH),
        P(None, CH),
        P(),
        P(CH),
        P(CH),
        P(CH),
        P(CH),
        P(CH, None),
    )
    return jax.shard_map(
        shards, mesh=torus, in_specs=placed, out_specs=P(SEQ, CH), check_vma=False
    )
```

```python
import math

import jax
import jax.numpy as jnp
from jax import lax
from jax.experimental import pallas as pl
from jax.experimental.pallas import tpu as pltpu
from jax.sharding import Mesh
from jax.sharding import PartitionSpec as P

BLOCK = 256
STATE = 64
HEADP = 64
REACH = 3
HALO = 8
LANES = 128
SEQ = ("seq_0", "seq_1", "seq_2")
CH = ("x_hi", "core")
EPS = 1e-05
LOG2E = math.log2(math.e)
F32 = jnp.float32
BF16 = jnp.bfloat16

VMEM = pl.BlockSpec(memory_space=pltpu.VMEM)
HBM = pl.BlockSpec(memory_space=pltpu.HBM)
SMEM = pl.BlockSpec(memory_space=pltpu.SMEM)


def cost(flops, transcendentals, bytes_accessed):
    return pl.CostEstimate(
        flops=flops, transcendentals=transcendentals, bytes_accessed=bytes_accessed
    )


def struct(shape, dtype):
    return jax.ShapeDtypeStruct(shape, dtype)


def lying(*arrays):
    return [pltpu.with_memory_space_constraint(array, pltpu.HBM) for array in arrays]


def start_copies(pairs, sems):
    copies = [
        pltpu.make_async_copy(source, target, sems.at[i]) for i, (source, target) in enumerate(pairs)
    ]
    for copy in copies:
        copy.start()
    return copies


def dma(n):
    return pltpu.SemaphoreType.DMA((n,))


def call(kernel, out_shape, specs, out_specs, estimate, mib=16, scratch=()):
    return pl.pallas_call(
        kernel,
        out_shape=out_shape,
        in_specs=specs,
        out_specs=out_specs,
        scratch_shapes=scratch,
        compiler_params=pltpu.CompilerParams(vmem_limit_bytes=mib * 1024 * 1024),
        cost_estimate=estimate,
    )


def iota(shape, dim):
    return lax.broadcasted_iota(jnp.int32, shape, dim)


def dot(a, b):
    return jnp.dot(a, b, preferred_element_type=F32)


def dot_nt(a, b):
    return lax.dot_general(a, b, (((1,), (1,)), ((), ())), preferred_element_type=F32)


def sigmoid(v):
    return 0.5 * jnp.tanh(0.5 * v) + 0.5


def parts_of(value):
    hi = value.astype(BF16).astype(F32)
    rest = value - hi
    mid = rest.astype(BF16).astype(F32)
    return hi, mid, rest - mid


def orient(n, strand):
    source, target = iota((n, n), 0), iota((n, n), 1)
    return (source == jnp.where(strand == 0, target, n - 1 - target)).astype(BF16)


DT_AT, TAP_AT, SMALL_AT, PACKED = 0, 8, 16, 32


def half_kernel(zx_ref, x_ref):
    x_ref[...] = zx_ref[:, x_ref.shape[1] :]


def pack_kernel(
    place_ref, zx_ref, dt_hbm, taps_hbm, bias_hbm, exp_hbm, skip_hbm, gain_hbm, hidden_hbm, out_hbm,
    pack_ref, late_ref, head_ref, tail_ref,
    dt_ref, taps_ref, bias_ref, exp_ref, skip_ref, gain_ref, sems,
):
    inner, heads = pack_ref.shape[1], dt_ref.shape[0]
    rows, width = hidden_hbm.shape[0], hidden_hbm.shape[1] // 2
    columns = pl.ds(pl.multiple_of(place_ref[0] * width, width), width)
    copies = start_copies(
        (
            (dt_hbm, dt_ref),
            (taps_hbm, taps_ref),
            (bias_hbm, bias_ref),
            (exp_hbm, exp_ref),
            (skip_hbm, skip_ref),
            (gain_hbm, gain_ref),
            (hidden_hbm.at[pl.ds(0, HALO), columns], head_ref),
            (hidden_hbm.at[pl.ds(rows - HALO, HALO), columns], tail_ref),
            (out_hbm.at[:, :inner], late_ref.at[:inner, inner:]),
            (out_hbm.at[:, inner:], late_ref.at[inner:, inner:]),
        ),
        sems,
    )
    late_ref[:, :inner] = zx_ref[:, :inner]
    for copy in copies:
        copy.wait()
    lane = iota((1, inner), 1)
    small = jnp.zeros((1, inner), F32)
    for h in range(heads):
        for k, ref in enumerate((bias_ref, exp_ref, skip_ref)):
            value = ref[:, h : h + 1].astype(F32)
            small = jnp.where(lane == k * heads + h, jnp.broadcast_to(value, (1, inner)), small)
    packed = [dt_ref[:, :inner].astype(F32), dt_ref[:, inner:].astype(F32), taps_ref[...].astype(F32)]
    packed.append(jnp.zeros((SMALL_AT - TAP_AT - taps_ref.shape[0], inner), F32))
    packed += parts_of(small) + parts_of(gain_ref[...])
    packed.append(jnp.zeros((PACKED - SMALL_AT - 6, inner), F32))
    pack_ref[...] = jnp.concatenate(packed, axis=0).astype(BF16)


def unpack(ref):
    tail = ref[SMALL_AT:].astype(F32)
    return tail[0:1] + tail[1:2] + tail[2:3], tail[3:4] + tail[4:5] + tail[5:6]


def column_of(smalls, at):
    row = iota((8, 1), 0)
    out = jnp.zeros((8, 1), F32)
    for g in range(2):
        for h in range(4):
            out = jnp.where(row == g * 4 + h, smalls[g][:, at + h : at + h + 1], out)
    return out


def spread(pieces, rows):
    half = iota((rows, LANES), 1) < HEADP
    wide = [jnp.broadcast_to(piece, (rows, LANES)) for piece in pieces]
    return jnp.concatenate(
        [jnp.where(half, wide[2 * q], wide[2 * q + 1]) for q in range(4)], axis=1
    )


def turned_out(place_ref, out):
    columns = out.shape[1]
    part = columns // 2
    source, target = iota((columns, columns), 0), iota((columns, columns), 1)
    column = jnp.where(target < part, target + place_ref[1] * part, target - place_ref[1] * part)
    wanted = jnp.where(place_ref[0] == 0, column, columns - 1 - column)
    return dot(out, (source == wanted).astype(BF16)).astype(BF16)


def gated_by(u, w):
    z = dot(u, w).astype(BF16).astype(F32)
    return z * sigmoid(z)


def front_kernel(
    place_ref, hidden_ref, zx_ref, other_x_ref, prev_ref, next_ref, own_ref, other_ref, bc_ref,
    tapbc_ref,
    u_ref, gate_ref, y_ref, c_ref, cols_ref, first_ref, gains_ref, send_ref,
    x_ref, b_ref, rows_ref, pad_ref,
):
    row_count, width = hidden_ref.shape[0], hidden_ref.shape[1] // 2
    inner = own_ref.shape[1]
    strand, position, count = place_ref[0], place_ref[2], place_ref[3]
    packs = (own_ref, other_ref)
    turn = orient(width, strand)
    u = hidden_ref[:, pl.ds(pl.multiple_of(strand * width, width), width)]
    u = dot(u, turn).astype(BF16)
    u_ref[...] = u
    gate_ref[...] = gated_by(u, zx_ref[:, :inner])
    before = jnp.where(position > 0, prev_ref[...].astype(F32), 0.0)
    after = jnp.where(position < count - 1, next_ref[...].astype(F32), 0.0)
    edge = dot(jnp.concatenate([before, after], axis=0).astype(BF16), turn)
    edge = edge.astype(BF16)

    raw = jnp.concatenate(
        [
            dot_nt(
                jnp.concatenate(
                    [ref[DT_AT : DT_AT + 4].astype(F32), ref[DT_AT + 4 : DT_AT + 8].astype(F32)],
                    axis=1,
                ).astype(BF16),
                u,
            )
            for ref in packs
        ],
        axis=0,
    )
    smalls, gains = zip(*[unpack(ref) for ref in packs])
    gains_ref[...] = jnp.concatenate(
        [
            jnp.concatenate(gains, axis=1),
            spread([smalls[g][:, 8 + h : 9 + h] for g in range(2) for h in range(4)], 1),
            jnp.zeros((6, 2 * inner), F32),
        ],
        axis=0,
    )
    v = raw + column_of(smalls, 0)
    rate = jnp.exp2(-column_of(smalls, 4)) * LOG2E
    step = jnp.maximum(v, 0.0) + jnp.log1p(jnp.exp(-jnp.abs(v)))
    parts = jnp.concatenate(parts_of(-step * rate), axis=0).astype(BF16)
    ahead = (iota((BLOCK, BLOCK), 0) <= iota((BLOCK, BLOCK), 1)).astype(BF16)
    behind = (iota((BLOCK, BLOCK), 0) >= iota((BLOCK, BLOCK), 1)).astype(BF16)
    cums, ends = [], []
    for b in range(2):
        piece = parts[:, b * BLOCK : (b + 1) * BLOCK]
        both = []
        for mask in (ahead, behind):
            full = dot(piece, mask)
            both.append(full[:8] + full[8:16] + full[16:])
        cums.append(jnp.concatenate(both, axis=0))
        last = jnp.concatenate([both[0][:, BLOCK - 1 :], both[1][:, :1]], axis=0)
        ends.append(jnp.broadcast_to(last, (16, BLOCK)))
    cum = jnp.concatenate(cums, axis=1)
    end = jnp.concatenate(ends, axis=1)
    step = jnp.concatenate([step, step], axis=0)
    rows_ref[:16] = cum
    rows_ref[16:32] = cum - jnp.log2(step)
    rows_ref[32:] = jnp.exp2(jnp.minimum(end - cum, 0.0)) * step
    cols_ref[...] = jnp.concatenate([cum, jnp.zeros((LANES - 16, row_count), F32)], axis=0).T
    totals = [ends[b][:, :1] for b in range(2)]

    chunk = 32
    tiles = inner // LANES
    for g in range(3):
        w = (zx_ref[:, inner:], other_x_ref[...], bc_ref[...])[g]
        middle = dot(u, w).astype(BF16).astype(F32)
        outer = dot(edge, w).astype(BF16).astype(F32)
        for k in range(w.shape[1] // LANES):
            at, lanes = g * tiles + k, slice(k * LANES, (k + 1) * LANES)
            pad_ref[at, :HALO] = outer[:HALO, lanes]
            pad_ref[at, HALO : HALO + row_count] = middle[:, lanes]
            pad_ref[at, HALO + row_count :] = outer[HALO:, lanes]
    taps = jnp.concatenate(
        [ref[TAP_AT : TAP_AT + REACH + 1].astype(F32) for ref in packs]
        + [tapbc_ref[...].astype(F32)],
        axis=1,
    )
    groups = taps.shape[1] // LANES
    low_lane = iota((chunk, LANES), 1) < STATE
    for group in range(groups):
        at = slice(group * LANES, (group + 1) * LANES)
        tap = [taps[j : j + 1, at] for j in range(REACH + 1)]
        for r in range(0, row_count, chunk):
            start = r + HALO - REACH
            window = [
                pad_ref[group, start + k : start + k + chunk] for k in range(2 * REACH + 1)
            ]
            for way in range(2):
                acc = tap[0] * window[0 if way == 0 else 2 * REACH]
                for j in range(1, REACH + 1):
                    acc = acc + tap[j] * window[j if way == 0 else 2 * REACH - j]
                value = (acc * sigmoid(acc)).astype(BF16)
                if group < groups - 1:
                    x_ref[way, r : r + chunk, at] = value
                else:
                    b_ref[way, r : r + chunk, :] = value
                    swapped = pltpu.roll(value.astype(F32), LANES - STATE, 1)
                    c_ref[way, r : r + chunk, :] = jnp.where(low_lane, swapped, 0.0).astype(BF16)


    half = iota((STATE, LANES), 1) < HEADP
    row8 = iota((8, LANES), 0)
    for way in range(2):
        states = []
        for b in range(2):
            block = slice(b * BLOCK, (b + 1) * BLOCK)
            bt = b_ref[way, block, :].astype(F32).T[:STATE]
            tiles = []
            for g in range(2):
                at = 32 + way * 8 + g * 4
                scaled = jnp.concatenate(
                    [
                        (bt * rows_ref[at + h : at + h + 1, block]).astype(BF16)
                        for h in range(4)
                    ],
                    axis=0,
                )
                full = dot(scaled, x_ref[way, block, g * inner : (g + 1) * inner])
                tiles.append(jnp.where(half, full[:64, :128], full[64:128, :128]))
                tiles.append(jnp.where(half, full[128:192, 128:], full[192:, 128:]))
            states.append(tiles)
        first, last = (0, 1) if way == 0 else (1, 0)
        at = slice(way * 8, way * 8 + 8)
        last_total = jnp.exp2(totals[last][at])
        both_total = jnp.exp2(totals[0][at] + totals[1][at])
        factor = spread([last_total[i : i + 1] for i in range(8)], 1)
        whole = spread([both_total[i : i + 1] for i in range(8)], 8)
        for q in range(4):
            lanes = slice(q * LANES, (q + 1) * LANES)
            state = factor[:, lanes] * states[first][q] + states[last][q]
            first_ref[way, :, lanes] = states[first][q]
            hi, mid, low = parts_of(whole[:, lanes])
            decay = jnp.where(
                row8 == 0, hi, jnp.where(row8 == 1, mid, jnp.where(row8 == 2, low, 0.0))
            )
            for n in range(8):
                send_ref[way * 32 + n * 4 + q] = jnp.concatenate(
                    [state[n * 8 : n * 8 + 8], decay], axis=0
                ).astype(BF16)
    inside(x_ref, b_ref, c_ref, rows_ref, cols_ref, gains_ref, y_ref)


def scan_kernel(place_ref, got_ref, out_ref):
    count = got_ref.shape[0]
    backward = place_ref[2] >= count // 2
    state = jnp.zeros((8, LANES), F32)
    for i in range(count):
        k = jnp.where(backward, count - 1 - i, i)
        piece = got_ref[k].astype(F32)
        out_ref[k] = state.astype(BF16)
        decay = jnp.sum(piece[8:], axis=0, keepdims=True)
        state = decay * state + piece[:8]


def inside(x_ref, b_ref, c_ref, rows_ref, cols_ref, gains_ref, y_ref):
    size = 128
    low = iota((size, size), 0) >= iota((size, size), 1)
    high = iota((size, size), 0) <= iota((size, size), 1)
    half = iota((size, LANES), 1) < HEADP
    skip = gains_ref[1:2]
    for way in range(2):
        for b in range(2):
            block = slice(b * BLOCK, (b + 1) * BLOCK)
            scores = dot_nt(c_ref[way, block, :], b_ref[way, block, :])
            for pair in range(4):
                at = slice(pair * LANES, (pair + 1) * LANES)
                for t in range(2):
                    here = slice(b * BLOCK + t * size, b * BLOCK + (t + 1) * size)
                    seen = [s for s in range(2) if (s <= t if way == 0 else s >= t)]
                    lo = b * BLOCK + seen[0] * size
                    hi = b * BLOCK + (seen[-1] + 1) * size
                    outs = []
                    for h in (2 * pair, 2 * pair + 1):
                        i = way * 8 + h
                        gone = jnp.broadcast_to(cols_ref[here, i : i + 1], (size, size))
                        tiles = []
                        for s in seen:
                            there = slice(b * BLOCK + s * size, b * BLOCK + (s + 1) * size)
                            gap = gone - rows_ref[16 + i : 17 + i, there]
                            if s == t:
                                gap = jnp.where(low if way == 0 else high, gap, -jnp.inf)
                            part = scores[t * size : (t + 1) * size, s * size : (s + 1) * size]
                            tiles.append((part * jnp.exp2(gap)).astype(BF16))
                        weights = tiles[0] if len(tiles) == 1 else jnp.concatenate(tiles, axis=1)
                        outs.append(dot(weights, x_ref[way, lo:hi, at]))
                    y_ref[way, here, at] = (
                        jnp.where(half, outs[0], outs[1])
                        + skip[:, at] * x_ref[way, here, at].astype(F32)
                    )


def back_kernel(
    place_ref, y_ref, c_ref, came_ref, first_ref, cols_ref, gains_ref, own_gate_ref, u_ref,
    own_out_ref, late_ref, hidden_ref, keep_ref, give_ref, state_ref, w_ref,
):
    part = own_out_ref.shape[1] // 2
    inner = y_ref.shape[2] // 2
    ours = pl.multiple_of((2 * place_ref[0] + place_ref[1]) * part, part)
    blocks = [slice(b * BLOCK, (b + 1) * BLOCK) for b in range(2)]
    w_ref[:inner] = turned_out(place_ref, own_out_ref[...])
    w_ref[inner:] = turned_out(
        place_ref, jnp.concatenate([late_ref[:inner, inner:], late_ref[inner:, inner:]], axis=1)
    )
    same = (iota((inner, inner), 0) // HEADP == iota((inner, inner), 1) // HEADP).astype(BF16)
    for way in range(2):
        for n in range(8):
            for q in range(4):
                state_ref[way, n * 8 : n * 8 + 8, q * LANES : (q + 1) * LANES] = came_ref[
                    way * 32 + n * 4 + q
                ].astype(F32)
    for b, block in enumerate(blocks):
        decays = jnp.exp2(cols_ref[block])
        gate = jnp.concatenate(
            [own_gate_ref[block, :], gated_by(u_ref[block, :], late_ref[:, :inner])], axis=1
        )
        total = None
        for way in range(2):
            state = state_ref[way]
            if b != way:
                edge = BLOCK - 1 if way == 0 else BLOCK
                passed = jnp.exp2(cols_ref[edge : edge + 1])
                factor = spread(
                    [passed[:, way * 8 + i : way * 8 + i + 1] for i in range(8)], 1
                )
                state = factor * state + first_ref[way]
            state = jnp.concatenate([state, jnp.zeros_like(state)], axis=0).astype(BF16)
            decay = spread([decays[:, way * 8 + i : way * 8 + i + 1] for i in range(8)], BLOCK)
            mixer = y_ref[way, block, :] + decay * dot(c_ref[way, block, :], state)
            gated = mixer * gate
            square = (gated * gated).astype(BF16)
            mean = jnp.concatenate(
                [dot(square[:, g * inner : (g + 1) * inner], same) for g in range(2)], axis=1
            ) * (1.0 / HEADP)
            normed = gated * lax.rsqrt(mean + EPS)
            total = normed if total is None else total + normed
        mixed = (total * gains_ref[0:1]).astype(BF16)
        give_ref[block, :] = dot(mixed, w_ref[:, part:]).astype(BF16)
        keep_ref[block, :] = dot(mixed, w_ref[:, :part]) + hidden_ref[
            block, pl.ds(ours, part)
        ].astype(F32)


def shards(
    hidden_in,
    proj_zx,
    proj_bc,
    proj_dt,
    conv_x,
    conv_bc,
    dt_bias,
    decay_exp,
    skip_gain,
    norm_gain,
    out_proj,
):
    rows, width = hidden_in.shape[0], hidden_in.shape[1] // 2
    inner = proj_zx.shape[2]
    count = math.prod(lax.axis_size(axis) for axis in SEQ)
    rise = [(i, (i + 1) % count) for i in range(count)]
    fall = [((i + 1) % count, i) for i in range(count)]
    swap = [(0, 1), (1, 0)]
    x_hi, core = lax.axis_index("x_hi"), lax.axis_index("core")
    place = jnp.stack([x_hi, core, lax.axis_index(SEQ), jnp.int32(count)]).astype(jnp.int32)
    beside = (("seq_1", "x_hi"), [(0, 3), (3, 0), (1, 2), (2, 1)])
    zx = proj_zx.reshape(width, 2 * inner)
    own_x = call(
        half_kernel, struct((width, inner), BF16), [VMEM], VMEM, cost(1_000, 0, 500_000), mib=2
    )(zx)
    other_x = lax.ppermute(own_x, *beside)

    pack, late, head, tail = call(
        pack_kernel,
        (
            struct((PACKED, inner), BF16),
            struct((width, 2 * inner), BF16),
            struct((HALO, width), BF16),
            struct((HALO, width), BF16),
        ),
        [SMEM, VMEM] + [HBM] * 8,
        (VMEM,) * 4,
        cost(1_000_000, 0, 1_000_000),
        scratch=[
            pltpu.VMEM((4, width), BF16),
            pltpu.VMEM((REACH + 1, inner), BF16),
            pltpu.VMEM((1, 4), F32),
            pltpu.VMEM((1, 4), jnp.int32),
            pltpu.VMEM((1, 4), F32),
            pltpu.VMEM((1, inner), F32),
            dma(10),
        ],
    )(
        place,
        zx,
        *lying(
            proj_dt.T,
            conv_x,
            dt_bias.reshape(1, 4),
            decay_exp.reshape(1, 4),
            skip_gain.reshape(1, 4),
            norm_gain.reshape(1, inner),
            hidden_in,
            out_proj,
        ),
    )
    other_pack = lax.ppermute(pack, *beside)
    prev = lax.ppermute(tail, SEQ, rise)
    following = lax.ppermute(head, SEQ, fall)

    other_late = lax.ppermute(late, *beside)
    u, own_gate, y, c, cols, first, gains, send = call(
        front_kernel,
        (
            struct((rows, width), BF16),
            struct((rows, inner), F32),
            struct((2, rows, 2 * inner), F32),
            struct((2, rows, LANES), BF16),
            struct((rows, LANES), F32),
            struct((2, STATE, 2 * inner), F32),
            struct((8, 2 * inner), F32),
            struct((count, 16, LANES), BF16),
        ),
        [SMEM] + [VMEM] * 9,
        (VMEM,) * 8,
        cost(8_000_000_000, 3_000_000, 24_000_000),
        scratch=[
            pltpu.VMEM((2, rows, 2 * inner), BF16),
            pltpu.VMEM((2, rows, LANES), BF16),
            pltpu.VMEM((48, rows), F32),
            pltpu.VMEM((2 * inner // LANES + 1, rows + 2 * HALO, LANES), F32),
        ],
    )(
        place, hidden_in, zx, other_x, prev, following, pack, other_pack, proj_bc, conv_bc
    )
    def passed_on(place, send, *others):
        got = lax.all_to_all(send, SEQ, 0, 0, tiled=True)
        scanned = call(
            scan_kernel,
            struct((count, 8, LANES), BF16),
            [SMEM, VMEM],
            VMEM,
            cost(1_000_000, 0, 400_000),
        )(place, got)
        return lax.all_to_all(scanned, SEQ, 0, 0, tiled=True), *others

    came, y, c, cols, first, gains, own_gate, u = lax.cond(
        core < 2,
        passed_on,
        lambda place, send, *others: (send[:, :8], *[-other for other in others]),
        place, send, y, c, cols, first, gains, own_gate, u,
    )

    keep, give = call(
        back_kernel,
        (struct((rows, inner), F32), struct((rows, inner), BF16)),
        [SMEM] + [VMEM] * 11,
        (VMEM, VMEM),
        cost(2_000_000_000, 600_000, 6_000_000),
        scratch=[
            pltpu.VMEM((2, STATE, 2 * inner), F32),
            pltpu.VMEM((2 * inner, 2 * inner), BF16),
        ],
    )(
        place, y, c, came, first, cols, gains, own_gate, u, out_proj, other_late, hidden_in
    )
    taken = lax.ppermute(give, "core", swap)
    return (keep + taken.astype(F32)).astype(BF16)


def solution(mesh):
    torus = Mesh(mesh.devices.reshape(8, 2, 4, 2, 2), SEQ + CH)
    placed = (
        P(SEQ, None),
        P(None, None, CH),
        P(),
        P(None, CH),
        P(None, CH),
        P(),
        P(CH),
        P(CH),
        P(CH),
        P(CH),
        P(CH, None),
    )
    return jax.shard_map(
        shards, mesh=torus, in_specs=placed, out_specs=P(SEQ, CH), check_vma=False
    )
```

```python
import math

import jax
import jax.numpy as jnp
from jax import lax
from jax.experimental import pallas as pl
from jax.experimental.pallas import tpu as pltpu
from jax.sharding import Mesh
from jax.sharding import PartitionSpec as P

BLOCK = 256
STATE = 64
HEADP = 64
REACH = 3
HALO = 8
LANES = 128
SEQ = ("seq_0", "seq_1", "seq_2")
CH = ("x_hi", "core")
EPS = 1e-05
LOG2E = math.log2(math.e)
F32 = jnp.float32
BF16 = jnp.bfloat16

VMEM = pl.BlockSpec(memory_space=pltpu.VMEM)
HBM = pl.BlockSpec(memory_space=pltpu.HBM)
SMEM = pl.BlockSpec(memory_space=pltpu.SMEM)


def cost(flops, transcendentals, bytes_accessed):
    return pl.CostEstimate(
        flops=flops, transcendentals=transcendentals, bytes_accessed=bytes_accessed
    )


def struct(shape, dtype):
    return jax.ShapeDtypeStruct(shape, dtype)


def lying(*arrays):
    return [pltpu.with_memory_space_constraint(array, pltpu.HBM) for array in arrays]


def start_copies(pairs, sems):
    copies = [
        pltpu.make_async_copy(source, target, sems.at[i]) for i, (source, target) in enumerate(pairs)
    ]
    for copy in copies:
        copy.start()
    return copies


def dma(n):
    return pltpu.SemaphoreType.DMA((n,))


def call(kernel, out_shape, specs, out_specs, estimate, mib=16, scratch=()):
    return pl.pallas_call(
        kernel,
        out_shape=out_shape,
        in_specs=specs,
        out_specs=out_specs,
        scratch_shapes=scratch,
        compiler_params=pltpu.CompilerParams(vmem_limit_bytes=mib * 1024 * 1024),
        cost_estimate=estimate,
    )


def iota(shape, dim):
    return lax.broadcasted_iota(jnp.int32, shape, dim)


def dot(a, b):
    return jnp.dot(a, b, preferred_element_type=F32)


def dot_nt(a, b):
    return lax.dot_general(a, b, (((1,), (1,)), ((), ())), preferred_element_type=F32)


def sigmoid(v):
    return 0.5 * jnp.tanh(0.5 * v) + 0.5


def parts_of(value):
    hi = value.astype(BF16).astype(F32)
    rest = value - hi
    mid = rest.astype(BF16).astype(F32)
    return hi, mid, rest - mid


def orient(n, strand):
    source, target = iota((n, n), 0), iota((n, n), 1)
    return (source == jnp.where(strand == 0, target, n - 1 - target)).astype(BF16)


DT_AT, TAP_AT, SMALL_AT, PACKED = 0, 8, 16, 32


def half_kernel(zx_ref, x_ref):
    x_ref[...] = zx_ref[:, x_ref.shape[1] :]


def pack_kernel(
    place_ref, zx_ref, dt_hbm, taps_hbm, bias_hbm, exp_hbm, skip_hbm, gain_hbm, hidden_hbm, out_hbm,
    pack_ref, late_ref, far_ref, near_ref,
    dt_ref, taps_ref, bias_ref, exp_ref, skip_ref, gain_ref, sems,
):
    inner, heads = pack_ref.shape[1], dt_ref.shape[0]
    rows, width = hidden_hbm.shape[0], hidden_hbm.shape[1] // 2
    columns = pl.ds(pl.multiple_of(place_ref[0] * width, width), width)
    odd, last = lax.rem(place_ref[2], 2), rows - HALO
    copies = start_copies(
        (
            (dt_hbm, dt_ref),
            (taps_hbm, taps_ref),
            (bias_hbm, bias_ref),
            (exp_hbm, exp_ref),
            (skip_hbm, skip_ref),
            (gain_hbm, gain_ref),
            (hidden_hbm.at[pl.ds(pl.multiple_of(odd * last, HALO), HALO), columns], far_ref),
            (hidden_hbm.at[pl.ds(pl.multiple_of((1 - odd) * last, HALO), HALO), columns], near_ref),
            (out_hbm.at[:, :inner], late_ref.at[:inner, inner:]),
            (out_hbm.at[:, inner:], late_ref.at[inner:, inner:]),
        ),
        sems,
    )
    late_ref[:, :inner] = zx_ref[:, :inner]
    for copy in copies:
        copy.wait()
    lane = iota((1, inner), 1)
    small = jnp.zeros((1, inner), F32)
    for h in range(heads):
        for k, ref in enumerate((bias_ref, exp_ref, skip_ref)):
            value = ref[:, h : h + 1].astype(F32)
            small = jnp.where(lane == k * heads + h, jnp.broadcast_to(value, (1, inner)), small)
    packed = [dt_ref[:, :inner].astype(F32), dt_ref[:, inner:].astype(F32), taps_ref[...].astype(F32)]
    packed.append(jnp.zeros((SMALL_AT - TAP_AT - taps_ref.shape[0], inner), F32))
    packed += parts_of(small) + parts_of(gain_ref[...])
    packed.append(jnp.zeros((PACKED - SMALL_AT - 6, inner), F32))
    pack_ref[...] = jnp.concatenate(packed, axis=0).astype(BF16)


def unpack(ref):
    tail = ref[SMALL_AT:].astype(F32)
    return tail[0:1] + tail[1:2] + tail[2:3], tail[3:4] + tail[4:5] + tail[5:6]


def column_of(smalls, at):
    row = iota((8, 1), 0)
    out = jnp.zeros((8, 1), F32)
    for g in range(2):
        for h in range(4):
            out = jnp.where(row == g * 4 + h, smalls[g][:, at + h : at + h + 1], out)
    return out


def spread(pieces, rows):
    half = iota((rows, LANES), 1) < HEADP
    wide = [jnp.broadcast_to(piece, (rows, LANES)) for piece in pieces]
    return jnp.concatenate(
        [jnp.where(half, wide[2 * q], wide[2 * q + 1]) for q in range(4)], axis=1
    )


def turned_out(place_ref, out):
    columns = out.shape[1]
    part = columns // 2
    source, target = iota((columns, columns), 0), iota((columns, columns), 1)
    column = jnp.where(target < part, target + place_ref[1] * part, target - place_ref[1] * part)
    wanted = jnp.where(place_ref[0] == 0, column, columns - 1 - column)
    return dot(out, (source == wanted).astype(BF16)).astype(BF16)


def gated_by(u, w):
    z = dot(u, w).astype(BF16).astype(F32)
    return z * sigmoid(z)


def front_kernel(
    place_ref, hidden_ref, zx_ref, other_x_ref, far_ref, near_ref, own_ref, other_ref, bc_ref,
    tapbc_ref,
    u_ref, gate_ref, y_ref, c_ref, cols_ref, first_ref, gains_ref, send_ref,
    x_ref, b_ref, rows_ref, pad_ref,
):
    row_count, width = hidden_ref.shape[0], hidden_ref.shape[1] // 2
    inner = own_ref.shape[1]
    strand, position, count = place_ref[0], place_ref[2], place_ref[3]
    packs = (own_ref, other_ref)
    turn = orient(width, strand)
    u = hidden_ref[:, pl.ds(pl.multiple_of(strand * width, width), width)]
    u = dot(u, turn).astype(BF16)
    u_ref[...] = u
    gate_ref[...] = gated_by(u, zx_ref[:, :inner])
    odd = lax.rem(position, 2) == 1
    far, near = far_ref[...].astype(F32), near_ref[...].astype(F32)
    before = jnp.where(position > 0, jnp.where(odd, near, far), 0.0)
    after = jnp.where(position < count - 1, jnp.where(odd, far, near), 0.0)
    edge = dot(jnp.concatenate([before, after], axis=0).astype(BF16), turn)
    edge = edge.astype(BF16)

    raw = jnp.concatenate(
        [
            dot_nt(
                jnp.concatenate(
                    [ref[DT_AT : DT_AT + 4].astype(F32), ref[DT_AT + 4 : DT_AT + 8].astype(F32)],
                    axis=1,
                ).astype(BF16),
                u,
            )
            for ref in packs
        ],
        axis=0,
    )
    smalls, gains = zip(*[unpack(ref) for ref in packs])
    gains_ref[...] = jnp.concatenate(
        [
            jnp.concatenate(gains, axis=1),
            spread([smalls[g][:, 8 + h : 9 + h] for g in range(2) for h in range(4)], 1),
            jnp.zeros((6, 2 * inner), F32),
        ],
        axis=0,
    )
    v = raw + column_of(smalls, 0)
    rate = jnp.exp2(-column_of(smalls, 4)) * LOG2E
    step = jnp.maximum(v, 0.0) + jnp.log1p(jnp.exp(-jnp.abs(v)))
    parts = jnp.concatenate(parts_of(-step * rate), axis=0).astype(BF16)
    ahead = (iota((BLOCK, BLOCK), 0) <= iota((BLOCK, BLOCK), 1)).astype(BF16)
    behind = (iota((BLOCK, BLOCK), 0) >= iota((BLOCK, BLOCK), 1)).astype(BF16)
    cums, ends = [], []
    for b in range(2):
        piece = parts[:, b * BLOCK : (b + 1) * BLOCK]
        both = []
        for mask in (ahead, behind):
            full = dot(piece, mask)
            both.append(full[:8] + full[8:16] + full[16:])
        cums.append(jnp.concatenate(both, axis=0))
        last = jnp.concatenate([both[0][:, BLOCK - 1 :], both[1][:, :1]], axis=0)
        ends.append(jnp.broadcast_to(last, (16, BLOCK)))
    cum = jnp.concatenate(cums, axis=1)
    end = jnp.concatenate(ends, axis=1)
    step = jnp.concatenate([step, step], axis=0)
    rows_ref[:16] = cum
    rows_ref[16:32] = cum - jnp.log2(step)
    rows_ref[32:] = jnp.exp2(jnp.minimum(end - cum, 0.0)) * step
    cols_ref[...] = jnp.concatenate([cum, jnp.zeros((LANES - 16, row_count), F32)], axis=0).T
    totals = [ends[b][:, :1] for b in range(2)]

    chunk = 32
    tiles = inner // LANES
    for g in range(3):
        w = (zx_ref[:, inner:], other_x_ref[...], bc_ref[...])[g]
        middle = dot(u, w).astype(BF16).astype(F32)
        outer = dot(edge, w).astype(BF16).astype(F32)
        for k in range(w.shape[1] // LANES):
            at, lanes = g * tiles + k, slice(k * LANES, (k + 1) * LANES)
            pad_ref[at, :HALO] = outer[:HALO, lanes]
            pad_ref[at, HALO : HALO + row_count] = middle[:, lanes]
            pad_ref[at, HALO + row_count :] = outer[HALO:, lanes]
    taps = jnp.concatenate(
        [ref[TAP_AT : TAP_AT + REACH + 1].astype(F32) for ref in packs]
        + [tapbc_ref[...].astype(F32)],
        axis=1,
    )
    groups = taps.shape[1] // LANES
    low_lane = iota((chunk, LANES), 1) < STATE
    for group in range(groups):
        at = slice(group * LANES, (group + 1) * LANES)
        tap = [taps[j : j + 1, at] for j in range(REACH + 1)]
        for r in range(0, row_count, chunk):
            start = r + HALO - REACH
            window = [
                pad_ref[group, start + k : start + k + chunk] for k in range(2 * REACH + 1)
            ]
            for way in range(2):
                acc = tap[0] * window[0 if way == 0 else 2 * REACH]
                for j in range(1, REACH + 1):
                    acc = acc + tap[j] * window[j if way == 0 else 2 * REACH - j]
                value = (acc * sigmoid(acc)).astype(BF16)
                if group < groups - 1:
                    x_ref[way, r : r + chunk, at] = value
                else:
                    b_ref[way, r : r + chunk, :] = value
                    swapped = pltpu.roll(value.astype(F32), LANES - STATE, 1)
                    c_ref[way, r : r + chunk, :] = jnp.where(low_lane, swapped, 0.0).astype(BF16)


    half = iota((STATE, LANES), 1) < HEADP
    row8 = iota((8, LANES), 0)
    for way in range(2):
        states = []
        for b in range(2):
            block = slice(b * BLOCK, (b + 1) * BLOCK)
            bt = b_ref[way, block, :].astype(F32).T[:STATE]
            tiles = []
            for g in range(2):
                at = 32 + way * 8 + g * 4
                scaled = jnp.concatenate(
                    [
                        (bt * rows_ref[at + h : at + h + 1, block]).astype(BF16)
                        for h in range(4)
                    ],
                    axis=0,
                )
                full = dot(scaled, x_ref[way, block, g * inner : (g + 1) * inner])
                tiles.append(jnp.where(half, full[:64, :128], full[64:128, :128]))
                tiles.append(jnp.where(half, full[128:192, 128:], full[192:, 128:]))
            states.append(tiles)
        first, last = (0, 1) if way == 0 else (1, 0)
        at = slice(way * 8, way * 8 + 8)
        last_total = jnp.exp2(totals[last][at])
        both_total = jnp.exp2(totals[0][at] + totals[1][at])
        factor = spread([last_total[i : i + 1] for i in range(8)], 1)
        whole = spread([both_total[i : i + 1] for i in range(8)], 8)
        for q in range(4):
            lanes = slice(q * LANES, (q + 1) * LANES)
            state = factor[:, lanes] * states[first][q] + states[last][q]
            first_ref[way, :, lanes] = states[first][q]
            hi, mid, low = parts_of(whole[:, lanes])
            decay = jnp.where(
                row8 == 0, hi, jnp.where(row8 == 1, mid, jnp.where(row8 == 2, low, 0.0))
            )
            for n in range(8):
                send_ref[way * 32 + n * 4 + q] = jnp.concatenate(
                    [state[n * 8 : n * 8 + 8], decay], axis=0
                ).astype(BF16)
    inside(x_ref, b_ref, c_ref, rows_ref, cols_ref, gains_ref, y_ref)


def scan_kernel(place_ref, got_ref, out_ref):
    count = got_ref.shape[0]
    backward = place_ref[2] >= count // 2
    state = jnp.zeros((8, LANES), F32)
    for i in range(count):
        k = jnp.where(backward, count - 1 - i, i)
        piece = got_ref[k].astype(F32)
        out_ref[k] = state.astype(BF16)
        decay = jnp.sum(piece[8:], axis=0, keepdims=True)
        state = decay * state + piece[:8]


def inside(x_ref, b_ref, c_ref, rows_ref, cols_ref, gains_ref, y_ref):
    size = 128
    low = iota((size, size), 0) >= iota((size, size), 1)
    high = iota((size, size), 0) <= iota((size, size), 1)
    half = iota((size, LANES), 1) < HEADP
    skip = gains_ref[1:2]
    for way in range(2):
        for b in range(2):
            block = slice(b * BLOCK, (b + 1) * BLOCK)
            scores = dot_nt(c_ref[way, block, :], b_ref[way, block, :])
            for pair in range(4):
                at = slice(pair * LANES, (pair + 1) * LANES)
                for t in range(2):
                    here = slice(b * BLOCK + t * size, b * BLOCK + (t + 1) * size)
                    seen = [s for s in range(2) if (s <= t if way == 0 else s >= t)]
                    lo = b * BLOCK + seen[0] * size
                    hi = b * BLOCK + (seen[-1] + 1) * size
                    outs = []
                    for h in (2 * pair, 2 * pair + 1):
                        i = way * 8 + h
                        gone = jnp.broadcast_to(cols_ref[here, i : i + 1], (size, size))
                        tiles = []
                        for s in seen:
                            there = slice(b * BLOCK + s * size, b * BLOCK + (s + 1) * size)
                            gap = gone - rows_ref[16 + i : 17 + i, there]
                            if s == t:
                                gap = jnp.where(low if way == 0 else high, gap, -jnp.inf)
                            part = scores[t * size : (t + 1) * size, s * size : (s + 1) * size]
                            tiles.append((part * jnp.exp2(gap)).astype(BF16))
                        weights = tiles[0] if len(tiles) == 1 else jnp.concatenate(tiles, axis=1)
                        outs.append(dot(weights, x_ref[way, lo:hi, at]))
                    y_ref[way, here, at] = (
                        jnp.where(half, outs[0], outs[1])
                        + skip[:, at] * x_ref[way, here, at].astype(F32)
                    )


def back_kernel(
    place_ref, y_ref, c_ref, came_ref, first_ref, cols_ref, gains_ref, own_gate_ref, u_ref,
    own_out_ref, late_ref, hidden_ref, keep_ref, give_ref, state_ref, w_ref,
):
    part = own_out_ref.shape[1] // 2
    inner = y_ref.shape[2] // 2
    ours = pl.multiple_of((2 * place_ref[0] + place_ref[1]) * part, part)
    blocks = [slice(b * BLOCK, (b + 1) * BLOCK) for b in range(2)]
    w_ref[:inner] = turned_out(place_ref, own_out_ref[...])
    w_ref[inner:] = turned_out(
        place_ref, jnp.concatenate([late_ref[:inner, inner:], late_ref[inner:, inner:]], axis=1)
    )
    same = (iota((inner, inner), 0) // HEADP == iota((inner, inner), 1) // HEADP).astype(BF16)
    for way in range(2):
        for n in range(8):
            for q in range(4):
                state_ref[way, n * 8 : n * 8 + 8, q * LANES : (q + 1) * LANES] = came_ref[
                    way * 32 + n * 4 + q
                ].astype(F32)
    for b, block in enumerate(blocks):
        decays = jnp.exp2(cols_ref[block])
        gate = jnp.concatenate(
            [own_gate_ref[block, :], gated_by(u_ref[block, :], late_ref[:, :inner])], axis=1
        )
        total = None
        for way in range(2):
            state = state_ref[way]
            if b != way:
                edge = BLOCK - 1 if way == 0 else BLOCK
                passed = jnp.exp2(cols_ref[edge : edge + 1])
                factor = spread(
                    [passed[:, way * 8 + i : way * 8 + i + 1] for i in range(8)], 1
                )
                state = factor * state + first_ref[way]
            state = jnp.concatenate([state, jnp.zeros_like(state)], axis=0).astype(BF16)
            decay = spread([decays[:, way * 8 + i : way * 8 + i + 1] for i in range(8)], BLOCK)
            mixer = y_ref[way, block, :] + decay * dot(c_ref[way, block, :], state)
            gated = mixer * gate
            square = (gated * gated).astype(BF16)
            mean = jnp.concatenate(
                [dot(square[:, g * inner : (g + 1) * inner], same) for g in range(2)], axis=1
            ) * (1.0 / HEADP)
            normed = gated * lax.rsqrt(mean + EPS)
            total = normed if total is None else total + normed
        mixed = (total * gains_ref[0:1]).astype(BF16)
        give_ref[block, :] = dot(mixed, w_ref[:, part:]).astype(BF16)
        keep_ref[block, :] = dot(mixed, w_ref[:, :part]) + hidden_ref[
            block, pl.ds(ours, part)
        ].astype(F32)


def shards(
    hidden_in,
    proj_zx,
    proj_bc,
    proj_dt,
    conv_x,
    conv_bc,
    dt_bias,
    decay_exp,
    skip_gain,
    norm_gain,
    out_proj,
):
    rows, width = hidden_in.shape[0], hidden_in.shape[1] // 2
    inner = proj_zx.shape[2]
    count = math.prod(lax.axis_size(axis) for axis in SEQ)
    outer = [(i, i + 1 if i % 2 else i - 1) for i in range(1, count - 1)]
    inside_pairs = [(i, i - 1 if i % 2 else i + 1) for i in range(count)]
    swap = [(0, 1), (1, 0)]
    x_hi, core = lax.axis_index("x_hi"), lax.axis_index("core")
    place = jnp.stack([x_hi, core, lax.axis_index(SEQ), jnp.int32(count)]).astype(jnp.int32)
    beside = (("seq_1", "x_hi"), [(0, 3), (3, 0), (1, 2), (2, 1)])
    zx = proj_zx.reshape(width, 2 * inner)
    own_x = call(
        half_kernel, struct((width, inner), BF16), [VMEM], VMEM, cost(1_000, 0, 500_000), mib=2
    )(zx)
    other_x = lax.ppermute(own_x, *beside)

    pack, late, far, near = call(
        pack_kernel,
        (
            struct((PACKED, inner), BF16),
            struct((width, 2 * inner), BF16),
            struct((HALO, width), BF16),
            struct((HALO, width), BF16),
        ),
        [SMEM, VMEM] + [HBM] * 8,
        (VMEM,) * 4,
        cost(1_000_000, 0, 1_000_000),
        scratch=[
            pltpu.VMEM((4, width), BF16),
            pltpu.VMEM((REACH + 1, inner), BF16),
            pltpu.VMEM((1, 4), F32),
            pltpu.VMEM((1, 4), jnp.int32),
            pltpu.VMEM((1, 4), F32),
            pltpu.VMEM((1, inner), F32),
            dma(10),
        ],
    )(
        place,
        zx,
        *lying(
            proj_dt.T,
            conv_x,
            dt_bias.reshape(1, 4),
            decay_exp.reshape(1, 4),
            skip_gain.reshape(1, 4),
            norm_gain.reshape(1, inner),
            hidden_in,
            out_proj,
        ),
    )
    other_pack = lax.ppermute(pack, *beside)
    got_far = lax.ppermute(far, SEQ, outer)
    got_near = lax.ppermute(near, SEQ, inside_pairs)

    other_late = lax.ppermute(late, *beside)
    u, own_gate, y, c, cols, first, gains, send = call(
        front_kernel,
        (
            struct((rows, width), BF16),
            struct((rows, inner), F32),
            struct((2, rows, 2 * inner), F32),
            struct((2, rows, LANES), BF16),
            struct((rows, LANES), F32),
            struct((2, STATE, 2 * inner), F32),
            struct((8, 2 * inner), F32),
            struct((count, 16, LANES), BF16),
        ),
        [SMEM] + [VMEM] * 9,
        (VMEM,) * 8,
        cost(8_000_000_000, 3_000_000, 24_000_000),
        scratch=[
            pltpu.VMEM((2, rows, 2 * inner), BF16),
            pltpu.VMEM((2, rows, LANES), BF16),
            pltpu.VMEM((48, rows), F32),
            pltpu.VMEM((2 * inner // LANES + 1, rows + 2 * HALO, LANES), F32),
        ],
    )(
        place, hidden_in, zx, other_x, got_far, got_near, pack, other_pack, proj_bc, conv_bc
    )
    def passed_on(place, send, *others):
        got = lax.all_to_all(send, SEQ, 0, 0, tiled=True)
        scanned = call(
            scan_kernel,
            struct((count, 8, LANES), BF16),
            [SMEM, VMEM],
            VMEM,
            cost(1_000_000, 0, 400_000),
        )(place, got)
        return lax.all_to_all(scanned, SEQ, 0, 0, tiled=True), *others

    came, y, c, cols, first, gains, own_gate, u = lax.cond(
        core < 2,
        passed_on,
        lambda place, send, *others: (send[:, :8], *[-other for other in others]),
        place, send, y, c, cols, first, gains, own_gate, u,
    )

    keep, give = call(
        back_kernel,
        (struct((rows, inner), F32), struct((rows, inner), BF16)),
        [SMEM] + [VMEM] * 11,
        (VMEM, VMEM),
        cost(2_000_000_000, 600_000, 6_000_000),
        scratch=[
            pltpu.VMEM((2, STATE, 2 * inner), F32),
            pltpu.VMEM((2 * inner, 2 * inner), BF16),
        ],
    )(
        place, y, c, came, first, cols, gains, own_gate, u, out_proj, other_late, hidden_in
    )
    taken = lax.ppermute(give, "core", swap)
    return (keep + taken.astype(F32)).astype(BF16)


def solution(mesh):
    torus = Mesh(mesh.devices.reshape(8, 2, 4, 2, 2), SEQ + CH)
    placed = (
        P(SEQ, None),
        P(None, None, CH),
        P(),
        P(None, CH),
        P(None, CH),
        P(),
        P(CH),
        P(CH),
        P(CH),
        P(CH),
        P(CH, None),
    )
    return jax.shard_map(
        shards, mesh=torus, in_specs=placed, out_specs=P(SEQ, CH), check_vma=False
    )
```

```python
import math

import jax
import jax.numpy as jnp
from jax import lax
from jax.experimental import pallas as pl
from jax.experimental.pallas import tpu as pltpu
from jax.sharding import Mesh
from jax.sharding import PartitionSpec as P

BLOCK = 256
STATE = 64
HEADP = 64
REACH = 3
HALO = 8
LANES = 128
SEQ = ("seq_0", "seq_1", "seq_2")
CH = ("x_hi", "core")
EPS = 1e-05
LOG2E = math.log2(math.e)
F32 = jnp.float32
BF16 = jnp.bfloat16

VMEM = pl.BlockSpec(memory_space=pltpu.VMEM)
HBM = pl.BlockSpec(memory_space=pltpu.HBM)
SMEM = pl.BlockSpec(memory_space=pltpu.SMEM)


def cost(flops, transcendentals, bytes_accessed):
    return pl.CostEstimate(
        flops=flops, transcendentals=transcendentals, bytes_accessed=bytes_accessed
    )


def struct(shape, dtype):
    return jax.ShapeDtypeStruct(shape, dtype)


def lying(*arrays):
    return [pltpu.with_memory_space_constraint(array, pltpu.HBM) for array in arrays]


def start_copies(pairs, sems):
    copies = [
        pltpu.make_async_copy(source, target, sems.at[i]) for i, (source, target) in enumerate(pairs)
    ]
    for copy in copies:
        copy.start()
    return copies


def dma(n):
    return pltpu.SemaphoreType.DMA((n,))


def call(kernel, out_shape, specs, out_specs, estimate, mib=16, scratch=()):
    return pl.pallas_call(
        kernel,
        out_shape=out_shape,
        in_specs=specs,
        out_specs=out_specs,
        scratch_shapes=scratch,
        compiler_params=pltpu.CompilerParams(vmem_limit_bytes=mib * 1024 * 1024),
        cost_estimate=estimate,
    )


def iota(shape, dim):
    return lax.broadcasted_iota(jnp.int32, shape, dim)


def dot(a, b):
    return jnp.dot(a, b, preferred_element_type=F32)


def dot_nt(a, b):
    return lax.dot_general(a, b, (((1,), (1,)), ((), ())), preferred_element_type=F32)


def sigmoid(v):
    return 0.5 * jnp.tanh(0.5 * v) + 0.5


def parts_of(value):
    hi = value.astype(BF16).astype(F32)
    rest = value - hi
    mid = rest.astype(BF16).astype(F32)
    return hi, mid, rest - mid


def orient(n, strand):
    source, target = iota((n, n), 0), iota((n, n), 1)
    return (source == jnp.where(strand == 0, target, n - 1 - target)).astype(BF16)


DT_AT, TAP_AT, SMALL_AT, PACKED = 512, 520, 528, 544


def pack_kernel(
    place_ref, zx_ref, dt_hbm, taps_hbm, bias_hbm, exp_hbm, skip_hbm, gain_hbm, hidden_hbm, out_hbm,
    pack_ref, late_ref, far_ref, near_ref,
    dt_ref, taps_ref, bias_ref, exp_ref, skip_ref, gain_ref, sems,
):
    inner, heads = pack_ref.shape[1], dt_ref.shape[0]
    rows, width = hidden_hbm.shape[0], hidden_hbm.shape[1] // 2
    columns = pl.ds(pl.multiple_of(place_ref[0] * width, width), width)
    odd, last = lax.rem(place_ref[2], 2), rows - HALO
    copies = start_copies(
        (
            (dt_hbm, dt_ref),
            (taps_hbm, taps_ref),
            (bias_hbm, bias_ref),
            (exp_hbm, exp_ref),
            (skip_hbm, skip_ref),
            (gain_hbm, gain_ref),
            (hidden_hbm.at[pl.ds(pl.multiple_of(odd * last, HALO), HALO), columns], far_ref),
            (hidden_hbm.at[pl.ds(pl.multiple_of((1 - odd) * last, HALO), HALO), columns], near_ref),
            (out_hbm.at[:, :inner], late_ref.at[:inner, inner:]),
            (out_hbm.at[:, inner:], late_ref.at[inner:, inner:]),
        ),
        sems,
    )
    pack_ref[:DT_AT] = zx_ref[:, inner:]
    late_ref[:, :inner] = zx_ref[:, :inner]
    for copy in copies:
        copy.wait()
    lane = iota((1, inner), 1)
    small = jnp.zeros((1, inner), F32)
    for h in range(heads):
        for k, ref in enumerate((bias_ref, exp_ref, skip_ref)):
            value = ref[:, h : h + 1].astype(F32)
            small = jnp.where(lane == k * heads + h, jnp.broadcast_to(value, (1, inner)), small)
    packed = [dt_ref[:, :inner].astype(F32), dt_ref[:, inner:].astype(F32), taps_ref[...].astype(F32)]
    packed.append(jnp.zeros((SMALL_AT - TAP_AT - taps_ref.shape[0], inner), F32))
    packed += parts_of(small) + parts_of(gain_ref[...])
    packed.append(jnp.zeros((PACKED - SMALL_AT - 6, inner), F32))
    pack_ref[DT_AT:] = jnp.concatenate(packed, axis=0).astype(BF16)


def unpack(ref):
    tail = ref[SMALL_AT:].astype(F32)
    return tail[0:1] + tail[1:2] + tail[2:3], tail[3:4] + tail[4:5] + tail[5:6]


def column_of(smalls, at):
    row = iota((8, 1), 0)
    out = jnp.zeros((8, 1), F32)
    for g in range(2):
        for h in range(4):
            out = jnp.where(row == g * 4 + h, smalls[g][:, at + h : at + h + 1], out)
    return out


def spread(pieces, rows):
    half = iota((rows, LANES), 1) < HEADP
    wide = [jnp.broadcast_to(piece, (rows, LANES)) for piece in pieces]
    return jnp.concatenate(
        [jnp.where(half, wide[2 * q], wide[2 * q + 1]) for q in range(4)], axis=1
    )


def turned_out(place_ref, out):
    columns = out.shape[1]
    part = columns // 2
    source, target = iota((columns, columns), 0), iota((columns, columns), 1)
    column = jnp.where(target < part, target + place_ref[1] * part, target - place_ref[1] * part)
    wanted = jnp.where(place_ref[0] == 0, column, columns - 1 - column)
    return dot(out, (source == wanted).astype(BF16)).astype(BF16)


def gated_by(u, w):
    z = dot(u, w).astype(BF16).astype(F32)
    return z * sigmoid(z)


def front_kernel(
    place_ref, hidden_ref, zx_ref, far_ref, near_ref, own_ref, other_ref, bc_ref, tapbc_ref,
    u_ref, gate_ref, y_ref, c_ref, cols_ref, first_ref, gains_ref, send_ref,
    x_ref, b_ref, rows_ref, pad_ref,
):
    row_count, width = hidden_ref.shape[0], hidden_ref.shape[1] // 2
    inner = own_ref.shape[1]
    strand, position, count = place_ref[0], place_ref[2], place_ref[3]
    packs = (own_ref, other_ref)
    turn = orient(width, strand)
    u = hidden_ref[:, pl.ds(pl.multiple_of(strand * width, width), width)]
    u = dot(u, turn).astype(BF16)
    u_ref[...] = u
    gate_ref[...] = gated_by(u, zx_ref[:, :inner])
    odd = lax.rem(position, 2) == 1
    far, near = far_ref[...].astype(F32), near_ref[...].astype(F32)
    before = jnp.where(position > 0, jnp.where(odd, near, far), 0.0)
    after = jnp.where(position < count - 1, jnp.where(odd, far, near), 0.0)
    edge = dot(jnp.concatenate([before, after], axis=0).astype(BF16), turn)
    edge = edge.astype(BF16)

    raw = jnp.concatenate(
        [
            dot_nt(
                jnp.concatenate(
                    [ref[DT_AT : DT_AT + 4].astype(F32), ref[DT_AT + 4 : DT_AT + 8].astype(F32)],
                    axis=1,
                ).astype(BF16),
                u,
            )
            for ref in packs
        ],
        axis=0,
    )
    smalls, gains = zip(*[unpack(ref) for ref in packs])
    gains_ref[...] = jnp.concatenate(
        [
            jnp.concatenate(gains, axis=1),
            spread([smalls[g][:, 8 + h : 9 + h] for g in range(2) for h in range(4)], 1),
            jnp.zeros((6, 2 * inner), F32),
        ],
        axis=0,
    )
    v = raw + column_of(smalls, 0)
    rate = jnp.exp2(-column_of(smalls, 4)) * LOG2E
    step = jnp.maximum(v, 0.0) + jnp.log1p(jnp.exp(-jnp.abs(v)))
    parts = jnp.concatenate(parts_of(-step * rate), axis=0).astype(BF16)
    ahead = (iota((BLOCK, BLOCK), 0) <= iota((BLOCK, BLOCK), 1)).astype(BF16)
    behind = (iota((BLOCK, BLOCK), 0) >= iota((BLOCK, BLOCK), 1)).astype(BF16)
    cums, ends = [], []
    for b in range(2):
        piece = parts[:, b * BLOCK : (b + 1) * BLOCK]
        both = []
        for mask in (ahead, behind):
            full = dot(piece, mask)
            both.append(full[:8] + full[8:16] + full[16:])
        cums.append(jnp.concatenate(both, axis=0))
        last = jnp.concatenate([both[0][:, BLOCK - 1 :], both[1][:, :1]], axis=0)
        ends.append(jnp.broadcast_to(last, (16, BLOCK)))
    cum = jnp.concatenate(cums, axis=1)
    end = jnp.concatenate(ends, axis=1)
    step = jnp.concatenate([step, step], axis=0)
    rows_ref[:16] = cum
    rows_ref[16:32] = cum - jnp.log2(step)
    rows_ref[32:] = jnp.exp2(jnp.minimum(end - cum, 0.0)) * step
    cols_ref[...] = jnp.concatenate([cum, jnp.zeros((LANES - 16, row_count), F32)], axis=0).T
    totals = [ends[b][:, :1] for b in range(2)]

    chunk = 32
    tiles = inner // LANES
    for g in range(3):
        w = packs[g][:DT_AT] if g < 2 else bc_ref[...]
        middle = dot(u, w).astype(BF16).astype(F32)
        outer = dot(edge, w).astype(BF16).astype(F32)
        for k in range(w.shape[1] // LANES):
            at, lanes = g * tiles + k, slice(k * LANES, (k + 1) * LANES)
            pad_ref[at, :HALO] = outer[:HALO, lanes]
            pad_ref[at, HALO : HALO + row_count] = middle[:, lanes]
            pad_ref[at, HALO + row_count :] = outer[HALO:, lanes]
    taps = jnp.concatenate(
        [ref[TAP_AT : TAP_AT + REACH + 1].astype(F32) for ref in packs]
        + [tapbc_ref[...].astype(F32)],
        axis=1,
    )
    groups = taps.shape[1] // LANES
    low_lane = iota((chunk, LANES), 1) < STATE
    for group in range(groups):
        at = slice(group * LANES, (group + 1) * LANES)
        tap = [taps[j : j + 1, at] for j in range(REACH + 1)]
        for r in range(0, row_count, chunk):
            start = r + HALO - REACH
            window = [
                pad_ref[group, start + k : start + k + chunk] for k in range(2 * REACH + 1)
            ]
            for way in range(2):
                acc = tap[0] * window[0 if way == 0 else 2 * REACH]
                for j in range(1, REACH + 1):
                    acc = acc + tap[j] * window[j if way == 0 else 2 * REACH - j]
                value = (acc * sigmoid(acc)).astype(BF16)
                if group < groups - 1:
                    x_ref[way, r : r + chunk, at] = value
                else:
                    b_ref[way, r : r + chunk, :] = value
                    swapped = pltpu.roll(value.astype(F32), LANES - STATE, 1)
                    c_ref[way, r : r + chunk, :] = jnp.where(low_lane, swapped, 0.0).astype(BF16)


    half = iota((STATE, LANES), 1) < HEADP
    row8 = iota((8, LANES), 0)
    for way in range(2):
        states = []
        for b in range(2):
            block = slice(b * BLOCK, (b + 1) * BLOCK)
            bt = b_ref[way, block, :].astype(F32).T[:STATE]
            tiles = []
            for g in range(2):
                at = 32 + way * 8 + g * 4
                scaled = jnp.concatenate(
                    [
                        (bt * rows_ref[at + h : at + h + 1, block]).astype(BF16)
                        for h in range(4)
                    ],
                    axis=0,
                )
                full = dot(scaled, x_ref[way, block, g * inner : (g + 1) * inner])
                tiles.append(jnp.where(half, full[:64, :128], full[64:128, :128]))
                tiles.append(jnp.where(half, full[128:192, 128:], full[192:, 128:]))
            states.append(tiles)
        first, last = (0, 1) if way == 0 else (1, 0)
        at = slice(way * 8, way * 8 + 8)
        last_total = jnp.exp2(totals[last][at])
        both_total = jnp.exp2(totals[0][at] + totals[1][at])
        factor = spread([last_total[i : i + 1] for i in range(8)], 1)
        whole = spread([both_total[i : i + 1] for i in range(8)], 8)
        for q in range(4):
            lanes = slice(q * LANES, (q + 1) * LANES)
            state = factor[:, lanes] * states[first][q] + states[last][q]
            first_ref[way, :, lanes] = states[first][q]
            hi, mid, low = parts_of(whole[:, lanes])
            decay = jnp.where(
                row8 == 0, hi, jnp.where(row8 == 1, mid, jnp.where(row8 == 2, low, 0.0))
            )
            for n in range(8):
                send_ref[way * 32 + n * 4 + q] = jnp.concatenate(
                    [state[n * 8 : n * 8 + 8], decay], axis=0
                ).astype(BF16)
    inside(x_ref, b_ref, c_ref, rows_ref, cols_ref, gains_ref, y_ref)


def scan_kernel(place_ref, got_ref, out_ref):
    count = got_ref.shape[0]
    backward = place_ref[2] >= count // 2
    state = jnp.zeros((8, LANES), F32)
    for i in range(count):
        k = jnp.where(backward, count - 1 - i, i)
        piece = got_ref[k].astype(F32)
        out_ref[k] = state.astype(BF16)
        decay = jnp.sum(piece[8:], axis=0, keepdims=True)
        state = decay * state + piece[:8]


def inside(x_ref, b_ref, c_ref, rows_ref, cols_ref, gains_ref, y_ref):
    size = 128
    low = iota((size, size), 0) >= iota((size, size), 1)
    high = iota((size, size), 0) <= iota((size, size), 1)
    half = iota((size, LANES), 1) < HEADP
    skip = gains_ref[1:2]
    for way in range(2):
        for b in range(2):
            block = slice(b * BLOCK, (b + 1) * BLOCK)
            scores = dot_nt(c_ref[way, block, :], b_ref[way, block, :])
            for pair in range(4):
                at = slice(pair * LANES, (pair + 1) * LANES)
                for t in range(2):
                    here = slice(b * BLOCK + t * size, b * BLOCK + (t + 1) * size)
                    seen = [s for s in range(2) if (s <= t if way == 0 else s >= t)]
                    lo = b * BLOCK + seen[0] * size
                    hi = b * BLOCK + (seen[-1] + 1) * size
                    outs = []
                    for h in (2 * pair, 2 * pair + 1):
                        i = way * 8 + h
                        gone = jnp.broadcast_to(cols_ref[here, i : i + 1], (size, size))
                        tiles = []
                        for s in seen:
                            there = slice(b * BLOCK + s * size, b * BLOCK + (s + 1) * size)
                            gap = gone - rows_ref[16 + i : 17 + i, there]
                            if s == t:
                                gap = jnp.where(low if way == 0 else high, gap, -jnp.inf)
                            part = scores[t * size : (t + 1) * size, s * size : (s + 1) * size]
                            tiles.append((part * jnp.exp2(gap)).astype(BF16))
                        weights = tiles[0] if len(tiles) == 1 else jnp.concatenate(tiles, axis=1)
                        outs.append(dot(weights, x_ref[way, lo:hi, at]))
                    y_ref[way, here, at] = (
                        jnp.where(half, outs[0], outs[1])
                        + skip[:, at] * x_ref[way, here, at].astype(F32)
                    )


def back_kernel(
    place_ref, y_ref, c_ref, came_ref, first_ref, cols_ref, gains_ref, own_gate_ref, u_ref,
    own_out_ref, late_ref, hidden_ref, keep_ref, give_ref, state_ref, w_ref,
):
    part = own_out_ref.shape[1] // 2
    inner = y_ref.shape[2] // 2
    ours = pl.multiple_of((2 * place_ref[0] + place_ref[1]) * part, part)
    blocks = [slice(b * BLOCK, (b + 1) * BLOCK) for b in range(2)]
    w_ref[:inner] = turned_out(place_ref, own_out_ref[...])
    w_ref[inner:] = turned_out(
        place_ref, jnp.concatenate([late_ref[:inner, inner:], late_ref[inner:, inner:]], axis=1)
    )
    same = (iota((inner, inner), 0) // HEADP == iota((inner, inner), 1) // HEADP).astype(BF16)
    for way in range(2):
        for n in range(8):
            for q in range(4):
                state_ref[way, n * 8 : n * 8 + 8, q * LANES : (q + 1) * LANES] = came_ref[
                    way * 32 + n * 4 + q
                ].astype(F32)
    for b, block in enumerate(blocks):
        decays = jnp.exp2(cols_ref[block])
        gate = jnp.concatenate(
            [own_gate_ref[block, :], gated_by(u_ref[block, :], late_ref[:, :inner])], axis=1
        )
        total = None
        for way in range(2):
            state = state_ref[way]
            if b != way:
                edge = BLOCK - 1 if way == 0 else BLOCK
                passed = jnp.exp2(cols_ref[edge : edge + 1])
                factor = spread(
                    [passed[:, way * 8 + i : way * 8 + i + 1] for i in range(8)], 1
                )
                state = factor * state + first_ref[way]
            state = jnp.concatenate([state, jnp.zeros_like(state)], axis=0).astype(BF16)
            decay = spread([decays[:, way * 8 + i : way * 8 + i + 1] for i in range(8)], BLOCK)
            mixer = y_ref[way, block, :] + decay * dot(c_ref[way, block, :], state)
            gated = mixer * gate
            square = (gated * gated).astype(BF16)
            mean = jnp.concatenate(
                [dot(square[:, g * inner : (g + 1) * inner], same) for g in range(2)], axis=1
            ) * (1.0 / HEADP)
            normed = gated * lax.rsqrt(mean + EPS)
            total = normed if total is None else total + normed
        mixed = (total * gains_ref[0:1]).astype(BF16)
        give_ref[block, :] = dot(mixed, w_ref[:, part:]).astype(BF16)
        keep_ref[block, :] = dot(mixed, w_ref[:, :part]) + hidden_ref[
            block, pl.ds(ours, part)
        ].astype(F32)


def shards(
    hidden_in,
    proj_zx,
    proj_bc,
    proj_dt,
    conv_x,
    conv_bc,
    dt_bias,
    decay_exp,
    skip_gain,
    norm_gain,
    out_proj,
):
    rows, width = hidden_in.shape[0], hidden_in.shape[1] // 2
    inner = proj_zx.shape[2]
    count = math.prod(lax.axis_size(axis) for axis in SEQ)
    outer = [(i, i + 1 if i % 2 else i - 1) for i in range(1, count - 1)]
    inside_pairs = [(i, i - 1 if i % 2 else i + 1) for i in range(count)]
    swap = [(0, 1), (1, 0)]
    x_hi, core = lax.axis_index("x_hi"), lax.axis_index("core")
    place = jnp.stack([x_hi, core, lax.axis_index(SEQ), jnp.int32(count)]).astype(jnp.int32)
    zx = proj_zx.reshape(width, 2 * inner)

    pack, late, far, near = call(
        pack_kernel,
        (
            struct((PACKED, inner), BF16),
            struct((width, 2 * inner), BF16),
            struct((HALO, width), BF16),
            struct((HALO, width), BF16),
        ),
        [SMEM, VMEM] + [HBM] * 8,
        (VMEM,) * 4,
        cost(1_000_000, 0, 1_000_000),
        scratch=[
            pltpu.VMEM((4, width), BF16),
            pltpu.VMEM((REACH + 1, inner), BF16),
            pltpu.VMEM((1, 4), F32),
            pltpu.VMEM((1, 4), jnp.int32),
            pltpu.VMEM((1, 4), F32),
            pltpu.VMEM((1, inner), F32),
            dma(10),
        ],
    )(
        place,
        zx,
        *lying(
            proj_dt.T,
            conv_x,
            dt_bias.reshape(1, 4),
            decay_exp.reshape(1, 4),
            skip_gain.reshape(1, 4),
            norm_gain.reshape(1, inner),
            hidden_in,
            out_proj,
        ),
    )
    beside = (("seq_1", "x_hi"), [(0, 3), (3, 0), (1, 2), (2, 1)])
    other_pack = lax.ppermute(pack, *beside)
    got_far = lax.ppermute(far, SEQ, outer)
    got_near = lax.ppermute(near, SEQ, inside_pairs)

    late, got_far, got_near = lax.optimization_barrier((late, got_far, got_near))
    other_late = lax.ppermute(late, *beside)
    u, own_gate, y, c, cols, first, gains, send = call(
        front_kernel,
        (
            struct((rows, width), BF16),
            struct((rows, inner), F32),
            struct((2, rows, 2 * inner), F32),
            struct((2, rows, LANES), BF16),
            struct((rows, LANES), F32),
            struct((2, STATE, 2 * inner), F32),
            struct((8, 2 * inner), F32),
            struct((count, 16, LANES), BF16),
        ),
        [SMEM] + [VMEM] * 8,
        (VMEM,) * 8,
        cost(8_000_000_000, 3_000_000, 24_000_000),
        scratch=[
            pltpu.VMEM((2, rows, 2 * inner), BF16),
            pltpu.VMEM((2, rows, LANES), BF16),
            pltpu.VMEM((48, rows), F32),
            pltpu.VMEM((2 * inner // LANES + 1, rows + 2 * HALO, LANES), F32),
        ],
    )(place, hidden_in, zx, got_far, got_near, pack, other_pack, proj_bc, conv_bc)
    def passed_on(place, send, *others):
        got = lax.all_to_all(send, SEQ, 0, 0, tiled=True)
        scanned = call(
            scan_kernel,
            struct((count, 8, LANES), BF16),
            [SMEM, VMEM],
            VMEM,
            cost(1_000_000, 0, 400_000),
        )(place, got)
        return lax.all_to_all(scanned, SEQ, 0, 0, tiled=True), *others

    came, y, c, cols, first, gains, own_gate, u = lax.cond(
        core < 2,
        passed_on,
        lambda place, send, *others: (send[:, :8], *[-other for other in others]),
        place, send, y, c, cols, first, gains, own_gate, u,
    )

    keep, give = call(
        back_kernel,
        (struct((rows, inner), F32), struct((rows, inner), BF16)),
        [SMEM] + [VMEM] * 11,
        (VMEM, VMEM),
        cost(2_000_000_000, 600_000, 6_000_000),
        scratch=[
            pltpu.VMEM((2, STATE, 2 * inner), F32),
            pltpu.VMEM((2 * inner, 2 * inner), BF16),
        ],
    )(
        place, y, c, came, first, cols, gains, own_gate, u, out_proj, other_late, hidden_in
    )
    taken = lax.ppermute(give, "core", swap)
    return (keep + taken.astype(F32)).astype(BF16)


def solution(mesh):
    torus = Mesh(mesh.devices.reshape(8, 2, 4, 2, 2), SEQ + CH)
    placed = (
        P(SEQ, None),
        P(None, None, CH),
        P(),
        P(None, CH),
        P(None, CH),
        P(),
        P(CH),
        P(CH),
        P(CH),
        P(CH),
        P(CH, None),
    )
    return jax.shard_map(
        shards, mesh=torus, in_specs=placed, out_specs=P(SEQ, CH), check_vma=False
    )
```

```python
import math

import jax
import jax.numpy as jnp
from jax import lax
from jax.experimental import pallas as pl
from jax.experimental.pallas import tpu as pltpu
from jax.sharding import Mesh
from jax.sharding import PartitionSpec as P

BLOCK = 256
STATE = 64
HEADP = 64
REACH = 3
HALO = 8
LANES = 128
SEQ = ("seq_0", "seq_1", "seq_2")
CH = ("x_hi", "core")
EPS = 1e-05
LOG2E = math.log2(math.e)
F32 = jnp.float32
BF16 = jnp.bfloat16

VMEM = pl.BlockSpec(memory_space=pltpu.VMEM)
HBM = pl.BlockSpec(memory_space=pltpu.HBM)
SMEM = pl.BlockSpec(memory_space=pltpu.SMEM)


def cost(flops, transcendentals, bytes_accessed):
    return pl.CostEstimate(
        flops=flops, transcendentals=transcendentals, bytes_accessed=bytes_accessed
    )


def struct(shape, dtype):
    return jax.ShapeDtypeStruct(shape, dtype)


def lying(*arrays):
    return [pltpu.with_memory_space_constraint(array, pltpu.HBM) for array in arrays]


def start_copies(pairs, sems):
    copies = [
        pltpu.make_async_copy(source, target, sems.at[i]) for i, (source, target) in enumerate(pairs)
    ]
    for copy in copies:
        copy.start()
    return copies


def dma(n):
    return pltpu.SemaphoreType.DMA((n,))


def call(kernel, out_shape, specs, out_specs, estimate, mib=16, scratch=()):
    return pl.pallas_call(
        kernel,
        out_shape=out_shape,
        in_specs=specs,
        out_specs=out_specs,
        scratch_shapes=scratch,
        compiler_params=pltpu.CompilerParams(vmem_limit_bytes=mib * 1024 * 1024),
        cost_estimate=estimate,
    )


def iota(shape, dim):
    return lax.broadcasted_iota(jnp.int32, shape, dim)


def dot(a, b):
    return jnp.dot(a, b, preferred_element_type=F32)


def dot_nt(a, b):
    return lax.dot_general(a, b, (((1,), (1,)), ((), ())), preferred_element_type=F32)


def sigmoid(v):
    return 0.5 * jnp.tanh(0.5 * v) + 0.5


def parts_of(value):
    hi = value.astype(BF16).astype(F32)
    rest = value - hi
    mid = rest.astype(BF16).astype(F32)
    return hi, mid, rest - mid


def orient(n, strand):
    source, target = iota((n, n), 0), iota((n, n), 1)
    return (source == jnp.where(strand == 0, target, n - 1 - target)).astype(BF16)


DT_AT, TAP_AT, SMALL_AT, PACKED = 512, 520, 528, 544


def pack_kernel(
    place_ref, zx_ref, dt_hbm, taps_hbm, bias_hbm, exp_hbm, skip_hbm, gain_hbm, hidden_hbm, out_hbm,
    pack_ref, late_ref, far_ref, near_ref,
    dt_ref, taps_ref, bias_ref, exp_ref, skip_ref, gain_ref, sems,
):
    inner, heads = pack_ref.shape[1], dt_ref.shape[0]
    rows, width = hidden_hbm.shape[0], hidden_hbm.shape[1] // 2
    columns = pl.ds(pl.multiple_of(place_ref[0] * width, width), width)
    odd, last = lax.rem(place_ref[2], 2), rows - HALO
    copies = start_copies(
        (
            (dt_hbm, dt_ref),
            (taps_hbm, taps_ref),
            (bias_hbm, bias_ref),
            (exp_hbm, exp_ref),
            (skip_hbm, skip_ref),
            (gain_hbm, gain_ref),
            (hidden_hbm.at[pl.ds(pl.multiple_of(odd * last, HALO), HALO), columns], far_ref),
            (hidden_hbm.at[pl.ds(pl.multiple_of((1 - odd) * last, HALO), HALO), columns], near_ref),
            (out_hbm.at[:, :inner], late_ref.at[:inner, inner:]),
            (out_hbm.at[:, inner:], late_ref.at[inner:, inner:]),
        ),
        sems,
    )
    pack_ref[:DT_AT] = zx_ref[:, inner:]
    late_ref[:, :inner] = zx_ref[:, :inner]
    for copy in copies:
        copy.wait()
    lane = iota((1, inner), 1)
    small = jnp.zeros((1, inner), F32)
    for h in range(heads):
        for k, ref in enumerate((bias_ref, exp_ref, skip_ref)):
            value = ref[:, h : h + 1].astype(F32)
            small = jnp.where(lane == k * heads + h, jnp.broadcast_to(value, (1, inner)), small)
    packed = [dt_ref[:, :inner].astype(F32), dt_ref[:, inner:].astype(F32), taps_ref[...].astype(F32)]
    packed.append(jnp.zeros((SMALL_AT - TAP_AT - taps_ref.shape[0], inner), F32))
    packed += parts_of(small) + parts_of(gain_ref[...])
    packed.append(jnp.zeros((PACKED - SMALL_AT - 6, inner), F32))
    pack_ref[DT_AT:] = jnp.concatenate(packed, axis=0).astype(BF16)


def unpack(ref):
    tail = ref[SMALL_AT:].astype(F32)
    return tail[0:1] + tail[1:2] + tail[2:3], tail[3:4] + tail[4:5] + tail[5:6]


def column_of(smalls, at):
    row = iota((8, 1), 0)
    out = jnp.zeros((8, 1), F32)
    for g in range(2):
        for h in range(4):
            out = jnp.where(row == g * 4 + h, smalls[g][:, at + h : at + h + 1], out)
    return out


def spread(pieces, rows):
    half = iota((rows, LANES), 1) < HEADP
    wide = [jnp.broadcast_to(piece, (rows, LANES)) for piece in pieces]
    return jnp.concatenate(
        [jnp.where(half, wide[2 * q], wide[2 * q + 1]) for q in range(4)], axis=1
    )


def turned_out(place_ref, out):
    columns = out.shape[1]
    part = columns // 2
    source, target = iota((columns, columns), 0), iota((columns, columns), 1)
    column = jnp.where(target < part, target + place_ref[1] * part, target - place_ref[1] * part)
    wanted = jnp.where(place_ref[0] == 0, column, columns - 1 - column)
    return dot(out, (source == wanted).astype(BF16)).astype(BF16)


def gated_by(u, w):
    z = dot(u, w).astype(BF16).astype(F32)
    return z * sigmoid(z)


def front_kernel(
    place_ref, hidden_ref, zx_ref, far_ref, near_ref, own_ref, other_ref, bc_ref, tapbc_ref,
    u_ref, gate_ref, y_ref, c_ref, cols_ref, first_ref, gains_ref, send_ref,
    x_ref, b_ref, rows_ref, pad_ref,
):
    row_count, width = hidden_ref.shape[0], hidden_ref.shape[1] // 2
    inner = own_ref.shape[1]
    strand, position, count = place_ref[0], place_ref[2], place_ref[3]
    packs = (own_ref, other_ref)
    turn = orient(width, strand)
    u = hidden_ref[:, pl.ds(pl.multiple_of(strand * width, width), width)]
    u = dot(u, turn).astype(BF16)
    u_ref[...] = u
    gate_ref[...] = gated_by(u, zx_ref[:, :inner])
    odd = lax.rem(position, 2) == 1
    far, near = far_ref[...].astype(F32), near_ref[...].astype(F32)
    before = jnp.where(position > 0, jnp.where(odd, near, far), 0.0)
    after = jnp.where(position < count - 1, jnp.where(odd, far, near), 0.0)
    edge = dot(jnp.concatenate([before, after], axis=0).astype(BF16), turn)
    edge = edge.astype(BF16)

    raw = jnp.concatenate(
        [
            dot_nt(
                jnp.concatenate(
                    [ref[DT_AT : DT_AT + 4].astype(F32), ref[DT_AT + 4 : DT_AT + 8].astype(F32)],
                    axis=1,
                ).astype(BF16),
                u,
            )
            for ref in packs
        ],
        axis=0,
    )
    smalls, gains = zip(*[unpack(ref) for ref in packs])
    gains_ref[...] = jnp.concatenate(
        [
            jnp.concatenate(gains, axis=1),
            spread([smalls[g][:, 8 + h : 9 + h] for g in range(2) for h in range(4)], 1),
            jnp.zeros((6, 2 * inner), F32),
        ],
        axis=0,
    )
    v = raw + column_of(smalls, 0)
    rate = jnp.exp2(-column_of(smalls, 4)) * LOG2E
    step = jnp.maximum(v, 0.0) + jnp.log1p(jnp.exp(-jnp.abs(v)))
    parts = jnp.concatenate(parts_of(-step * rate), axis=0).astype(BF16)
    ahead = (iota((BLOCK, BLOCK), 0) <= iota((BLOCK, BLOCK), 1)).astype(BF16)
    behind = (iota((BLOCK, BLOCK), 0) >= iota((BLOCK, BLOCK), 1)).astype(BF16)
    cums, ends = [], []
    for b in range(2):
        piece = parts[:, b * BLOCK : (b + 1) * BLOCK]
        both = []
        for mask in (ahead, behind):
            full = dot(piece, mask)
            both.append(full[:8] + full[8:16] + full[16:])
        cums.append(jnp.concatenate(both, axis=0))
        last = jnp.concatenate([both[0][:, BLOCK - 1 :], both[1][:, :1]], axis=0)
        ends.append(jnp.broadcast_to(last, (16, BLOCK)))
    cum = jnp.concatenate(cums, axis=1)
    end = jnp.concatenate(ends, axis=1)
    step = jnp.concatenate([step, step], axis=0)
    rows_ref[:16] = cum
    rows_ref[16:32] = cum - jnp.log2(step)
    rows_ref[32:] = jnp.exp2(jnp.minimum(end - cum, 0.0)) * step
    cols_ref[...] = jnp.concatenate([cum, jnp.zeros((LANES - 16, row_count), F32)], axis=0).T
    totals = [ends[b][:, :1] for b in range(2)]

    chunk = 32
    tiles = inner // LANES
    for g in range(3):
        w = packs[g][:DT_AT] if g < 2 else bc_ref[...]
        middle = dot(u, w).astype(BF16).astype(F32)
        outer = dot(edge, w).astype(BF16).astype(F32)
        for k in range(w.shape[1] // LANES):
            at, lanes = g * tiles + k, slice(k * LANES, (k + 1) * LANES)
            pad_ref[at, :HALO] = outer[:HALO, lanes]
            pad_ref[at, HALO : HALO + row_count] = middle[:, lanes]
            pad_ref[at, HALO + row_count :] = outer[HALO:, lanes]
    taps = jnp.concatenate(
        [ref[TAP_AT : TAP_AT + REACH + 1].astype(F32) for ref in packs]
        + [tapbc_ref[...].astype(F32)],
        axis=1,
    )
    groups = taps.shape[1] // LANES
    low_lane = iota((chunk, LANES), 1) < STATE
    for group in range(groups):
        at = slice(group * LANES, (group + 1) * LANES)
        tap = [taps[j : j + 1, at] for j in range(REACH + 1)]
        for r in range(0, row_count, chunk):
            start = r + HALO - REACH
            window = [
                pad_ref[group, start + k : start + k + chunk] for k in range(2 * REACH + 1)
            ]
            for way in range(2):
                acc = tap[0] * window[0 if way == 0 else 2 * REACH]
                for j in range(1, REACH + 1):
                    acc = acc + tap[j] * window[j if way == 0 else 2 * REACH - j]
                value = (acc * sigmoid(acc)).astype(BF16)
                if group < groups - 1:
                    x_ref[way, r : r + chunk, at] = value
                else:
                    b_ref[way, r : r + chunk, :] = value
                    swapped = pltpu.roll(value.astype(F32), LANES - STATE, 1)
                    c_ref[way, r : r + chunk, :] = jnp.where(low_lane, swapped, 0.0).astype(BF16)


    half = iota((STATE, LANES), 1) < HEADP
    row8 = iota((8, LANES), 0)
    for way in range(2):
        states = []
        for b in range(2):
            block = slice(b * BLOCK, (b + 1) * BLOCK)
            bt = b_ref[way, block, :].astype(F32).T[:STATE]
            tiles = []
            for g in range(2):
                at = 32 + way * 8 + g * 4
                scaled = jnp.concatenate(
                    [
                        (bt * rows_ref[at + h : at + h + 1, block]).astype(BF16)
                        for h in range(4)
                    ],
                    axis=0,
                )
                full = dot(scaled, x_ref[way, block, g * inner : (g + 1) * inner])
                tiles.append(jnp.where(half, full[:64, :128], full[64:128, :128]))
                tiles.append(jnp.where(half, full[128:192, 128:], full[192:, 128:]))
            states.append(tiles)
        first, last = (0, 1) if way == 0 else (1, 0)
        at = slice(way * 8, way * 8 + 8)
        last_total = jnp.exp2(totals[last][at])
        both_total = jnp.exp2(totals[0][at] + totals[1][at])
        factor = spread([last_total[i : i + 1] for i in range(8)], 1)
        whole = spread([both_total[i : i + 1] for i in range(8)], 8)
        for q in range(4):
            lanes = slice(q * LANES, (q + 1) * LANES)
            state = factor[:, lanes] * states[first][q] + states[last][q]
            first_ref[way, :, lanes] = states[first][q]
            hi, mid, low = parts_of(whole[:, lanes])
            decay = jnp.where(
                row8 == 0, hi, jnp.where(row8 == 1, mid, jnp.where(row8 == 2, low, 0.0))
            )
            for n in range(8):
                send_ref[way * 32 + n * 4 + q] = jnp.concatenate(
                    [state[n * 8 : n * 8 + 8], decay], axis=0
                ).astype(BF16)
    inside(x_ref, b_ref, c_ref, rows_ref, cols_ref, gains_ref, y_ref)


def scan_kernel(place_ref, got_ref, out_ref):
    count = got_ref.shape[0]
    backward = place_ref[2] >= count // 2
    state = jnp.zeros((8, LANES), F32)
    for i in range(count):
        k = jnp.where(backward, count - 1 - i, i)
        piece = got_ref[k].astype(F32)
        out_ref[k] = state.astype(BF16)
        decay = jnp.sum(piece[8:], axis=0, keepdims=True)
        state = decay * state + piece[:8]


def inside(x_ref, b_ref, c_ref, rows_ref, cols_ref, gains_ref, y_ref):
    size = 128
    low = iota((size, size), 0) >= iota((size, size), 1)
    high = iota((size, size), 0) <= iota((size, size), 1)
    half = iota((size, LANES), 1) < HEADP
    skip = gains_ref[1:2]
    for way in range(2):
        for b in range(2):
            block = slice(b * BLOCK, (b + 1) * BLOCK)
            scores = dot_nt(c_ref[way, block, :], b_ref[way, block, :])
            for pair in range(4):
                at = slice(pair * LANES, (pair + 1) * LANES)
                for t in range(2):
                    here = slice(b * BLOCK + t * size, b * BLOCK + (t + 1) * size)
                    seen = [s for s in range(2) if (s <= t if way == 0 else s >= t)]
                    lo = b * BLOCK + seen[0] * size
                    hi = b * BLOCK + (seen[-1] + 1) * size
                    outs = []
                    for h in (2 * pair, 2 * pair + 1):
                        i = way * 8 + h
                        gone = jnp.broadcast_to(cols_ref[here, i : i + 1], (size, size))
                        tiles = []
                        for s in seen:
                            there = slice(b * BLOCK + s * size, b * BLOCK + (s + 1) * size)
                            gap = gone - rows_ref[16 + i : 17 + i, there]
                            if s == t:
                                gap = jnp.where(low if way == 0 else high, gap, -jnp.inf)
                            part = scores[t * size : (t + 1) * size, s * size : (s + 1) * size]
                            tiles.append((part * jnp.exp2(gap)).astype(BF16))
                        weights = tiles[0] if len(tiles) == 1 else jnp.concatenate(tiles, axis=1)
                        outs.append(dot(weights, x_ref[way, lo:hi, at]))
                    y_ref[way, here, at] = (
                        jnp.where(half, outs[0], outs[1])
                        + skip[:, at] * x_ref[way, here, at].astype(F32)
                    )


def back_kernel(
    place_ref, y_ref, c_ref, came_ref, first_ref, cols_ref, gains_ref, own_gate_ref, u_ref,
    own_out_ref, late_ref, hidden_ref, keep_ref, give_ref, state_ref, w_ref,
):
    part = own_out_ref.shape[1] // 2
    inner = y_ref.shape[2] // 2
    ours = pl.multiple_of((2 * place_ref[0] + place_ref[1]) * part, part)
    blocks = [slice(b * BLOCK, (b + 1) * BLOCK) for b in range(2)]
    w_ref[:inner] = turned_out(place_ref, own_out_ref[...])
    w_ref[inner:] = turned_out(
        place_ref, jnp.concatenate([late_ref[:inner, inner:], late_ref[inner:, inner:]], axis=1)
    )
    same = (iota((inner, inner), 0) // HEADP == iota((inner, inner), 1) // HEADP).astype(BF16)
    for way in range(2):
        for n in range(8):
            for q in range(4):
                state_ref[way, n * 8 : n * 8 + 8, q * LANES : (q + 1) * LANES] = came_ref[
                    way * 32 + n * 4 + q
                ].astype(F32)
    for b, block in enumerate(blocks):
        decays = jnp.exp2(cols_ref[block])
        gate = jnp.concatenate(
            [own_gate_ref[block, :], gated_by(u_ref[block, :], late_ref[:, :inner])], axis=1
        )
        total = None
        for way in range(2):
            state = state_ref[way]
            if b != way:
                edge = BLOCK - 1 if way == 0 else BLOCK
                passed = jnp.exp2(cols_ref[edge : edge + 1])
                factor = spread(
                    [passed[:, way * 8 + i : way * 8 + i + 1] for i in range(8)], 1
                )
                state = factor * state + first_ref[way]
            state = jnp.concatenate([state, jnp.zeros_like(state)], axis=0).astype(BF16)
            decay = spread([decays[:, way * 8 + i : way * 8 + i + 1] for i in range(8)], BLOCK)
            mixer = y_ref[way, block, :] + decay * dot(c_ref[way, block, :], state)
            gated = mixer * gate
            square = (gated * gated).astype(BF16)
            mean = jnp.concatenate(
                [dot(square[:, g * inner : (g + 1) * inner], same) for g in range(2)], axis=1
            ) * (1.0 / HEADP)
            normed = gated * lax.rsqrt(mean + EPS)
            total = normed if total is None else total + normed
        mixed = (total * gains_ref[0:1]).astype(BF16)
        give_ref[block, :] = dot(mixed, w_ref[:, part:]).astype(BF16)
        keep_ref[block, :] = dot(mixed, w_ref[:, :part]) + hidden_ref[
            block, pl.ds(ours, part)
        ].astype(F32)


def shards(
    hidden_in,
    proj_zx,
    proj_bc,
    proj_dt,
    conv_x,
    conv_bc,
    dt_bias,
    decay_exp,
    skip_gain,
    norm_gain,
    out_proj,
):
    rows, width = hidden_in.shape[0], hidden_in.shape[1] // 2
    inner = proj_zx.shape[2]
    count = math.prod(lax.axis_size(axis) for axis in SEQ)
    outer = [(i, i + 1 if i % 2 else i - 1) for i in range(1, count - 1)]
    inside_pairs = [(i, i - 1 if i % 2 else i + 1) for i in range(count)]
    swap = [(0, 1), (1, 0)]
    x_hi, core = lax.axis_index("x_hi"), lax.axis_index("core")
    place = jnp.stack([x_hi, core, lax.axis_index(SEQ), jnp.int32(count)]).astype(jnp.int32)
    zx = proj_zx.reshape(width, 2 * inner)

    pack, late, far, near = call(
        pack_kernel,
        (
            struct((PACKED, inner), BF16),
            struct((width, 2 * inner), BF16),
            struct((HALO, width), BF16),
            struct((HALO, width), BF16),
        ),
        [SMEM, VMEM] + [HBM] * 8,
        (VMEM,) * 4,
        cost(1_000_000, 0, 1_000_000),
        scratch=[
            pltpu.VMEM((4, width), BF16),
            pltpu.VMEM((REACH + 1, inner), BF16),
            pltpu.VMEM((1, 4), F32),
            pltpu.VMEM((1, 4), jnp.int32),
            pltpu.VMEM((1, 4), F32),
            pltpu.VMEM((1, inner), F32),
            dma(10),
        ],
    )(
        place,
        zx,
        *lying(
            proj_dt.T,
            conv_x,
            dt_bias.reshape(1, 4),
            decay_exp.reshape(1, 4),
            skip_gain.reshape(1, 4),
            norm_gain.reshape(1, inner),
            hidden_in,
            out_proj,
        ),
    )
    beside = (("seq_1", "x_hi"), [(0, 3), (3, 0), (1, 2), (2, 1)])
    other_pack = lax.ppermute(pack, *beside)
    got_far = lax.ppermute(far, SEQ, outer)
    got_near = lax.ppermute(near, SEQ, inside_pairs)

    other_late = lax.ppermute(late, *beside)
    u, own_gate, y, c, cols, first, gains, send = call(
        front_kernel,
        (
            struct((rows, width), BF16),
            struct((rows, inner), F32),
            struct((2, rows, 2 * inner), F32),
            struct((2, rows, LANES), BF16),
            struct((rows, LANES), F32),
            struct((2, STATE, 2 * inner), F32),
            struct((8, 2 * inner), F32),
            struct((count, 16, LANES), BF16),
        ),
        [SMEM] + [VMEM] * 8,
        (VMEM,) * 8,
        cost(8_000_000_000, 3_000_000, 24_000_000),
        scratch=[
            pltpu.VMEM((2, rows, 2 * inner), BF16),
            pltpu.VMEM((2, rows, LANES), BF16),
            pltpu.VMEM((48, rows), F32),
            pltpu.VMEM((2 * inner // LANES + 1, rows + 2 * HALO, LANES), F32),
        ],
    )(place, hidden_in, zx, got_far, got_near, pack, other_pack, proj_bc, conv_bc)
    def passed_on(place, send, *others):
        got = lax.all_to_all(send, SEQ, 0, 0, tiled=True)
        scanned = call(
            scan_kernel,
            struct((count, 8, LANES), BF16),
            [SMEM, VMEM],
            VMEM,
            cost(1_000_000, 0, 400_000),
        )(place, got)
        return lax.all_to_all(scanned, SEQ, 0, 0, tiled=True), *others

    came, y, c, cols, first, gains, own_gate, u = lax.cond(
        core < 2,
        passed_on,
        lambda place, send, *others: (send[:, :8], *[-other for other in others]),
        place, send, y, c, cols, first, gains, own_gate, u,
    )

    keep, give = call(
        back_kernel,
        (struct((rows, inner), F32), struct((rows, inner), BF16)),
        [SMEM] + [VMEM] * 11,
        (VMEM, VMEM),
        cost(2_000_000_000, 600_000, 6_000_000),
        scratch=[
            pltpu.VMEM((2, STATE, 2 * inner), F32),
            pltpu.VMEM((2 * inner, 2 * inner), BF16),
        ],
    )(
        place, y, c, came, first, cols, gains, own_gate, u, out_proj, other_late, hidden_in
    )
    taken = lax.ppermute(give, "core", swap)
    return (keep + taken.astype(F32)).astype(BF16)


def solution(mesh):
    torus = Mesh(mesh.devices.reshape(8, 2, 4, 2, 2), SEQ + CH)
    placed = (
        P(SEQ, None),
        P(None, None, CH),
        P(),
        P(None, CH),
        P(None, CH),
        P(),
        P(CH),
        P(CH),
        P(CH),
        P(CH),
        P(CH, None),
    )
    return jax.shard_map(
        shards, mesh=torus, in_specs=placed, out_specs=P(SEQ, CH), check_vma=False
    )
```

```python
import math

import jax
import jax.numpy as jnp
from jax import lax
from jax.experimental import pallas as pl
from jax.experimental.pallas import tpu as pltpu
from jax.sharding import Mesh
from jax.sharding import PartitionSpec as P

BLOCK = 256
STATE = 64
HEADP = 64
REACH = 3
HALO = 8
LANES = 128
SEQ = ("seq_0", "seq_1", "seq_2")
CH = ("x_hi", "core")
EPS = 1e-05
LOG2E = math.log2(math.e)
F32 = jnp.float32
BF16 = jnp.bfloat16

VMEM = pl.BlockSpec(memory_space=pltpu.VMEM)
HBM = pl.BlockSpec(memory_space=pltpu.HBM)
SMEM = pl.BlockSpec(memory_space=pltpu.SMEM)


def cost(flops, transcendentals, bytes_accessed):
    return pl.CostEstimate(
        flops=flops, transcendentals=transcendentals, bytes_accessed=bytes_accessed
    )


def struct(shape, dtype):
    return jax.ShapeDtypeStruct(shape, dtype)


def lying(*arrays):
    return [pltpu.with_memory_space_constraint(array, pltpu.HBM) for array in arrays]


def start_copies(pairs, sems):
    copies = [
        pltpu.make_async_copy(source, target, sems.at[i]) for i, (source, target) in enumerate(pairs)
    ]
    for copy in copies:
        copy.start()
    return copies


def dma(n):
    return pltpu.SemaphoreType.DMA((n,))


def call(kernel, out_shape, specs, out_specs, estimate, mib=16, scratch=()):
    return pl.pallas_call(
        kernel,
        out_shape=out_shape,
        in_specs=specs,
        out_specs=out_specs,
        scratch_shapes=scratch,
        compiler_params=pltpu.CompilerParams(vmem_limit_bytes=mib * 1024 * 1024),
        cost_estimate=estimate,
    )


def iota(shape, dim):
    return lax.broadcasted_iota(jnp.int32, shape, dim)


def dot(a, b):
    return jnp.dot(a, b, preferred_element_type=F32)


def dot_nt(a, b):
    return lax.dot_general(a, b, (((1,), (1,)), ((), ())), preferred_element_type=F32)


def sigmoid(v):
    return 0.5 * jnp.tanh(0.5 * v) + 0.5


def parts_of(value):
    hi = value.astype(BF16).astype(F32)
    rest = value - hi
    mid = rest.astype(BF16).astype(F32)
    return hi, mid, rest - mid


def orient(n, strand):
    source, target = iota((n, n), 0), iota((n, n), 1)
    return (source == jnp.where(strand == 0, target, n - 1 - target)).astype(BF16)


DT_AT, TAP_AT, SMALL_AT, PACKED = 512, 520, 528, 544


def late_kernel(zx_ref, after_ref, out_hbm, late_ref, sems):
    inner = out_hbm.shape[0]
    copies = start_copies(
        (
            (out_hbm.at[:, :inner], late_ref.at[:inner, inner:]),
            (out_hbm.at[:, inner:], late_ref.at[inner:, inner:]),
        ),
        sems,
    )
    late_ref[:, :inner] = zx_ref[:, :inner]
    for copy in copies:
        copy.wait()


def pack_kernel(
    place_ref, zx_ref, dt_hbm, taps_hbm, bias_hbm, exp_hbm, skip_hbm, gain_hbm, hidden_hbm,
    pack_ref, far_ref, near_ref,
    dt_ref, taps_ref, bias_ref, exp_ref, skip_ref, gain_ref, sems,
):
    inner, heads = pack_ref.shape[1], dt_ref.shape[0]
    rows, width = hidden_hbm.shape[0], hidden_hbm.shape[1] // 2
    columns = pl.ds(pl.multiple_of(place_ref[0] * width, width), width)
    odd, last = lax.rem(place_ref[2], 2), rows - HALO
    copies = start_copies(
        (
            (dt_hbm, dt_ref),
            (taps_hbm, taps_ref),
            (bias_hbm, bias_ref),
            (exp_hbm, exp_ref),
            (skip_hbm, skip_ref),
            (gain_hbm, gain_ref),
            (hidden_hbm.at[pl.ds(pl.multiple_of(odd * last, HALO), HALO), columns], far_ref),
            (hidden_hbm.at[pl.ds(pl.multiple_of((1 - odd) * last, HALO), HALO), columns], near_ref),
        ),
        sems,
    )
    pack_ref[:DT_AT] = zx_ref[:, inner:]
    for copy in copies:
        copy.wait()
    lane = iota((1, inner), 1)
    small = jnp.zeros((1, inner), F32)
    for h in range(heads):
        for k, ref in enumerate((bias_ref, exp_ref, skip_ref)):
            value = ref[:, h : h + 1].astype(F32)
            small = jnp.where(lane == k * heads + h, jnp.broadcast_to(value, (1, inner)), small)
    packed = [dt_ref[:, :inner].astype(F32), dt_ref[:, inner:].astype(F32), taps_ref[...].astype(F32)]
    packed.append(jnp.zeros((SMALL_AT - TAP_AT - taps_ref.shape[0], inner), F32))
    packed += parts_of(small) + parts_of(gain_ref[...])
    packed.append(jnp.zeros((PACKED - SMALL_AT - 6, inner), F32))
    pack_ref[DT_AT:] = jnp.concatenate(packed, axis=0).astype(BF16)


def unpack(ref):
    tail = ref[SMALL_AT:].astype(F32)
    return tail[0:1] + tail[1:2] + tail[2:3], tail[3:4] + tail[4:5] + tail[5:6]


def column_of(smalls, at):
    row = iota((8, 1), 0)
    out = jnp.zeros((8, 1), F32)
    for g in range(2):
        for h in range(4):
            out = jnp.where(row == g * 4 + h, smalls[g][:, at + h : at + h + 1], out)
    return out


def spread(pieces, rows):
    half = iota((rows, LANES), 1) < HEADP
    wide = [jnp.broadcast_to(piece, (rows, LANES)) for piece in pieces]
    return jnp.concatenate(
        [jnp.where(half, wide[2 * q], wide[2 * q + 1]) for q in range(4)], axis=1
    )


def turned_out(place_ref, out):
    columns = out.shape[1]
    part = columns // 2
    source, target = iota((columns, columns), 0), iota((columns, columns), 1)
    column = jnp.where(target < part, target + place_ref[1] * part, target - place_ref[1] * part)
    wanted = jnp.where(place_ref[0] == 0, column, columns - 1 - column)
    return dot(out, (source == wanted).astype(BF16)).astype(BF16)


def gated_by(u, w):
    z = dot(u, w).astype(BF16).astype(F32)
    return z * sigmoid(z)


def front_kernel(
    place_ref, hidden_ref, zx_ref, far_ref, near_ref, own_ref, other_ref, bc_ref, tapbc_ref,
    u_ref, gate_ref, y_ref, c_ref, cols_ref, first_ref, gains_ref, send_ref,
    x_ref, b_ref, rows_ref, pad_ref,
):
    row_count, width = hidden_ref.shape[0], hidden_ref.shape[1] // 2
    inner = own_ref.shape[1]
    strand, position, count = place_ref[0], place_ref[2], place_ref[3]
    packs = (own_ref, other_ref)
    turn = orient(width, strand)
    u = hidden_ref[:, pl.ds(pl.multiple_of(strand * width, width), width)]
    u = dot(u, turn).astype(BF16)
    u_ref[...] = u
    gate_ref[...] = gated_by(u, zx_ref[:, :inner])
    odd = lax.rem(position, 2) == 1
    far, near = far_ref[...].astype(F32), near_ref[...].astype(F32)
    before = jnp.where(position > 0, jnp.where(odd, near, far), 0.0)
    after = jnp.where(position < count - 1, jnp.where(odd, far, near), 0.0)
    edge = dot(jnp.concatenate([before, after], axis=0).astype(BF16), turn)
    edge = edge.astype(BF16)

    raw = jnp.concatenate(
        [
            dot_nt(
                jnp.concatenate(
                    [ref[DT_AT : DT_AT + 4].astype(F32), ref[DT_AT + 4 : DT_AT + 8].astype(F32)],
                    axis=1,
                ).astype(BF16),
                u,
            )
            for ref in packs
        ],
        axis=0,
    )
    smalls, gains = zip(*[unpack(ref) for ref in packs])
    gains_ref[...] = jnp.concatenate(
        [
            jnp.concatenate(gains, axis=1),
            spread([smalls[g][:, 8 + h : 9 + h] for g in range(2) for h in range(4)], 1),
            jnp.zeros((6, 2 * inner), F32),
        ],
        axis=0,
    )
    v = raw + column_of(smalls, 0)
    rate = jnp.exp2(-column_of(smalls, 4)) * LOG2E
    step = jnp.maximum(v, 0.0) + jnp.log1p(jnp.exp(-jnp.abs(v)))
    parts = jnp.concatenate(parts_of(-step * rate), axis=0).astype(BF16)
    ahead = (iota((BLOCK, BLOCK), 0) <= iota((BLOCK, BLOCK), 1)).astype(BF16)
    behind = (iota((BLOCK, BLOCK), 0) >= iota((BLOCK, BLOCK), 1)).astype(BF16)
    cums, ends = [], []
    for b in range(2):
        piece = parts[:, b * BLOCK : (b + 1) * BLOCK]
        both = []
        for mask in (ahead, behind):
            full = dot(piece, mask)
            both.append(full[:8] + full[8:16] + full[16:])
        cums.append(jnp.concatenate(both, axis=0))
        last = jnp.concatenate([both[0][:, BLOCK - 1 :], both[1][:, :1]], axis=0)
        ends.append(jnp.broadcast_to(last, (16, BLOCK)))
    cum = jnp.concatenate(cums, axis=1)
    end = jnp.concatenate(ends, axis=1)
    step = jnp.concatenate([step, step], axis=0)
    rows_ref[:16] = cum
    rows_ref[16:32] = cum - jnp.log2(step)
    rows_ref[32:] = jnp.exp2(jnp.minimum(end - cum, 0.0)) * step
    cols_ref[...] = jnp.concatenate([cum, jnp.zeros((LANES - 16, row_count), F32)], axis=0).T
    totals = [ends[b][:, :1] for b in range(2)]

    chunk = 32
    tiles = inner // LANES
    for g in range(3):
        w = packs[g][:DT_AT] if g < 2 else bc_ref[...]
        middle = dot(u, w).astype(BF16).astype(F32)
        outer = dot(edge, w).astype(BF16).astype(F32)
        for k in range(w.shape[1] // LANES):
            at, lanes = g * tiles + k, slice(k * LANES, (k + 1) * LANES)
            pad_ref[at, :HALO] = outer[:HALO, lanes]
            pad_ref[at, HALO : HALO + row_count] = middle[:, lanes]
            pad_ref[at, HALO + row_count :] = outer[HALO:, lanes]
    taps = jnp.concatenate(
        [ref[TAP_AT : TAP_AT + REACH + 1].astype(F32) for ref in packs]
        + [tapbc_ref[...].astype(F32)],
        axis=1,
    )
    groups = taps.shape[1] // LANES
    low_lane = iota((chunk, LANES), 1) < STATE
    for group in range(groups):
        at = slice(group * LANES, (group + 1) * LANES)
        tap = [taps[j : j + 1, at] for j in range(REACH + 1)]
        for r in range(0, row_count, chunk):
            start = r + HALO - REACH
            window = [
                pad_ref[group, start + k : start + k + chunk] for k in range(2 * REACH + 1)
            ]
            for way in range(2):
                acc = tap[0] * window[0 if way == 0 else 2 * REACH]
                for j in range(1, REACH + 1):
                    acc = acc + tap[j] * window[j if way == 0 else 2 * REACH - j]
                value = (acc * sigmoid(acc)).astype(BF16)
                if group < groups - 1:
                    x_ref[way, r : r + chunk, at] = value
                else:
                    b_ref[way, r : r + chunk, :] = value
                    swapped = pltpu.roll(value.astype(F32), LANES - STATE, 1)
                    c_ref[way, r : r + chunk, :] = jnp.where(low_lane, swapped, 0.0).astype(BF16)


    half = iota((STATE, LANES), 1) < HEADP
    row8 = iota((8, LANES), 0)
    for way in range(2):
        states = []
        for b in range(2):
            block = slice(b * BLOCK, (b + 1) * BLOCK)
            bt = b_ref[way, block, :].astype(F32).T[:STATE]
            tiles = []
            for g in range(2):
                at = 32 + way * 8 + g * 4
                scaled = jnp.concatenate(
                    [
                        (bt * rows_ref[at + h : at + h + 1, block]).astype(BF16)
                        for h in range(4)
                    ],
                    axis=0,
                )
                full = dot(scaled, x_ref[way, block, g * inner : (g + 1) * inner])
                tiles.append(jnp.where(half, full[:64, :128], full[64:128, :128]))
                tiles.append(jnp.where(half, full[128:192, 128:], full[192:, 128:]))
            states.append(tiles)
        first, last = (0, 1) if way == 0 else (1, 0)
        at = slice(way * 8, way * 8 + 8)
        last_total = jnp.exp2(totals[last][at])
        both_total = jnp.exp2(totals[0][at] + totals[1][at])
        factor = spread([last_total[i : i + 1] for i in range(8)], 1)
        whole = spread([both_total[i : i + 1] for i in range(8)], 8)
        for q in range(4):
            lanes = slice(q * LANES, (q + 1) * LANES)
            state = factor[:, lanes] * states[first][q] + states[last][q]
            first_ref[way, :, lanes] = states[first][q]
            hi, mid, low = parts_of(whole[:, lanes])
            decay = jnp.where(
                row8 == 0, hi, jnp.where(row8 == 1, mid, jnp.where(row8 == 2, low, 0.0))
            )
            for n in range(8):
                send_ref[way * 32 + n * 4 + q] = jnp.concatenate(
                    [state[n * 8 : n * 8 + 8], decay], axis=0
                ).astype(BF16)
    inside(x_ref, b_ref, c_ref, rows_ref, cols_ref, gains_ref, y_ref)


def scan_kernel(place_ref, got_ref, out_ref):
    count = got_ref.shape[0]
    backward = place_ref[2] >= count // 2
    state = jnp.zeros((8, LANES), F32)
    for i in range(count):
        k = jnp.where(backward, count - 1 - i, i)
        piece = got_ref[k].astype(F32)
        out_ref[k] = state.astype(BF16)
        decay = jnp.sum(piece[8:], axis=0, keepdims=True)
        state = decay * state + piece[:8]


def inside(x_ref, b_ref, c_ref, rows_ref, cols_ref, gains_ref, y_ref):
    size = 128
    low = iota((size, size), 0) >= iota((size, size), 1)
    high = iota((size, size), 0) <= iota((size, size), 1)
    half = iota((size, LANES), 1) < HEADP
    skip = gains_ref[1:2]
    for way in range(2):
        for b in range(2):
            block = slice(b * BLOCK, (b + 1) * BLOCK)
            scores = dot_nt(c_ref[way, block, :], b_ref[way, block, :])
            for pair in range(4):
                at = slice(pair * LANES, (pair + 1) * LANES)
                for t in range(2):
                    here = slice(b * BLOCK + t * size, b * BLOCK + (t + 1) * size)
                    seen = [s for s in range(2) if (s <= t if way == 0 else s >= t)]
                    lo = b * BLOCK + seen[0] * size
                    hi = b * BLOCK + (seen[-1] + 1) * size
                    outs = []
                    for h in (2 * pair, 2 * pair + 1):
                        i = way * 8 + h
                        gone = jnp.broadcast_to(cols_ref[here, i : i + 1], (size, size))
                        tiles = []
                        for s in seen:
                            there = slice(b * BLOCK + s * size, b * BLOCK + (s + 1) * size)
                            gap = gone - rows_ref[16 + i : 17 + i, there]
                            if s == t:
                                gap = jnp.where(low if way == 0 else high, gap, -jnp.inf)
                            part = scores[t * size : (t + 1) * size, s * size : (s + 1) * size]
                            tiles.append((part * jnp.exp2(gap)).astype(BF16))
                        weights = tiles[0] if len(tiles) == 1 else jnp.concatenate(tiles, axis=1)
                        outs.append(dot(weights, x_ref[way, lo:hi, at]))
                    y_ref[way, here, at] = (
                        jnp.where(half, outs[0], outs[1])
                        + skip[:, at] * x_ref[way, here, at].astype(F32)
                    )


def back_kernel(
    place_ref, y_ref, c_ref, came_ref, first_ref, cols_ref, gains_ref, own_gate_ref, u_ref,
    own_out_ref, late_ref, hidden_ref, keep_ref, give_ref, state_ref, w_ref,
):
    part = own_out_ref.shape[1] // 2
    inner = y_ref.shape[2] // 2
    ours = pl.multiple_of((2 * place_ref[0] + place_ref[1]) * part, part)
    blocks = [slice(b * BLOCK, (b + 1) * BLOCK) for b in range(2)]
    w_ref[:inner] = turned_out(place_ref, own_out_ref[...])
    w_ref[inner:] = turned_out(
        place_ref, jnp.concatenate([late_ref[:inner, inner:], late_ref[inner:, inner:]], axis=1)
    )
    same = (iota((inner, inner), 0) // HEADP == iota((inner, inner), 1) // HEADP).astype(BF16)
    for way in range(2):
        for n in range(8):
            for q in range(4):
                state_ref[way, n * 8 : n * 8 + 8, q * LANES : (q + 1) * LANES] = came_ref[
                    way * 32 + n * 4 + q
                ].astype(F32)
    for b, block in enumerate(blocks):
        decays = jnp.exp2(cols_ref[block])
        gate = jnp.concatenate(
            [own_gate_ref[block, :], gated_by(u_ref[block, :], late_ref[:, :inner])], axis=1
        )
        total = None
        for way in range(2):
            state = state_ref[way]
            if b != way:
                edge = BLOCK - 1 if way == 0 else BLOCK
                passed = jnp.exp2(cols_ref[edge : edge + 1])
                factor = spread(
                    [passed[:, way * 8 + i : way * 8 + i + 1] for i in range(8)], 1
                )
                state = factor * state + first_ref[way]
            state = jnp.concatenate([state, jnp.zeros_like(state)], axis=0).astype(BF16)
            decay = spread([decays[:, way * 8 + i : way * 8 + i + 1] for i in range(8)], BLOCK)
            mixer = y_ref[way, block, :] + decay * dot(c_ref[way, block, :], state)
            gated = mixer * gate
            square = (gated * gated).astype(BF16)
            mean = jnp.concatenate(
                [dot(square[:, g * inner : (g + 1) * inner], same) for g in range(2)], axis=1
            ) * (1.0 / HEADP)
            normed = gated * lax.rsqrt(mean + EPS)
            total = normed if total is None else total + normed
        mixed = (total * gains_ref[0:1]).astype(BF16)
        give_ref[block, :] = dot(mixed, w_ref[:, part:]).astype(BF16)
        keep_ref[block, :] = dot(mixed, w_ref[:, :part]) + hidden_ref[
            block, pl.ds(ours, part)
        ].astype(F32)


def shards(
    hidden_in,
    proj_zx,
    proj_bc,
    proj_dt,
    conv_x,
    conv_bc,
    dt_bias,
    decay_exp,
    skip_gain,
    norm_gain,
    out_proj,
):
    rows, width = hidden_in.shape[0], hidden_in.shape[1] // 2
    inner = proj_zx.shape[2]
    count = math.prod(lax.axis_size(axis) for axis in SEQ)
    outer = [(i, i + 1 if i % 2 else i - 1) for i in range(1, count - 1)]
    inside_pairs = [(i, i - 1 if i % 2 else i + 1) for i in range(count)]
    swap = [(0, 1), (1, 0)]
    x_hi, core = lax.axis_index("x_hi"), lax.axis_index("core")
    place = jnp.stack([x_hi, core, lax.axis_index(SEQ), jnp.int32(count)]).astype(jnp.int32)
    zx = proj_zx.reshape(width, 2 * inner)

    pack, far, near = call(
        pack_kernel,
        (
            struct((PACKED, inner), BF16),
            struct((HALO, width), BF16),
            struct((HALO, width), BF16),
        ),
        [SMEM, VMEM] + [HBM] * 7,
        (VMEM,) * 3,
        cost(1_000_000, 0, 1_000_000),
        scratch=[
            pltpu.VMEM((4, width), BF16),
            pltpu.VMEM((REACH + 1, inner), BF16),
            pltpu.VMEM((1, 4), F32),
            pltpu.VMEM((1, 4), jnp.int32),
            pltpu.VMEM((1, 4), F32),
            pltpu.VMEM((1, inner), F32),
            dma(8),
        ],
    )(
        place,
        zx,
        *lying(
            proj_dt.T,
            conv_x,
            dt_bias.reshape(1, 4),
            decay_exp.reshape(1, 4),
            skip_gain.reshape(1, 4),
            norm_gain.reshape(1, inner),
            hidden_in,
        ),
    )
    beside = (("seq_1", "x_hi"), [(0, 3), (3, 0), (1, 2), (2, 1)])
    other_pack = lax.ppermute(pack, *beside)
    got_far = lax.ppermute(far, SEQ, outer)
    got_near = lax.ppermute(near, SEQ, inside_pairs)

    late = call(
        late_kernel,
        struct((width, 2 * inner), BF16),
        [VMEM, VMEM, HBM],
        VMEM,
        cost(1_000_000, 0, 1_000_000),
        mib=4,
        scratch=[dma(2)],
    )(zx, near, *lying(out_proj))
    other_late = lax.ppermute(late, *beside)
    u, own_gate, y, c, cols, first, gains, send = call(
        front_kernel,
        (
            struct((rows, width), BF16),
            struct((rows, inner), F32),
            struct((2, rows, 2 * inner), F32),
            struct((2, rows, LANES), BF16),
            struct((rows, LANES), F32),
            struct((2, STATE, 2 * inner), F32),
            struct((8, 2 * inner), F32),
            struct((count, 16, LANES), BF16),
        ),
        [SMEM] + [VMEM] * 8,
        (VMEM,) * 8,
        cost(8_000_000_000, 3_000_000, 24_000_000),
        scratch=[
            pltpu.VMEM((2, rows, 2 * inner), BF16),
            pltpu.VMEM((2, rows, LANES), BF16),
            pltpu.VMEM((48, rows), F32),
            pltpu.VMEM((2 * inner // LANES + 1, rows + 2 * HALO, LANES), F32),
        ],
    )(place, hidden_in, zx, got_far, got_near, pack, other_pack, proj_bc, conv_bc)
    def passed_on(place, send, *others):
        got = lax.all_to_all(send, SEQ, 0, 0, tiled=True)
        scanned = call(
            scan_kernel,
            struct((count, 8, LANES), BF16),
            [SMEM, VMEM],
            VMEM,
            cost(1_000_000, 0, 400_000),
        )(place, got)
        return lax.all_to_all(scanned, SEQ, 0, 0, tiled=True), *others

    came, y, c, cols, first, gains, own_gate, u = lax.cond(
        core < 2,
        passed_on,
        lambda place, send, *others: (send[:, :8], *[-other for other in others]),
        place, send, y, c, cols, first, gains, own_gate, u,
    )

    keep, give = call(
        back_kernel,
        (struct((rows, inner), F32), struct((rows, inner), BF16)),
        [SMEM] + [VMEM] * 11,
        (VMEM, VMEM),
        cost(2_000_000_000, 600_000, 6_000_000),
        scratch=[
            pltpu.VMEM((2, STATE, 2 * inner), F32),
            pltpu.VMEM((2 * inner, 2 * inner), BF16),
        ],
    )(
        place, y, c, came, first, cols, gains, own_gate, u, out_proj, other_late, hidden_in
    )
    taken = lax.ppermute(give, "core", swap)
    return (keep + taken.astype(F32)).astype(BF16)


def solution(mesh):
    torus = Mesh(mesh.devices.reshape(8, 2, 4, 2, 2), SEQ + CH)
    placed = (
        P(SEQ, None),
        P(None, None, CH),
        P(),
        P(None, CH),
        P(None, CH),
        P(),
        P(CH),
        P(CH),
        P(CH),
        P(CH),
        P(CH, None),
    )
    return jax.shard_map(
        shards, mesh=torus, in_specs=placed, out_specs=P(SEQ, CH), check_vma=False
    )
```
